32 devices in a mesh: tile: 8 (over y, x, core), body: 4 (over z).
Axes of the slice: x: 2, y: 2, z: 4, core: 2. Of those that a mesh axis runs over, the one named last changes fastest.
Arguments:
- fluid_position: float32 [3, 128, 32, 128], P(None, 'tile', 'body'), may hold values from 0 to 128, as said below
- fluid_pressure: float32 [128, 32, 128], P('tile', 'body'), may hold values from 0 to 1
- source: float32 [128, 32, 128], P('tile', 'body'), may hold values from -12 to 12
- stiffness: float32 [128, 32, 128], P('tile', 'body'), may hold values from 0.5 to 2
- neighbours: int32 [128, 32, 6], P('tile', 'body'), may hold values from 0 to 8, as said below
- wall_position: float32 [3, 128, 32, 128], P(None, 'tile', 'body'), may hold values from 0 to 128, as said below
- wall_normal: float32 [3, 128, 32, 128], P(None, 'tile', 'body'), may hold values from -4 to 4
- wall_arm: float32 [3, 128, 32, 128], P(None, 'tile', 'body'), may hold values from -4 to 4
- wall_live: int32 [128, 32, 128], P('tile', 'body'), may hold values 0 or 1
- wall_body: int32 [128, 32, 128], P('tile', 'body'), may hold values from 0 to 30719, as said below
- linear_velocity: float32 [3, 30720], P(None, 'body'), may hold values from -6 to 6
- angular_velocity: float32 [3, 30720], P(None, 'body'), may hold values from -6 to 6
- inverse_mass: float32 [30720], P('body'), may hold values from 0.2 to 2
- inverse_inertia: float32 [3, 30720], P(None, 'body'), may hold values from 0.2 to 2
Outputs:
- pressure: float32 [128, 32, 128], P('tile', 'body')
- wall_pressure: float32 [128, 32, 128], P('tile', 'body')
- body_state: float32 [6, 30720], P(None, 'body')
- wall_velocity: float32 [3, 128, 32, 128], P(None, 'tile', 'body')
- density_error: float32 [], replicated
The draws below stay inside these ranges and needn't reach their ends.
Inputs may be any that keep to these rules, and one draw needn't show every extreme that they name: `neighbours`: entry 0 of every list is 4, the block itself; the other entries are distinct codes of the eight blocks around it. `fluid_position`: A particle of block (a, b) has its first coordinate in [a, a + 1), its second in [b, b + 1), its third in [0, 1). `wall_position`: A particle of block (a, b) has its first coordinate in [a, a + 1], its second in [b, b + 1], its third in [0, 1]. `wall_body`: bodies are compact: a boundary particle belongs to a body whose centre lies within a few blocks of its own block.
All inputs are finite; a program needn't handle non-finite values. No bound on the sum of `wall_live` on one device may be relied on, other than what follows from the above.
Results may differ from the reference program's by a relative error of at most 0.0003.
Values sent between devices are 32-bit elements; how exact they have to be, the bound alone decides.
A program may use at most 128 MiB of HBM per device.

```python
import math
import jax
import jax.numpy as jnp
from jax import lax

BLOCK = 128
NEIGH = 6
SWEEPS = 2
BODIES = 30720
NBX = 128
NBY = 32


def block_grid(unit):
    first = jnp.arange(NBX, dtype=jnp.float32)[:, None, None]
    second = jnp.arange(NBY, dtype=jnp.float32)[None, :, None]
    return jnp.stack([unit[0] + first, unit[1] + second, unit[2]], 0)


def draw_fluid_position(key, part):
    unit = jax.random.uniform(jax.random.fold_in(key, 11), (3, NBX, NBY, BLOCK), jnp.float32)
    return block_grid(unit)


def draw_wall_position(key, part):
    unit = jax.random.uniform(jax.random.fold_in(key, 23), (3, NBX, NBY, BLOCK), jnp.float32)
    return block_grid(unit)


def draw_source(key, part):
    rising = 1.0 + 2.0 * jnp.arange(NBX, dtype=jnp.float32)[:, None, None] / max(NBX - 1, 1)
    rough = jnp.clip(jax.random.normal(jax.random.fold_in(key, 37), (NBX, NBY, BLOCK), jnp.float32), -4.0, 4.0)
    return rough * rising


def draw_neighbours(key, part):
    scores = jax.random.randint(jax.random.fold_in(key, 41), (NBX, NBY, 8), 0, 1 << 20) * 8 + jnp.arange(8, dtype=jnp.int32)
    ordering = jnp.argsort(scores, axis=-1, stable=True)[..., :NEIGH - 1]
    others = jnp.array([0, 1, 2, 3, 5, 6, 7, 8], dtype=jnp.int32)
    picked = others[ordering].astype(jnp.int32)
    itself = jnp.full((NBX, NBY, 1), 4, jnp.int32)
    return jnp.concatenate([itself, picked], axis=-1)


def cluster_bodies(key):
    grid_count = NBX * NBY
    per_block = max((BODIES + grid_count - 1) // grid_count, 1)
    shape = (NBX, NBY, BLOCK)
    step_first = jax.random.randint(jax.random.fold_in(key, 51), shape, -1, 2)
    step_second = jax.random.randint(jax.random.fold_in(key, 52), shape, -1, 2)
    rank_pick = jax.random.randint(jax.random.fold_in(key, 53), shape, 0, per_block)
    first = jnp.arange(NBX, dtype=jnp.int32)[:, None, None]
    second = jnp.arange(NBY, dtype=jnp.int32)[None, :, None]
    centre_first = jnp.clip(first + step_first, 0, NBX - 1)
    centre_second = jnp.clip(second + step_second, 0, NBY - 1)
    linear_block = centre_first * NBY + centre_second
    chosen = linear_block * BODIES // grid_count + rank_pick
    return jnp.minimum(chosen, BODIES - 1).astype(jnp.int32)


def draw_wall_body(key, part):
    return cluster_bodies(key)


def draw_wall_arm(key, part):
    chosen = cluster_bodies(key)
    grid_count = NBX * NBY
    home = chosen * grid_count // BODIES
    home_first = (home // NBY).astype(jnp.float32) + 0.5
    home_second = (home % NBY).astype(jnp.float32) + 0.5
    centre = jnp.stack([home_first, home_second, jnp.full(chosen.shape, 0.5, jnp.float32)], 0)
    unit = jax.random.uniform(jax.random.fold_in(key, 23), (3, NBX, NBY, BLOCK), jnp.float32)
    position = block_grid(unit)
    return jnp.clip(position - centre, -4.0, 4.0)


def touch_ends(result, own_key, least, largest):
    dims = result.shape
    index_at = [jax.random.randint(jax.random.fold_in(own_key, axis), (), 0, dims[axis]) for axis in range(len(dims))]
    result = result.at[tuple(index_at)].set(least)
    longest = dims.index(max(dims))
    index_at[longest] = (index_at[longest] + 1) % dims[longest]
    return result.at[tuple(index_at)].set(largest)


def shard_levels(stream_key, extent, pieces, smallest, high):
    def one(dim, parts):
        heights = jax.random.uniform(jax.random.fold_in(jax.random.fold_in(stream_key, 6), dim), (parts,), jnp.float32, smallest / len(pieces), high / len(pieces))
        return jnp.repeat(jnp.exp(heights), extent[dim] // parts).reshape((-1,) + (1,) * (len(extent) - dim - 1))

    level = one(*pieces[0])
    for cut in pieces[1:]:
        level = level * one(*cut)
    return level


def scatter_about(stream_key, shape, scale, bound, cuts=(), kind=jnp.bfloat16):
    factor_of = shard_levels(stream_key, shape, cuts, -0.22, 0.18) if cuts else 1.0
    entries = jax.random.normal(stream_key, shape, jnp.float32) * scale * factor_of
    return jnp.minimum(jnp.maximum(entries, -bound), bound).astype(kind)


def setup_inputs(seed: int = 0) -> dict:
    seeds = jax.random.split(jax.random.key(seed), 15)
    fluid_position = draw_fluid_position(jax.random.fold_in(seeds[14], 71), 0)
    fluid_pressure = jnp.clip(1.0 * jax.random.uniform(seeds[1], (NBX, NBY, BLOCK), jnp.float32) ** shard_levels(seeds[1], (NBX, NBY, BLOCK), ((0, 8), (1, 4)), -0.2, 0.2), 0.0, 1.0)
    source = draw_source(jax.random.fold_in(seeds[14], 71), 0)
    stiffness = jnp.clip(jnp.exp(math.log(2.0) - 1.3862944 * jax.random.uniform(seeds[3], (NBX, NBY, BLOCK), jnp.float32) ** shard_levels(seeds[3], (NBX, NBY, BLOCK), ((0, 8), (1, 4)), -0.2, 0.2)), 0.5, 2.0)
    neighbours = draw_neighbours(jax.random.fold_in(seeds[14], 71), 0)
    wall_position = draw_wall_position(jax.random.fold_in(seeds[14], 71), 0)
    wall_normal = scatter_about(seeds[6], (3, NBX, NBY, BLOCK), 1.0, 4.0, ((1, 8), (2, 4)), jnp.float32)
    wall_arm = draw_wall_arm(jax.random.fold_in(seeds[14], 71), 0)
    wall_live = touch_ends((jax.random.randint(seeds[8], (NBX, NBY, BLOCK), 0, 2) < 1).astype(jnp.int32), jax.random.fold_in(seeds[8], 1), 0, 1)
    wall_body = draw_wall_body(jax.random.fold_in(seeds[14], 71), 0)
    linear_velocity = scatter_about(seeds[10], (3, BODIES), 1.0, 6.0, ((1, 4),), jnp.float32)
    angular_velocity = scatter_about(seeds[11], (3, BODIES), 1.0, 6.0, ((1, 4),), jnp.float32)
    inverse_mass = jnp.clip(jnp.exp(math.log(2.0) - 2.3025851 * jax.random.uniform(seeds[12], (BODIES,), jnp.float32) ** shard_levels(seeds[12], (BODIES,), ((0, 4),), -0.2, 0.2)), 0.2, 2.0)
    inverse_inertia = jnp.clip(jnp.exp(math.log(2.0) - 2.3025851 * jax.random.uniform(seeds[13], (3, BODIES), jnp.float32) ** shard_levels(seeds[13], (3, BODIES), ((1, 4),), -0.2, 0.2)), 0.2, 2.0)
    return dict(fluid_position=fluid_position, fluid_pressure=fluid_pressure, source=source, stiffness=stiffness, neighbours=neighbours, wall_position=wall_position, wall_normal=wall_normal, wall_arm=wall_arm, wall_live=wall_live, wall_body=wall_body, linear_velocity=linear_velocity, angular_velocity=angular_velocity, inverse_mass=inverse_mass, inverse_inertia=inverse_inertia)


relax_factor = 0.5
inv_width = 2.0
kernel_scale = 0.0078125
wall_offset = 0.5
time_step = 0.25
gravity_z = -9.81


def pair_sums(padded_pos, padded_val, own_pos, neighbours):
    row_count = own_pos.shape[1]
    columns = own_pos.shape[2]

    def one_row(row_index):
        window_pos = lax.dynamic_slice_in_dim(padded_pos, row_index, 3, 1)
        window_val = lax.dynamic_slice_in_dim(padded_val, row_index, 3, 0)
        shifted_pos = jnp.stack([window_pos[:, i, j:j + columns] for i in range(3) for j in range(3)], 0)
        shifted_val = jnp.stack([window_val[i, j:j + columns] for i in range(3) for j in range(3)], 0)
        code_list = lax.dynamic_index_in_dim(neighbours, row_index, 0, keepdims=False)
        near_pos = jnp.take_along_axis(jnp.transpose(shifted_pos, (2, 0, 1, 3)), code_list[:, :, None, None], axis=1)
        near_val = jnp.take_along_axis(jnp.transpose(shifted_val, (1, 0, 2)), code_list[:, :, None], axis=1)
        own_rows = lax.dynamic_index_in_dim(own_pos, row_index, 1, keepdims=False)
        distance = None
        for component in range(3):
            offset = own_rows[component][:, None, :, None] - near_pos[:, :, component][:, :, None, :]
            distance = offset * offset if distance is None else distance + offset * offset
        weight = jnp.exp(-distance * inv_width) * kernel_scale
        weight_sum = jnp.sum(weight, axis=(1, 3))
        weighted = jnp.einsum("ckij,ckj->ci", weight, near_val, precision=lax.Precision.HIGHEST)
        return weight_sum, weighted

    return lax.map(one_row, jnp.arange(row_count, dtype=jnp.int32))


def cross_product(left, right):
    return jnp.stack([left[1] * right[2] - left[2] * right[1],
                      left[2] * right[0] - left[0] * right[2],
                      left[0] * right[1] - left[1] * right[0]], 0)


def advance(params, totals):
    lift = jnp.array([0.0, 0.0, time_step * gravity_z], dtype=jnp.float32)[:, None]
    linear = params[0:3] + time_step * (params[6][None] * totals[0:3]) + lift
    angular = params[3:6] + time_step * params[7:10] * totals[3:6]
    return jnp.concatenate([linear, angular], 0)


def reference(fluid_position, fluid_pressure, source, stiffness, neighbours, wall_position, wall_normal, wall_arm, wall_live, wall_body, linear_velocity, angular_velocity, inverse_mass, inverse_inertia):
    padded_pos = jnp.pad(fluid_position, ((0, 0), (1, 1), (1, 1), (0, 0)))
    pressure = fluid_pressure
    residual = source
    for sweep_index in range(SWEEPS):
        padded_val = jnp.pad(pressure, ((1, 1), (1, 1), (0, 0)))
        weight_sum, weighted = pair_sums(padded_pos, padded_val, fluid_position, neighbours)
        diagonal = stiffness + weight_sum
        residual = source - (diagonal * pressure - weighted)
        pressure = jnp.maximum(pressure + relax_factor * residual / diagonal, 0.0)
    density_error = jnp.sum(residual * residual) / (NBX * NBY * BLOCK)
    padded_val = jnp.pad(pressure, ((1, 1), (1, 1), (0, 0)))
    weight_sum, weighted = pair_sums(padded_pos, padded_val, wall_position, neighbours)
    wall_pressure = weighted / (wall_offset + weight_sum) * wall_live.astype(jnp.float32)
    force = wall_pressure[None] * wall_normal
    torque = cross_product(wall_arm, force)
    stacked = jnp.concatenate([force, torque], 0).reshape(6, -1).T
    totals = jax.ops.segment_sum(stacked, wall_body.reshape(-1), num_segments=BODIES).T
    params = jnp.concatenate([linear_velocity, angular_velocity, inverse_mass[None], inverse_inertia], 0)
    body_state = advance(params, totals)
    index_flat = wall_body.reshape(-1)
    moving = jnp.take(body_state[0:3], index_flat, axis=1).reshape(wall_arm.shape)
    turning = jnp.take(body_state[3:6], index_flat, axis=1).reshape(wall_arm.shape)
    wall_velocity = moving + cross_product(turning, wall_arm)
    return pressure, wall_pressure, body_state, wall_velocity, density_error
```

```python
import math
import functools
import jax
import jax.numpy as jnp
from jax import lax
from jax.experimental import pallas as pl
from jax.experimental.pallas import tpu as pltpu
from jax.sharding import PartitionSpec as P

SWEEPS = 2

relax_factor = 0.5
inv_width = 2.0
kernel_scale = 0.0078125
wall_offset = 0.5
time_step = 0.25
gravity_z = -9.81

UNIT = math.sqrt(inv_width / math.log(2.0))
DEPTH = 32
LOW = 128
WINDOW = 6
F32, BF16 = jnp.float32, jnp.bfloat16
VMEM = pltpu.VMEM
SMEM = pltpu.SMEM


def pieces(x, count):
    out = []
    for _ in range(count):
        piece = x.astype(BF16).astype(F32)
        out.append(piece)
        x = x - piece
    return out


def own_features(x, y, z):
    rows = []
    for coordinate in (x, y, z):
        h, m, l = pieces(2.0 * coordinate, 3)
        rows += [h, h, m, m, h, l]
    rows += pieces(-(x * x + y * y + z * z), 3)
    one = jnp.ones_like(x)
    return rows + [one, one, one]


def near_features(x, y, z):
    rows = []
    for coordinate in (x, y, z):
        h, m, l = pieces(coordinate, 3)
        rows += [h, m, h, m, l, h]
    one = jnp.ones_like(x)
    rows += [one, one, one]
    return rows + pieces(-(x * x + y * y + z * z), 3)


def column_base(shape, first):
    return (first + lax.broadcasted_iota(jnp.int32, shape, 0)).astype(F32) + 0.5


def build_near(pos_ref, base_ref, fj_ref, stage_ref, cols):
    rows, wide = pos_ref.shape[1], pos_ref.shape[2]
    stage_ref[...] = jnp.zeros_like(stage_ref)

    def row(r, carry):
        x = (pos_ref[0, r] - ((base_ref[0] + r - 1).astype(F32) + 0.5)) * UNIT
        y = (pos_ref[1, r] - column_base((wide, 128), base_ref[1] - 1)) * UNIT
        z = (pos_ref[2, r] - 0.5) * UNIT
        for k, value in enumerate(near_features(x, y, z)):
            stage_ref[k * wide : (k + 1) * wide] = value
        for c in range(cols + 2):
            features = stage_ref[pl.ds(c, DEPTH, stride=wide), :]
            start = pl.multiple_of((r * (cols + 2) + c) * 128, 128)
            fj_ref[pl.ds(start, 128), 0:DEPTH] = features.T.astype(BF16)
        return carry

    lax.fori_loop(0, rows, row, 0)


def build_values(val_ref, pb_ref, cols):
    def row(r, carry):
        turned = val_ref[r].T
        for c in range(cols + 2):
            start = pl.multiple_of((r * (cols + 2) + c) * 128, 128)
            pb_ref[pl.ds(start, 128), :] = jnp.broadcast_to(turned[:, c : c + 1], (128, 128))
        return carry

    lax.fori_loop(0, val_ref.shape[0], row, 0)


def pair_row(r, own, base_ref, near_ref, fj_ref, pb_ref, si_ref, ws_ref, wv_ref, cols):
    x = (own[0] - ((base_ref[0] + r).astype(F32) + 0.5)) * UNIT
    y = (own[1] - column_base((cols, 128), base_ref[1])) * UNIT
    z = (own[2] - 0.5) * UNIT
    for q in range(9):
        shifted = own_features(x - (q // 3 - 1) * UNIT, y - (q % 3 - 1) * UNIT, z)
        for k, value in enumerate(shifted):
            at = (q * DEPTH + k) * cols
            si_ref[at : at + cols] = value
    listed = near_ref.shape[2]
    for c in range(cols):
        ws = jnp.zeros((8, 128), F32)
        wv = jnp.zeros((8, 128), F32)
        for k in range(listed):
            code = near_ref[r, c, k]
            up = (code * 11) >> 5
            block = (r + up) * (cols + 2) + c + code - up * 3
            start = pl.multiple_of(block * 128, 128)
            features = si_ref[pl.ds(code * (DEPTH * cols) + c, DEPTH, stride=cols), :]
            exponent = jnp.dot(
                fj_ref[pl.ds(start, 128), 0:DEPTH],
                features.astype(BF16),
                preferred_element_type=F32,
            )
            weight = jnp.exp2(exponent)
            product = weight * pb_ref[pl.ds(start, 128), :]
            ws = ws + jnp.sum(weight.reshape(16, 8, 128), axis=0)
            wv = wv + jnp.sum(product.reshape(16, 8, 128), axis=0)
        ws_ref[r, c : c + 1] = jnp.sum(ws, axis=0, keepdims=True) * kernel_scale
        wv_ref[r, c : c + 1] = jnp.sum(wv, axis=0, keepdims=True) * kernel_scale


def sweep_kernel(
    first, base_ref, near_ref, pos_ref, own_ref, val_ref, p_ref, source_ref, stiff_ref, *rest
):
    if first:
        p_out, fj_ref, pb_ref, si_ref, ws_ref, wv_ref, stage_ref = rest
    else:
        fj_ref, p_out, error_ref, pb_ref, si_ref, ws_ref, wv_ref = rest
    rows, cols = p_ref.shape[0], p_ref.shape[1]
    if first:
        build_near(pos_ref, base_ref, fj_ref, stage_ref, cols)
    si_ref[...] = jnp.zeros_like(si_ref)
    build_values(val_ref, pb_ref, cols)

    def row(r, carry):
        own = [own_ref[d, r] for d in range(3)]
        pair_row(r, own, base_ref, near_ref, fj_ref, pb_ref, si_ref, ws_ref, wv_ref, cols)
        return carry

    lax.fori_loop(0, rows, row, 0)
    pressure = p_ref[...]
    diagonal = stiff_ref[...] + ws_ref[...]
    residual = source_ref[...] - (diagonal * pressure - wv_ref[...])
    p_out[...] = jnp.maximum(pressure + relax_factor * residual / diagonal, 0.0)
    if not first:
        error_ref[...] = jnp.sum(residual * residual, axis=0)


def wall_kernel(
    base_ref, near_ref, own_ref, val_ref, live_ref, fj_ref, out_ref, pb_ref, si_ref, ws_ref, wv_ref
):
    rows, cols = out_ref.shape[0], out_ref.shape[1]
    si_ref[...] = jnp.zeros_like(si_ref)
    build_values(val_ref, pb_ref, cols)

    def row(r, carry):
        own = [own_ref[d, r] for d in range(3)]
        pair_row(r, own, base_ref, near_ref, fj_ref, pb_ref, si_ref, ws_ref, wv_ref, cols)
        return carry

    lax.fori_loop(0, rows, row, 0)
    out_ref[...] = wv_ref[...] / (wall_offset + ws_ref[...]) * live_ref[...].astype(F32)


def scatter_kernel(
    per,
    owned,
    spare,
    wp_ref,
    normal_ref,
    arm_ref,
    body_ref,
    error_ref,
    out_ref,
    first_ref,
    last_ref,
    stage_ref,
    hot_ref,
    acc_ref,
):
    rows, cols = wp_ref.shape[0], wp_ref.shape[1]
    tiles, parts = lax.axis_size("tile"), lax.axis_size("body")
    shard = per * tiles
    for r in range(rows):
        top, _ = two_level(body_ref[r], owned, shard)
        first_ref[r] = jnp.min(top)
        last_ref[r] = jnp.max(top)
    acc_ref[...] = jnp.zeros_like(acc_ref)
    stage_ref[...] = jnp.zeros_like(stage_ref)
    low_iota = lax.broadcasted_iota(jnp.int32, (LOW, 128), 0)
    lines = WINDOW * 16

    def row(r, carry):
        wp = wp_ref[r]
        fx, fy, fz = [wp * normal_ref[d, r] for d in range(3)]
        ax, ay, az = [arm_ref[d, r] for d in range(3)]
        values = [fx, fy, fz, ay * fz - az * fy, az * fx - ax * fz, ax * fy - ay * fx]
        split = [pieces(value, 2) for value in values]
        top, low = two_level(body_ref[r], owned, shard)
        for c in range(cols):
            hot_ref[:, c * 128 : (c + 1) * 128] = (
                (low_iota == low[c : c + 1]).astype(F32).astype(BF16)
            )
        first = first_ref[r]

        def window(j, carry):
            start = first + j * WINDOW
            for w in range(WINDOW):
                here = top == start + w
                for q in range(6):
                    for s in range(2):
                        at = (w * 16 + s * 8 + q) * cols
                        stage_ref[at : at + cols] = jnp.where(here, split[q][s], 0.0)
            total = jnp.zeros((lines, LOW), F32)
            for c in range(0, cols, 2):
                lhs = jnp.concatenate(
                    [stage_ref[pl.ds(c + e, lines, stride=cols), :] for e in range(2)], axis=1
                )
                total = total + lax.dot_general(
                    lhs.astype(BF16),
                    hot_ref[:, c * 128 : (c + 2) * 128],
                    (((1,), (1,)), ((), ())),
                    preferred_element_type=F32,
                )
            for w in range(WINDOW):
                found = total[w * 16 : w * 16 + 8] + total[w * 16 + 8 : w * 16 + 16]
                acc_ref[start + w] += found
            return carry

        lax.fori_loop(0, (last_ref[r] - first) // WINDOW + 1, window, 0)
        return carry

    lax.fori_loop(0, rows, row, 0)
    lane = lax.broadcasted_iota(jnp.int32, (8, LOW), 1)
    acc_ref[spare] = jnp.where(lane == 0, jnp.sum(error_ref[...]), 0.0)
    for p in range(parts):
        for t in range(tiles):
            for n in range(per):
                moved = acc_ref[p * shard + t * per + n]
                for q in range(6):
                    out_ref[t % 2, t // 2, p, q * per + n : q * per + n + 1] = moved[q : q + 1]


def gather_kernel(
    per, owned, first_ref, last_ref, table_ref, arm_ref, body_ref, out_ref, own_ref, error_ref
):
    rows, cols = body_ref.shape[0], body_ref.shape[1]
    tiles, parts = lax.axis_size("tile"), lax.axis_size("body")
    shard = per * tiles
    spare = -(-owned // LOW)
    b = lax.axis_index("body")

    def line(place, q):
        p, rest = place // shard, place % shard
        t, n = rest // per, rest % per
        return table_ref[t % 2, t // 2, p, pl.ds(q * per + n, 1), :]

    def row(r, carry):
        top, low = two_level(body_ref[r], owned, shard)
        first, last = first_ref[r], last_ref[r]

        def window(j, got):
            start = first + j * WINDOW
            for w in range(WINDOW):
                here = top == start + w
                place = jnp.minimum(start + w, last)
                got = tuple(
                    jnp.where(
                        here,
                        jnp.take_along_axis(
                            jnp.broadcast_to(line(place, q), (cols, LOW)),
                            low,
                            axis=1,
                            mode="promise_in_bounds",
                        ),
                        got[q],
                    )
                    for q in range(6)
                )
            return got

        zero = jnp.zeros((cols, LOW), F32)
        vx, vy, vz, wx, wy, wz = lax.fori_loop(
            0, (last - first) // WINDOW + 1, window, (zero,) * 6
        )
        ax, ay, az = [arm_ref[d, r] for d in range(3)]
        out_ref[0, r] = vx + (wy * az - wz * ay)
        out_ref[1, r] = vy + (wz * ax - wx * az)
        out_ref[2, r] = vz + (wx * ay - wy * ax)
        return carry

    lax.fori_loop(0, rows, row, 0)
    for n in range(spare):
        wide = min(LOW, owned - n * LOW)
        for q in range(6):
            own_ref[q : q + 1, n * LOW : n * LOW + wide] = line(b * shard + n, q)[:, :wide]
    error_ref[...] = line(spare, 0)


def remote(src, dst, send, recv, device):
    return pltpu.make_async_remote_copy(
        src_ref=src,
        dst_ref=dst,
        send_sem=send,
        recv_sem=recv,
        device_id=device,
        device_id_type=pl.DeviceIdType.MESH,
    )


WAYS = ((-1, 0), (1, 0), (0, -1), (0, 1), (-1, -1), (-1, 1), (1, -1), (1, 1))


def halo_kernel(x_ref, out_ref, row_in, col_send, col_in, corner_send, corner_in, send, recv):
    depth, rows, cols, _ = x_ref.shape
    tiles, parts = lax.axis_size("tile"), lax.axis_size("body")
    t, b = lax.axis_index("tile"), lax.axis_index("body")

    def exists(dt, db):
        ok = jnp.bool_(True)
        if dt:
            ok = (t > 0) if dt < 0 else (t < tiles - 1)
        if db:
            side = (b > 0) if db < 0 else (b < parts - 1)
            ok = jnp.logical_and(ok, side) if dt else side
        return ok

    barrier = pltpu.get_barrier_semaphore()
    for dt, db in WAYS:

        @pl.when(exists(dt, db))
        def _():
            pl.semaphore_signal(
                barrier, inc=1, device_id=(t + dt, b + db), device_id_type=pl.DeviceIdType.MESH
            )

    for side in range(2):
        col_send[side] = x_ref[:, :, side * (cols - 1), :]
    for n, (dt, db) in enumerate(WAYS[4:]):
        r, c = (dt > 0) * (rows - 1), (db > 0) * (cols - 1)
        for d in range(depth):
            corner_send[n, d : d + 1] = x_ref[d, r, c : c + 1]

    along = 1 + (t > 0).astype(jnp.int32) + (t < tiles - 1).astype(jnp.int32)
    across = 1 + (b > 0).astype(jnp.int32) + (b < parts - 1).astype(jnp.int32)
    pl.semaphore_wait(barrier, along * across - 1)

    def copy(n):
        dt, db = WAYS[n]
        if n < 2:
            src, dst = x_ref.at[:, (dt > 0) * (rows - 1)], row_in.at[n]
        elif n < 4:
            src, dst = col_send.at[n - 2], col_in.at[n - 2]
        else:
            src, dst = corner_send.at[n - 4], corner_in.at[n - 4]
        return remote(src, dst, send.at[n], recv.at[n], (t + dt, b + db))

    for n, (dt, db) in enumerate(WAYS):

        @pl.when(exists(dt, db))
        def _():
            copy(n).start()

    out_ref[...] = jnp.zeros_like(out_ref)
    for d in range(depth):
        for r in range(rows):
            out_ref[d, r + 1, 1 : cols + 1] = x_ref[d, r]
    for n, (dt, db) in enumerate(WAYS):

        @pl.when(exists(-dt, -db))
        def _():
            copy(n).wait_recv()
            r = 0 if dt > 0 else rows + 1
            c = 0 if db > 0 else cols + 1
            for d in range(depth):
                if n < 2:
                    out_ref[d, r, 1 : cols + 1] = row_in[n, d]
                elif n < 4:
                    for i in range(rows):
                        out_ref[d, i + 1, c : c + 1] = col_in[n - 2, d, i : i + 1]
                else:
                    out_ref[d, r, c : c + 1] = corner_in[n - 4, d : d + 1]

    for n, (dt, db) in enumerate(WAYS):

        @pl.when(exists(dt, db))
        def _():
            copy(n).wait_send()


def halo(x, number):
    depth, rows, cols, _ = x.shape
    wide = -(-(cols + 2) // 8) * 8
    return pl.pallas_call(
        halo_kernel,
        out_shape=shape((depth, rows + 2, wide, 128)),
        in_specs=[pl.BlockSpec(memory_space=VMEM)],
        out_specs=pl.BlockSpec(memory_space=VMEM),
        scratch_shapes=[
            VMEM((2, depth, cols, 128), F32),
            VMEM((2, depth, rows, 128), F32),
            VMEM((2, depth, rows, 128), F32),
            VMEM((4, 8, 128), F32),
            VMEM((4, 8, 128), F32),
            pltpu.SemaphoreType.DMA((8,)),
            pltpu.SemaphoreType.DMA((8,)),
        ],
        compiler_params=pltpu.CompilerParams(collective_id=number, has_side_effects=True),
        name="halo%d" % number,
    )(x)


def exchange_kernel(
    per,
    partial_ref,
    params_ref,
    g1_ref,
    r1_ref,
    s1_ref,
    r2_ref,
    s2_ref,
    r3_ref,
    g3_ref,
    g2_ref,
    send1,
    recv1,
    send2,
    recv2,
    send3,
    recv3,
):
    chips, parts = r1_ref.shape[0], r1_ref.shape[1]
    t, b = lax.axis_index("tile"), lax.axis_index("body")
    core, chip = t % 2, t // 2
    barrier = pltpu.get_barrier_semaphore()
    partner = (chip * 2 + 1 - core, b)
    others2 = [(chip + k) % chips for k in range(1, chips)]
    others3 = [(b + k) % parts for k in range(1, parts)]
    greeted = [partner] + [(g * 2 + core, b) for g in others2] + [(t, g) for g in others3]
    for device in greeted:
        pl.semaphore_signal(barrier, inc=1, device_id=device, device_id_type=pl.DeviceIdType.MESH)
    pl.semaphore_wait(barrier, len(greeted))

    first = remote(partial_ref.at[1 - core], r1_ref, send1.at[0], recv1.at[0], partner)
    first.start()
    first.wait()
    s1_ref[...] = partial_ref[core] + r1_ref[...]

    copies = [
        remote(s1_ref.at[g], r2_ref.at[chip], send2.at[g], recv2.at[chip], (g * 2 + core, b))
        for g in others2
    ]
    for item in copies:
        item.start()
    total = s1_ref[chip]
    for g in others2:
        remote(s1_ref.at[g], r2_ref.at[g], send2.at[g], recv2.at[g], partner).wait_recv()
        total = total + r2_ref[g]
    s2_ref[...] = total
    for item in copies:
        item.wait_send()

    copies = [
        remote(s2_ref.at[g], r3_ref.at[b], send3.at[g], recv3.at[b], (t, g)) for g in others3
    ]
    for item in copies:
        item.start()
    total = s2_ref[b]
    for g in others3:
        remote(s2_ref.at[g], r3_ref.at[g], send3.at[g], recv3.at[g], partner).wait_recv()
        total = total + r3_ref[g]
    for item in copies:
        item.wait_send()

    g3_ref[b] = jnp.zeros_like(total)
    mine = [params_ref[n, t] for n in range(10)]
    for q in range(6):
        moved = total[q * per : (q + 1) * per]
        if q < 3:
            state = mine[q] + time_step * (mine[6] * moved)
        else:
            state = mine[q] + time_step * mine[4 + q] * moved
        if q == 2:
            state = state + time_step * gravity_z
        g3_ref[b, q * per : (q + 1) * per] = state

    copies = [
        remote(
            g3_ref.at[b], g3_ref.at[b], send3.at[parts + g], recv3.at[parts + b], (t, g)
        )
        for g in others3
    ]
    for item in copies:
        item.start()
    for g in others3:
        remote(
            g3_ref.at[g], g3_ref.at[g], send3.at[parts + g], recv3.at[parts + g], partner
        ).wait_recv()
    for item in copies:
        item.wait_send()

    copies = [
        remote(
            g3_ref, g2_ref.at[chip], send2.at[chips + g], recv2.at[chips + chip], (g * 2 + core, b)
        )
        for g in others2
    ]
    for item in copies:
        item.start()
    g2_ref[chip] = g3_ref[...]
    for g in others2:
        remote(
            g3_ref, g2_ref.at[g], send2.at[chips + g], recv2.at[chips + g], partner
        ).wait_recv()
    for item in copies:
        item.wait_send()

    last = remote(g2_ref, g1_ref.at[core], send1.at[1], recv1.at[1 + core], partner)
    last.start()
    g1_ref[core] = g2_ref[...]
    remote(g2_ref, g1_ref.at[1 - core], send1.at[1], recv1.at[2 - core], partner).wait_recv()
    last.wait_send()


def exchange(partials, params, per):
    tiles, parts = lax.axis_size("tile"), lax.axis_size("body")
    chips = tiles // 2
    chunk = partials.shape[3:]
    dma = pltpu.SemaphoreType.DMA
    return pl.pallas_call(
        functools.partial(exchange_kernel, per),
        out_shape=shape((2, chips, parts) + chunk),
        in_specs=[pl.BlockSpec(memory_space=VMEM)] * 2,
        out_specs=pl.BlockSpec(memory_space=VMEM),
        scratch_shapes=[
            VMEM((chips, parts) + chunk, F32),
            VMEM((chips, parts) + chunk, F32),
            VMEM((chips, parts) + chunk, F32),
            VMEM((parts,) + chunk, F32),
            VMEM((parts,) + chunk, F32),
            VMEM((parts,) + chunk, F32),
            VMEM((chips, parts) + chunk, F32),
            dma((2,)),
            dma((3,)),
            dma((2 * chips,)),
            dma((2 * chips,)),
            dma((2 * parts,)),
            dma((2 * parts,)),
        ],
        compiler_params=pltpu.CompilerParams(
            collective_id=9, has_side_effects=True, vmem_limit_bytes=32 * 2**20
        ),
        name="exchange",
    )(partials, params)


def two_level(body, owned, shard):
    index = body
    for part in range(1, lax.axis_size("body")):
        index = index + jnp.where(body >= part * owned, shard * LOW - owned, 0)
    return index >> (LOW.bit_length() - 1), index & (LOW - 1)


def call(kernel, shapes, ins, scratch, spaces, name, outs=None, limit=60):
    outs = outs or jax.tree.map(lambda _: VMEM, shapes)
    return pl.pallas_call(
        kernel,
        out_shape=shapes,
        in_specs=[pl.BlockSpec(memory_space=s) for s in spaces],
        out_specs=jax.tree.map(lambda s: pl.BlockSpec(memory_space=s), outs),
        scratch_shapes=scratch,
        compiler_params=pltpu.CompilerParams(vmem_limit_bytes=limit * 2**20),
        name=name,
    )(*ins)


def shape(dims, kind=F32):
    return jax.ShapeDtypeStruct(tuple(dims), kind)


def shards(
    fluid_position,
    fluid_pressure,
    source,
    stiffness,
    neighbours,
    wall_position,
    wall_normal,
    wall_arm,
    wall_live,
    wall_body,
    linear_velocity,
    angular_velocity,
    inverse_mass,
    inverse_inertia,
):
    rows, cols, _ = fluid_pressure.shape
    blocks = (rows + 2) * (cols + 2)
    base = jnp.stack([lax.axis_index("tile") * rows, lax.axis_index("body") * cols]).astype(jnp.int32)
    both = halo(jnp.concatenate([fluid_position, fluid_pressure[None]], 0), 1)
    wide = both.shape[2]
    small = shape((rows, cols, 128))
    fj_shape = (blocks * 128, 128)
    pair_scratch = [
        VMEM((blocks * 128, 128), F32),
        VMEM((9 * DEPTH * cols, 128), F32),
        VMEM((rows, cols, 128), F32),
        VMEM((rows, cols, 128), F32),
    ]
    def opening(base_ref, near_ref, both_ref, own_ref, *rest):
        sweep_kernel(
            True, base_ref, near_ref, both_ref, own_ref, both_ref.at[both_ref.shape[0] - 1], *rest
        )

    pressure, near = call(
        opening,
        (small, shape(fj_shape, BF16)),
        (base, neighbours, both, fluid_position, fluid_pressure, source, stiffness),
        pair_scratch + [VMEM((DEPTH * wide, 128), F32)],
        [SMEM] * 2 + [VMEM] * 5,
        "sweep_first",
    )

    def second(base_ref, near_ref, own_ref, val_ref, *rest):
        sweep_kernel(False, base_ref, near_ref, None, own_ref, val_ref, *rest)

    pressure, error = call(
        second,
        (small, shape((cols, 128))),
        (base, neighbours, fluid_position, halo(pressure[None], 2)[0], pressure, source, stiffness, near),
        pair_scratch,
        [SMEM] * 2 + [VMEM] * 6,
        "sweep_second",
    )
    wall_pressure = call(
        wall_kernel,
        small,
        (base, neighbours, wall_position, halo(pressure[None], 3)[0], wall_live, near),
        pair_scratch,
        [SMEM] * 2 + [VMEM] * 4,
        "wall",
    )
    particle_total = rows * cols * 128 * lax.axis_size("tile") * lax.axis_size("body")
    owned = inverse_mass.shape[0]
    tiles = lax.axis_size("tile")
    parts = lax.axis_size("body")
    spare = -(-owned // LOW)
    per = spare // tiles + 1
    shard = per * tiles
    chunk = (-(-6 * per // 8) * 8, LOW)
    spans = shape((rows,), jnp.int32)
    partials, first, last = call(
        functools.partial(scatter_kernel, per, owned, spare),
        (shape((2, tiles // 2, parts) + chunk), spans, spans),
        (wall_pressure, wall_normal, wall_arm, wall_body, error),
        [
            VMEM((WINDOW * 16 * cols, 128), F32),
            VMEM((LOW, cols * 128), BF16),
            VMEM((parts * shard + WINDOW, 8, LOW), F32),
        ],
        [VMEM] * 5,
        "scatter",
        (VMEM, SMEM, SMEM),
        16,
    )
    params = jnp.concatenate(
        [linear_velocity, angular_velocity, inverse_mass[None], inverse_inertia], 0
    )
    fill = jnp.zeros((10, shard * LOW - owned), F32).at[6].set(1.0 / time_step)
    params = jnp.concatenate([params, fill], 1).reshape(10, tiles, per, LOW)
    table = exchange(partials, params, per)
    wall_velocity, own_state, error = call(
        functools.partial(gather_kernel, per, owned),
        (shape((3, rows, cols, 128)), shape((6, owned)), shape((1, LOW))),
        (first, last, table, wall_arm, wall_body),
        [],
        [SMEM] * 2 + [VMEM] * 3,
        "gather",
        None,
        16,
    )
    density_error = error[0, 0] / particle_total
    return (pressure, wall_pressure, own_state, wall_velocity, density_error)


def solution(mesh):
    placed = (
        P(None, "tile", "body", None),
        P("tile", "body", None),
        P("tile", "body", None),
        P("tile", "body", None),
        P("tile", "body", None),
        P(None, "tile", "body", None),
        P(None, "tile", "body", None),
        P(None, "tile", "body", None),
        P("tile", "body", None),
        P("tile", "body", None),
        P(None, "body"),
        P(None, "body"),
        P("body"),
        P(None, "body"),
    )
    return jax.shard_map(
        shards,
        mesh=mesh,
        in_specs=placed,
        out_specs=(
            P("tile", "body", None),
            P("tile", "body", None),
            P(None, "body"),
            P(None, "tile", "body", None),
            P(),
        ),
        check_vma=False,
    )
```

```python
import math
import functools
import jax
import jax.numpy as jnp
from jax import lax
from jax.experimental import pallas as pl
from jax.experimental.pallas import tpu as pltpu
from jax.sharding import PartitionSpec as P

SWEEPS = 2

relax_factor = 0.5
inv_width = 2.0
kernel_scale = 0.0078125
wall_offset = 0.5
time_step = 0.25
gravity_z = -9.81

UNIT = math.sqrt(inv_width / math.log(2.0))
DEPTH = 32
LOW = 128
WINDOW = 6
TABLE = 7
GROUP = 4
F32, BF16 = jnp.float32, jnp.bfloat16
VMEM = pltpu.VMEM
SMEM = pltpu.SMEM


def pieces(x, count):
    out = []
    for _ in range(count):
        piece = x.astype(BF16).astype(F32)
        out.append(piece)
        x = x - piece
    return out


def near_rows(x):
    h, m, l = pieces(x, 3)
    return [h, m, h, l, h] + pieces(-(x * x), 3)


def own_rows(x):
    h, m, l = pieces(2.0 * x, 3)
    one = jnp.ones_like(x)
    return [h, h, m, h, l, one, one, one]


def centre(first, size, axis):
    at = first + lax.broadcasted_iota(jnp.int32, (size, 128), 0) if axis else first
    return at.astype(F32) + 0.5


def build_near(tab_ref, start, stride, x, y, z):
    count = x.shape[0]
    groups = [near_rows(x + (v - 1) * UNIT) for v in range(3)]
    groups += [near_rows(y + (v - 1) * UNIT) for v in range(3)]
    groups += [near_rows(z)]
    for g, group in enumerate(groups):
        for k, value in enumerate(group):
            if count == 1:
                tab_ref[start + g, k : k + 1] = value
            else:
                tab_ref[pl.ds(start + g, count, stride=stride * TABLE), k, :] = value


def build_own(pos_ref, lhs_ref, stage_ref, bx, by):
    rows, cols = pos_ref.shape[1], pos_ref.shape[2]
    stage_ref[...] = jnp.zeros_like(stage_ref)

    def group(i, carry):
        for e in range(GROUP):
            r = i * GROUP + e
            x = (pos_ref[0, r] - centre(bx + r, cols, 0)) * UNIT
            y = (pos_ref[1, r] - centre(by, cols, 1)) * UNIT
            z = (pos_ref[2, r] - 0.5) * UNIT
            norm = pieces(-(x * x + y * y + z * z), 3)
            for k, value in enumerate(own_rows(x) + own_rows(y) + own_rows(z) + norm):
                stage_ref[e, k * cols : (k + 1) * cols] = value
        for e in range(GROUP):
            for c in range(cols):
                start = pl.multiple_of(((i * GROUP + e) * cols + c) * 128, 128)
                turned = stage_ref[e, pl.ds(c, DEPTH, stride=cols), :].T
                lhs_ref[pl.ds(start, 128), 0:DEPTH] = turned.astype(BF16)
        return carry

    lax.fori_loop(0, rows // GROUP, group, 0)


def pair_block(r, c, near_ref, tab_ref, val_ref, lhs_ref, keep_ref, cols):
    ones = (lax.broadcasted_iota(jnp.int32, (8, 128), 0) < 3).astype(F32)
    listed = near_ref.shape[0]
    sides, values = [], []
    for k in range(listed):
        code = near_ref[k, c, r]
        up = (code * 11) >> 5
        side = code - up * 3
        base = ((r + up) * (cols + 2) + c + side) * TABLE
        rows = [tab_ref[at] for at in (base + up, base + 3 + side, base + 6)]
        sides.append(jnp.concatenate(rows + [ones], axis=0).astype(BF16))
        values.append(val_ref[pl.ds((r + up) * 16 + c + side, 1), :])
    block = r * cols + c
    lhs = lhs_ref[pl.ds(pl.multiple_of(block * 128, 128), 128), 0:DEPTH]
    ws = wv = None
    for k in range(0, listed, 2):
        exponent = jnp.dot(
            lhs, jnp.concatenate(sides[k : k + 2], axis=1), preferred_element_type=F32
        )
        weight = jnp.exp2(exponent)
        for e in range(2):
            part = weight[:, e * 128 : (e + 1) * 128]
            if keep_ref is not None:
                at = pl.multiple_of((block * listed + k + e) * 128, 128)
                keep_ref[pl.ds(at, 128), :] = part
            product = part * values[k + e]
            ws = part if ws is None else ws + part
            wv = product if wv is None else wv + product
    return [jnp.sum(total.T, axis=0, keepdims=True) * kernel_scale for total in (ws, wv)]


def kept_block(r, c, near_ref, val_ref, keep_ref, cols):
    listed = near_ref.shape[0]
    block = r * cols + c
    wv = None
    for k in range(listed):
        code = near_ref[k, c, r]
        up = (code * 11) >> 5
        value = val_ref[pl.ds((r + up) * 16 + c + code - up * 3, 1), :]
        at = pl.multiple_of((block * listed + k) * 128, 128)
        product = keep_ref[pl.ds(at, 128), :] * value
        wv = product if wv is None else wv + product
    return jnp.sum(wv.T, axis=0, keepdims=True) * kernel_scale


WAYS = ((-1, 0), (1, 0), (0, -1), (0, 1), (-1, -1), (-1, 1), (1, -1), (1, 1))


def fluid_kernel(
    near_ref,
    pos_ref,
    p_ref,
    source_ref,
    stiff_ref,
    wall_ref,
    live_ref,
    p_out,
    wp_out,
    error_out,
    tab_ref,
    val_ref,
    lhs_ref,
    keep_ref,
    stage_ref,
    ws_ref,
    wv_ref,
    mid_ref,
    row_send,
    row_in,
    col_send,
    col_in,
    corner_send,
    corner_in,
    row_in2,
    col_send2,
    col_in2,
    corner_send2,
    corner_in2,
    send,
    recv,
):
    rows, cols = p_ref.shape[0], p_ref.shape[1]
    tiles, parts = lax.axis_size("tile"), lax.axis_size("body")
    t, b = lax.axis_index("tile"), lax.axis_index("body")
    bx, by = t * rows, b * cols

    def exists(dt, db):
        ok = jnp.bool_(True)
        if dt:
            ok = (t > 0) if dt < 0 else (t < tiles - 1)
        if db:
            side = (b > 0) if db < 0 else (b < parts - 1)
            ok = jnp.logical_and(ok, side) if dt else side
        return ok

    barrier = pltpu.get_barrier_semaphore()
    for dt, db in WAYS:

        @pl.when(exists(dt, db))
        def _():
            pl.semaphore_signal(
                barrier, inc=1, device_id=(t + dt, b + db), device_id_type=pl.DeviceIdType.MESH
            )

    def copy(phase, n):
        dt, db = WAYS[n]
        if n < 2:
            src = row_send.at[n] if phase == 0 else (mid_ref, p_out)[phase - 1].at[n * (rows - 1)]
            dst = row_in.at[n] if phase == 0 else row_in2.at[phase - 1, n]
        elif n < 4:
            src = col_send.at[n - 2] if phase == 0 else col_send2.at[phase - 1, n - 2]
            dst = col_in.at[n - 2] if phase == 0 else col_in2.at[phase - 1, n - 2]
        else:
            src = corner_send.at[n - 4] if phase == 0 else corner_send2.at[phase - 1, n - 4]
            dst = corner_in.at[n - 4] if phase == 0 else corner_in2.at[phase - 1, n - 4]
        return remote(src, dst, send.at[phase, n], recv.at[phase, n], (t + dt, b + db))

    def launch(phase):
        for n, (dt, db) in enumerate(WAYS):

            @pl.when(exists(dt, db))
            def _():
                copy(phase, n).start()

    def arrive(phase):
        for n, (dt, db) in enumerate(WAYS):

            @pl.when(exists(-dt, -db))
            def _():
                copy(phase, n).wait_recv()

    def depart(phase):
        for n, (dt, db) in enumerate(WAYS):

            @pl.when(exists(dt, db))
            def _():
                copy(phase, n).wait_send()

    def pack(phase, ref):
        for side in range(2):
            for r in range(rows):
                line = ref[r, side * (cols - 1) : side * (cols - 1) + 1]
                col_send2[phase - 1, side, r : r + 1] = line
        for n, (dt, db) in enumerate(WAYS[4:]):
            r, c = (dt > 0) * (rows - 1), (db > 0) * (cols - 1)
            corner_send2[phase - 1, n, 0:1] = ref[r, c : c + 1]

    fields = [(pos_ref, d) for d in range(3)] + [(p_ref, None)]
    for d, (ref, at) in enumerate(fields):
        view = ref if at is None else ref.at[at]
        for side in range(2):
            row_send[side, d] = view[side * (rows - 1)]
            for r in range(rows):
                line = view[r, side * (cols - 1) : side * (cols - 1) + 1]
                col_send[side, d, r : r + 1] = line
        for n, (dt, db) in enumerate(WAYS[4:]):
            r, c = (dt > 0) * (rows - 1), (db > 0) * (cols - 1)
            corner_send[n, d : d + 1] = view[r, c : c + 1]

    along = 1 + (t > 0).astype(jnp.int32) + (t < tiles - 1).astype(jnp.int32)
    across = 1 + (b > 0).astype(jnp.int32) + (b < parts - 1).astype(jnp.int32)
    pl.semaphore_wait(barrier, along * across - 1)
    launch(0)

    build_own(pos_ref, lhs_ref, stage_ref, bx, by)

    def near_row(r, carry):
        x = (pos_ref[0, r] - centre(bx + r, cols, 0)) * UNIT
        y = (pos_ref[1, r] - centre(by, cols, 1)) * UNIT
        z = (pos_ref[2, r] - 0.5) * UNIT
        build_near(tab_ref, ((r + 1) * (cols + 2) + 1) * TABLE, 1, x, y, z)
        return carry

    lax.fori_loop(0, rows, near_row, 0)

    def fill(ref):
        for r in range(rows):
            val_ref[(r + 1) * 16 + 1 : (r + 1) * 16 + 1 + cols] = ref[r]

    def slots(n):
        dt, db = WAYS[n]
        return (0 if dt > 0 else rows + 1), (0 if db > 0 else cols + 1)

    def halo_values(phase):
        for n, (dt, db) in enumerate(WAYS):
            ok = exists(-dt, -db)
            r, c = slots(n)
            if n < 2:
                got = row_in[n, 3] if phase == 0 else row_in2[phase - 1, n]
                val_ref[r * 16 + 1 : r * 16 + 1 + cols] = jnp.where(ok, got, 0.0)
            elif n < 4:
                got = col_in[n - 2, 3] if phase == 0 else col_in2[phase - 1, n - 2]
                val_ref[pl.ds(16 + c, rows, stride=16), :] = jnp.where(ok, got, 0.0)
            else:
                got = (
                    corner_in[n - 4, 3:4]
                    if phase == 0
                    else corner_in2[phase - 1, n - 4, 0:1]
                )
                val_ref[r * 16 + c : r * 16 + c + 1] = jnp.where(ok, got, 0.0)

    def halo_tables():
        for n, (dt, db) in enumerate(WAYS):
            ok = exists(-dt, -db)
            r, c = slots(n)
            across_r = bx - 1 if dt > 0 else bx + rows
            across_c = by - 1 if db > 0 else by + cols
            if n < 2:
                x, y, z = [jnp.where(ok, row_in[n, d], 0.0) for d in range(3)]
                x = x - centre(across_r, cols, 0)
                y = y - centre(by, cols, 1)
                start, stride = (r * (cols + 2) + 1) * TABLE, 1
            elif n < 4:
                x, y, z = [jnp.where(ok, col_in[n - 2, d], 0.0) for d in range(3)]
                x = x - centre(bx, rows, 1)
                y = y - centre(across_c, rows, 0)
                start, stride = (cols + 2 + c) * TABLE, cols + 2
            else:
                x, y, z = [jnp.where(ok, corner_in[n - 4, d : d + 1], 0.0) for d in range(3)]
                x = x - centre(across_r, 1, 0)
                y = y - centre(across_c, 1, 0)
                start, stride = (r * (cols + 2) + c) * TABLE, 1
            build_near(tab_ref, start, stride, x * UNIT, y * UNIT, (z - 0.5) * UNIT)

    def sweep(first, meet):
        def block(r, c):
            if first is None:
                wv = kept_block(r, c, near_ref, val_ref, keep_ref, cols)
            else:
                ws, wv = pair_block(
                    r, c, near_ref, tab_ref, val_ref, lhs_ref, keep_ref if first else None, cols
                )
                ws_ref[r, pl.ds(c, 1), :] = ws
            wv_ref[r, pl.ds(c, 1), :] = wv

        def column(c, carry):
            for r in range(1, rows - 1):
                block(r, c)
            return carry

        lax.fori_loop(1, cols - 1, column, 0)
        meet()
        lax.fori_loop(0, 2, lambda i, carry: column(i * (cols - 1), carry), 0)

        def end(i, carry):
            for c in range(cols):
                block(i * (rows - 1), c)
            return carry

        lax.fori_loop(0, 2, end, 0)

    fill(p_ref)

    def meet(phase):
        arrive(phase)
        if phase == 0:
            halo_tables()
        halo_values(phase)

    def relax(before_ref, after_ref):
        pressure = before_ref[...]
        diagonal = stiff_ref[...] + ws_ref[...]
        residual = source_ref[...] - (diagonal * pressure - wv_ref[...])
        after_ref[...] = jnp.maximum(pressure + relax_factor * residual / diagonal, 0.0)
        return residual

    sweep(True, lambda: meet(0))
    relax(p_ref, mid_ref)
    pack(1, mid_ref)
    launch(1)
    fill(mid_ref)
    build_own(wall_ref, lhs_ref, stage_ref, bx, by)
    sweep(None, lambda: meet(1))
    residual = relax(mid_ref, p_out)
    pack(2, p_out)
    launch(2)
    error_out[...] = jnp.sum(residual * residual, axis=0)
    fill(p_out)
    sweep(False, lambda: meet(2))
    wp_out[...] = wv_ref[...] / (wall_offset + ws_ref[...]) * live_ref[...].astype(F32)
    for phase in range(3):
        depart(phase)


def fluid(near, pos, p, source, stiff, wall, live):
    rows, cols, _ = p.shape
    small = shape((rows, cols, 128))
    return pl.pallas_call(
        fluid_kernel,
        out_shape=(small, small, shape((cols, 128))),
        in_specs=[pl.BlockSpec(memory_space=SMEM)] + [pl.BlockSpec(memory_space=VMEM)] * 6,
        out_specs=(pl.BlockSpec(memory_space=VMEM),) * 3,
        scratch_shapes=[
            VMEM(((rows + 2) * (cols + 2) * TABLE, 8, 128), F32),
            VMEM(((rows + 2) * 16, 128), F32),
            VMEM((rows * cols * 128, 128), BF16),
            VMEM((rows * cols * near.shape[0] * 128, 128), F32),
            VMEM((GROUP, DEPTH * cols, 128), F32),
            VMEM((rows, cols, 128), F32),
            VMEM((rows, cols, 128), F32),
            VMEM((rows, cols, 128), F32),
            VMEM((2, 4, cols, 128), F32),
            VMEM((2, 4, cols, 128), F32),
            VMEM((2, 4, rows, 128), F32),
            VMEM((2, 4, rows, 128), F32),
            VMEM((4, 8, 128), F32),
            VMEM((4, 8, 128), F32),
            VMEM((2, 2, cols, 128), F32),
            VMEM((2, 2, rows, 128), F32),
            VMEM((2, 2, rows, 128), F32),
            VMEM((2, 4, 8, 128), F32),
            VMEM((2, 4, 8, 128), F32),
            pltpu.SemaphoreType.DMA((3, 8)),
            pltpu.SemaphoreType.DMA((3, 8)),
        ],
        compiler_params=pltpu.CompilerParams(
            collective_id=1, has_side_effects=True, vmem_limit_bytes=62 * 2**20
        ),
        name="fluid",
    )(near, pos, p, source, stiff, wall, live)


def scatter_kernel(
    per,
    owned,
    spare,
    wp_ref,
    normal_ref,
    arm_ref,
    body_ref,
    error_ref,
    out_ref,
    first_ref,
    last_ref,
    stage_ref,
    hot_ref,
    acc_ref,
):
    rows, cols = wp_ref.shape[0], wp_ref.shape[1]
    tiles, parts = lax.axis_size("tile"), lax.axis_size("body")
    shard = per * tiles
    for r in range(rows):
        top, _ = two_level(body_ref[r], owned, shard)
        first_ref[r] = jnp.min(top)
        last_ref[r] = jnp.max(top)
    acc_ref[...] = jnp.zeros_like(acc_ref)
    stage_ref[...] = jnp.zeros_like(stage_ref)
    low_iota = lax.broadcasted_iota(jnp.int32, (LOW, 128), 0)
    lines = WINDOW * 16

    def row(r, carry):
        wp = wp_ref[r]
        fx, fy, fz = [wp * normal_ref[d, r] for d in range(3)]
        ax, ay, az = [arm_ref[d, r] for d in range(3)]
        values = [fx, fy, fz, ay * fz - az * fy, az * fx - ax * fz, ax * fy - ay * fx]
        split = [pieces(value, 2) for value in values]
        top, low = two_level(body_ref[r], owned, shard)
        for c in range(cols):
            hot_ref[:, c * 128 : (c + 1) * 128] = (
                (low_iota == low[c : c + 1]).astype(F32).astype(BF16)
            )
        first = first_ref[r]

        def window(j, carry):
            start = first + j * WINDOW
            for w in range(WINDOW):
                here = top == start + w
                for q in range(6):
                    for s in range(2):
                        at = (w * 16 + s * 8 + q) * cols
                        stage_ref[at : at + cols] = jnp.where(here, split[q][s], 0.0)
            total = jnp.zeros((lines, LOW), F32)
            for c in range(0, cols, 2):
                lhs = jnp.concatenate(
                    [stage_ref[pl.ds(c + e, lines, stride=cols), :] for e in range(2)], axis=1
                )
                total = total + lax.dot_general(
                    lhs.astype(BF16),
                    hot_ref[:, c * 128 : (c + 2) * 128],
                    (((1,), (1,)), ((), ())),
                    preferred_element_type=F32,
                )
            for w in range(WINDOW):
                found = total[w * 16 : w * 16 + 8] + total[w * 16 + 8 : w * 16 + 16]
                acc_ref[start + w] += found
            return carry

        lax.fori_loop(0, (last_ref[r] - first) // WINDOW + 1, window, 0)
        return carry

    lax.fori_loop(0, rows, row, 0)
    lane = lax.broadcasted_iota(jnp.int32, (8, LOW), 1)
    acc_ref[spare] = jnp.where(lane == 0, jnp.sum(error_ref[...]), 0.0)
    for p in range(parts):
        for t in range(tiles):
            for n in range(per):
                moved = acc_ref[p * shard + t * per + n]
                for q in range(6):
                    out_ref[t % 2, t // 2, p, q * per + n : q * per + n + 1] = moved[q : q + 1]


def gather_kernel(
    per, owned, first_ref, last_ref, table_ref, arm_ref, body_ref, out_ref, own_ref, error_ref
):
    rows, cols = body_ref.shape[0], body_ref.shape[1]
    tiles, parts = lax.axis_size("tile"), lax.axis_size("body")
    shard = per * tiles
    spare = -(-owned // LOW)
    b = lax.axis_index("body")

    def line(place, q):
        p, rest = place // shard, place % shard
        t, n = rest // per, rest % per
        return table_ref[t % 2, t // 2, p, pl.ds(q * per + n, 1), :]

    def row(r, carry):
        top, low = two_level(body_ref[r], owned, shard)
        first, last = first_ref[r], last_ref[r]

        def window(j, got):
            start = first + j * WINDOW
            for w in range(WINDOW):
                here = top == start + w
                place = jnp.minimum(start + w, last)
                got = tuple(
                    jnp.where(
                        here,
                        jnp.take_along_axis(
                            jnp.broadcast_to(line(place, q), (cols, LOW)),
                            low,
                            axis=1,
                            mode="promise_in_bounds",
                        ),
                        got[q],
                    )
                    for q in range(6)
                )
            return got

        zero = jnp.zeros((cols, LOW), F32)
        vx, vy, vz, wx, wy, wz = lax.fori_loop(
            0, (last - first) // WINDOW + 1, window, (zero,) * 6
        )
        ax, ay, az = [arm_ref[d, r] for d in range(3)]
        out_ref[0, r] = vx + (wy * az - wz * ay)
        out_ref[1, r] = vy + (wz * ax - wx * az)
        out_ref[2, r] = vz + (wx * ay - wy * ax)
        return carry

    lax.fori_loop(0, rows, row, 0)
    for n in range(spare):
        wide = min(LOW, owned - n * LOW)
        for q in range(6):
            own_ref[q : q + 1, n * LOW : n * LOW + wide] = line(b * shard + n, q)[:, :wide]
    error_ref[...] = line(spare, 0)


def remote(src, dst, send, recv, device):
    return pltpu.make_async_remote_copy(
        src_ref=src,
        dst_ref=dst,
        send_sem=send,
        recv_sem=recv,
        device_id=device,
        device_id_type=pl.DeviceIdType.MESH,
    )


def exchange_kernel(
    per,
    partial_ref,
    params_ref,
    g1_ref,
    r1_ref,
    s1_ref,
    r2_ref,
    s2_ref,
    r3_ref,
    g3_ref,
    g2_ref,
    send1,
    recv1,
    send2,
    recv2,
    send3,
    recv3,
):
    chips, parts = r1_ref.shape[0], r1_ref.shape[1]
    t, b = lax.axis_index("tile"), lax.axis_index("body")
    core, chip = t % 2, t // 2
    barrier = pltpu.get_barrier_semaphore()
    partner = (chip * 2 + 1 - core, b)
    others2 = [(chip + k) % chips for k in range(1, chips)]
    others3 = [(b + k) % parts for k in range(1, parts)]
    greeted = [partner] + [(g * 2 + core, b) for g in others2] + [(t, g) for g in others3]
    for device in greeted:
        pl.semaphore_signal(barrier, inc=1, device_id=device, device_id_type=pl.DeviceIdType.MESH)
    pl.semaphore_wait(barrier, len(greeted))

    first = remote(partial_ref.at[1 - core], r1_ref, send1.at[0], recv1.at[0], partner)
    first.start()
    first.wait()
    s1_ref[...] = partial_ref[core] + r1_ref[...]

    copies = [
        remote(s1_ref.at[g], r2_ref.at[chip], send2.at[g], recv2.at[chip], (g * 2 + core, b))
        for g in others2
    ]
    for item in copies:
        item.start()
    total = s1_ref[chip]
    for g in others2:
        remote(s1_ref.at[g], r2_ref.at[g], send2.at[g], recv2.at[g], partner).wait_recv()
        total = total + r2_ref[g]
    s2_ref[...] = total
    for item in copies:
        item.wait_send()

    copies = [
        remote(s2_ref.at[g], r3_ref.at[b], send3.at[g], recv3.at[b], (t, g)) for g in others3
    ]
    for item in copies:
        item.start()
    total = s2_ref[b]
    for g in others3:
        remote(s2_ref.at[g], r3_ref.at[g], send3.at[g], recv3.at[g], partner).wait_recv()
        total = total + r3_ref[g]
    for item in copies:
        item.wait_send()

    g3_ref[b] = jnp.zeros_like(total)
    mine = [params_ref[n, t] for n in range(10)]
    for q in range(6):
        moved = total[q * per : (q + 1) * per]
        if q < 3:
            state = mine[q] + time_step * (mine[6] * moved)
        else:
            state = mine[q] + time_step * mine[4 + q] * moved
        if q == 2:
            state = state + time_step * gravity_z
        g3_ref[b, q * per : (q + 1) * per] = state

    copies = [
        remote(
            g3_ref.at[b], g3_ref.at[b], send3.at[parts + g], recv3.at[parts + b], (t, g)
        )
        for g in others3
    ]
    for item in copies:
        item.start()
    for g in others3:
        remote(
            g3_ref.at[g], g3_ref.at[g], send3.at[parts + g], recv3.at[parts + g], partner
        ).wait_recv()
    for item in copies:
        item.wait_send()

    copies = [
        remote(
            g3_ref, g2_ref.at[chip], send2.at[chips + g], recv2.at[chips + chip], (g * 2 + core, b)
        )
        for g in others2
    ]
    for item in copies:
        item.start()
    g2_ref[chip] = g3_ref[...]
    for g in others2:
        remote(
            g3_ref, g2_ref.at[g], send2.at[chips + g], recv2.at[chips + g], partner
        ).wait_recv()
    for item in copies:
        item.wait_send()

    last = remote(g2_ref, g1_ref.at[core], send1.at[1], recv1.at[1 + core], partner)
    last.start()
    g1_ref[core] = g2_ref[...]
    remote(g2_ref, g1_ref.at[1 - core], send1.at[1], recv1.at[2 - core], partner).wait_recv()
    last.wait_send()


def exchange(partials, params, per):
    tiles, parts = lax.axis_size("tile"), lax.axis_size("body")
    chips = tiles // 2
    chunk = partials.shape[3:]
    dma = pltpu.SemaphoreType.DMA
    return pl.pallas_call(
        functools.partial(exchange_kernel, per),
        out_shape=shape((2, chips, parts) + chunk),
        in_specs=[pl.BlockSpec(memory_space=VMEM)] * 2,
        out_specs=pl.BlockSpec(memory_space=VMEM),
        scratch_shapes=[
            VMEM((chips, parts) + chunk, F32),
            VMEM((chips, parts) + chunk, F32),
            VMEM((chips, parts) + chunk, F32),
            VMEM((parts,) + chunk, F32),
            VMEM((parts,) + chunk, F32),
            VMEM((parts,) + chunk, F32),
            VMEM((chips, parts) + chunk, F32),
            dma((2,)),
            dma((3,)),
            dma((2 * chips,)),
            dma((2 * chips,)),
            dma((2 * parts,)),
            dma((2 * parts,)),
        ],
        compiler_params=pltpu.CompilerParams(
            collective_id=9, has_side_effects=True, vmem_limit_bytes=32 * 2**20
        ),
        name="exchange",
    )(partials, params)


def two_level(body, owned, shard):
    index = body
    for part in range(1, lax.axis_size("body")):
        index = index + jnp.where(body >= part * owned, shard * LOW - owned, 0)
    return index >> (LOW.bit_length() - 1), index & (LOW - 1)


def call(kernel, shapes, ins, scratch, spaces, name, outs=None, limit=60):
    outs = outs or jax.tree.map(lambda _: VMEM, shapes)
    return pl.pallas_call(
        kernel,
        out_shape=shapes,
        in_specs=[pl.BlockSpec(memory_space=s) for s in spaces],
        out_specs=jax.tree.map(lambda s: pl.BlockSpec(memory_space=s), outs),
        scratch_shapes=scratch,
        compiler_params=pltpu.CompilerParams(vmem_limit_bytes=limit * 2**20),
        name=name,
    )(*ins)


def shape(dims, kind=F32):
    return jax.ShapeDtypeStruct(tuple(dims), kind)


def shards(
    fluid_position,
    fluid_pressure,
    source,
    stiffness,
    neighbours,
    wall_position,
    wall_normal,
    wall_arm,
    wall_live,
    wall_body,
    linear_velocity,
    angular_velocity,
    inverse_mass,
    inverse_inertia,
):
    rows, cols, _ = fluid_pressure.shape
    near = jnp.transpose(neighbours, (2, 1, 0))
    pressure, wall_pressure, error = fluid(
        near, fluid_position, fluid_pressure, source, stiffness, wall_position, wall_live
    )
    particle_total = rows * cols * 128 * lax.axis_size("tile") * lax.axis_size("body")
    owned = inverse_mass.shape[0]
    tiles = lax.axis_size("tile")
    parts = lax.axis_size("body")
    spare = -(-owned // LOW)
    per = spare // tiles + 1
    shard = per * tiles
    chunk = (-(-6 * per // 8) * 8, LOW)
    spans = shape((rows,), jnp.int32)
    partials, first, last = call(
        functools.partial(scatter_kernel, per, owned, spare),
        (shape((2, tiles // 2, parts) + chunk), spans, spans),
        (wall_pressure, wall_normal, wall_arm, wall_body, error),
        [
            VMEM((WINDOW * 16 * cols, 128), F32),
            VMEM((LOW, cols * 128), BF16),
            VMEM((parts * shard + WINDOW, 8, LOW), F32),
        ],
        [VMEM] * 5,
        "scatter",
        (VMEM, SMEM, SMEM),
        16,
    )
    params = jnp.concatenate(
        [linear_velocity, angular_velocity, inverse_mass[None], inverse_inertia], 0
    )
    fill = jnp.zeros((10, shard * LOW - owned), F32).at[6].set(1.0 / time_step)
    params = jnp.concatenate([params, fill], 1).reshape(10, tiles, per, LOW)
    table = exchange(partials, params, per)
    wall_velocity, own_state, error = call(
        functools.partial(gather_kernel, per, owned),
        (shape((3, rows, cols, 128)), shape((6, owned)), shape((1, LOW))),
        (first, last, table, wall_arm, wall_body),
        [],
        [SMEM] * 2 + [VMEM] * 3,
        "gather",
        None,
        16,
    )
    density_error = error[0, 0] / particle_total
    return (pressure, wall_pressure, own_state, wall_velocity, density_error)


def solution(mesh):
    placed = (
        P(None, "tile", "body", None),
        P("tile", "body", None),
        P("tile", "body", None),
        P("tile", "body", None),
        P("tile", "body", None),
        P(None, "tile", "body", None),
        P(None, "tile", "body", None),
        P(None, "tile", "body", None),
        P("tile", "body", None),
        P("tile", "body", None),
        P(None, "body"),
        P(None, "body"),
        P("body"),
        P(None, "body"),
    )
    return jax.shard_map(
        shards,
        mesh=mesh,
        in_specs=placed,
        out_specs=(
            P("tile", "body", None),
            P("tile", "body", None),
            P(None, "body"),
            P(None, "tile", "body", None),
            P(),
        ),
        check_vma=False,
    )
```

```python
import math
import functools
import jax
import jax.numpy as jnp
from jax import lax
from jax.experimental import pallas as pl
from jax.experimental.pallas import tpu as pltpu
from jax.sharding import PartitionSpec as P

SWEEPS = 2

relax_factor = 0.5
inv_width = 2.0
kernel_scale = 0.0078125
wall_offset = 0.5
time_step = 0.25
gravity_z = -9.81

UNIT = math.sqrt(inv_width / math.log(2.0))
DEPTH = 32
LOW = 128
WINDOW = 6
TABLE = 7
GROUP = 4
F32, BF16 = jnp.float32, jnp.bfloat16
VMEM = pltpu.VMEM
SMEM = pltpu.SMEM


def pieces(x, count):
    out = []
    for _ in range(count):
        piece = x.astype(BF16).astype(F32)
        out.append(piece)
        x = x - piece
    return out


def near_rows(x):
    h, m, l = pieces(x, 3)
    return [h, m, h, l, h] + pieces(-(x * x), 3)


def own_rows(x):
    h, m, l = pieces(2.0 * x, 3)
    one = jnp.ones_like(x)
    return [h, h, m, h, l, one, one, one]


def centre(first, size, axis):
    at = first + lax.broadcasted_iota(jnp.int32, (size, 128), 0) if axis else first
    return at.astype(F32) + 0.5


def build_near(tab_ref, start, stride, x, y, z):
    count = x.shape[0]
    groups = [near_rows(x + (v - 1) * UNIT) for v in range(3)]
    groups += [near_rows(y + (v - 1) * UNIT) for v in range(3)]
    groups += [near_rows(z)]
    for g, group in enumerate(groups):
        for k, value in enumerate(group):
            if count == 1:
                tab_ref[start + g, k : k + 1] = value
            else:
                tab_ref[pl.ds(start + g, count, stride=stride * TABLE), k, :] = value


def build_own(pos_ref, lhs_ref, stage_ref, bx, by):
    rows, cols = pos_ref.shape[1], pos_ref.shape[2]
    stage_ref[...] = jnp.zeros_like(stage_ref)

    def group(i, carry):
        for e in range(GROUP):
            r = i * GROUP + e
            x = (pos_ref[0, r] - centre(bx + r, cols, 0)) * UNIT
            y = (pos_ref[1, r] - centre(by, cols, 1)) * UNIT
            z = (pos_ref[2, r] - 0.5) * UNIT
            norm = pieces(-(x * x + y * y + z * z), 3)
            for k, value in enumerate(own_rows(x) + own_rows(y) + own_rows(z) + norm):
                stage_ref[e, k * cols : (k + 1) * cols] = value
        for e in range(GROUP):
            for c in range(cols):
                start = pl.multiple_of(((i * GROUP + e) * cols + c) * 128, 128)
                turned = stage_ref[e, pl.ds(c, DEPTH, stride=cols), :].T
                lhs_ref[pl.ds(start, 128), 0:DEPTH] = turned.astype(BF16)
        return carry

    lax.fori_loop(0, rows // GROUP, group, 0)


def pair_block(r, c, near_ref, tab_ref, val_ref, lhs_ref, keep_ref, cols):
    ones = (lax.broadcasted_iota(jnp.int32, (8, 128), 0) < 3).astype(F32)
    listed = near_ref.shape[0]
    sides, values = [], []
    for k in range(listed):
        code = near_ref[k, c, r]
        up = (code * 11) >> 5
        side = code - up * 3
        base = ((r + up) * (cols + 2) + c + side) * TABLE
        rows = [tab_ref[at] for at in (base + up, base + 3 + side, base + 6)]
        sides.append(jnp.concatenate(rows + [ones], axis=0).astype(BF16))
        values.append(val_ref[pl.ds((r + up) * 16 + c + side, 1), :])
    block = r * cols + c
    lhs = lhs_ref[pl.ds(pl.multiple_of(block * 128, 128), 128), 0:DEPTH]
    ws = wv = None
    for k in range(0, listed, 2):
        exponent = jnp.dot(
            lhs, jnp.concatenate(sides[k : k + 2], axis=1), preferred_element_type=F32
        )
        weight = jnp.exp2(exponent)
        for e in range(2):
            part = weight[:, e * 128 : (e + 1) * 128]
            if keep_ref is not None:
                at = pl.multiple_of((block * listed + k + e) * 128, 128)
                keep_ref[pl.ds(at, 128), :] = part
            product = part * values[k + e]
            ws = part if ws is None else ws + part
            wv = product if wv is None else wv + product
    return [jnp.sum(total.T, axis=0, keepdims=True) * kernel_scale for total in (ws, wv)]


def kept_block(r, c, near_ref, val_ref, keep_ref, cols):
    listed = near_ref.shape[0]
    block = r * cols + c
    wv = None
    for k in range(listed):
        code = near_ref[k, c, r]
        up = (code * 11) >> 5
        value = val_ref[pl.ds((r + up) * 16 + c + code - up * 3, 1), :]
        at = pl.multiple_of((block * listed + k) * 128, 128)
        product = keep_ref[pl.ds(at, 128), :] * value
        wv = product if wv is None else wv + product
    return jnp.sum(wv.T, axis=0, keepdims=True) * kernel_scale


WAYS = ((-1, 0), (1, 0), (0, -1), (0, 1), (-1, -1), (-1, 1), (1, -1), (1, 1))


def fluid_kernel(
    near_ref,
    pos_ref,
    p_ref,
    source_ref,
    stiff_ref,
    wall_ref,
    live_ref,
    p_out,
    wp_out,
    error_out,
    tab_ref,
    val_ref,
    lhs_ref,
    keep_ref,
    stage_ref,
    ws_ref,
    wv_ref,
    mid_ref,
    row_send,
    row_in,
    col_send,
    col_in,
    corner_send,
    corner_in,
    row_in2,
    col_send2,
    col_in2,
    corner_send2,
    corner_in2,
    send,
    recv,
):
    rows, cols = p_ref.shape[0], p_ref.shape[1]
    tiles, parts = lax.axis_size("tile"), lax.axis_size("body")
    t, b = lax.axis_index("tile"), lax.axis_index("body")
    bx, by = t * rows, b * cols

    def exists(dt, db):
        ok = jnp.bool_(True)
        if dt:
            ok = (t > 0) if dt < 0 else (t < tiles - 1)
        if db:
            side = (b > 0) if db < 0 else (b < parts - 1)
            ok = jnp.logical_and(ok, side) if dt else side
        return ok

    barrier = pltpu.get_barrier_semaphore()
    for dt, db in WAYS:

        @pl.when(exists(dt, db))
        def _():
            pl.semaphore_signal(
                barrier, inc=1, device_id=(t + dt, b + db), device_id_type=pl.DeviceIdType.MESH
            )

    def copy(phase, n):
        dt, db = WAYS[n]
        if n < 2:
            src = row_send.at[n] if phase == 0 else (mid_ref, p_out)[phase - 1].at[n * (rows - 1)]
            dst = row_in.at[n] if phase == 0 else row_in2.at[phase - 1, n]
        elif n < 4:
            src = col_send.at[n - 2] if phase == 0 else col_send2.at[phase - 1, n - 2]
            dst = col_in.at[n - 2] if phase == 0 else col_in2.at[phase - 1, n - 2]
        else:
            src = corner_send.at[n - 4] if phase == 0 else corner_send2.at[phase - 1, n - 4]
            dst = corner_in.at[n - 4] if phase == 0 else corner_in2.at[phase - 1, n - 4]
        return remote(src, dst, send.at[phase, n], recv.at[phase, n], (t + dt, b + db))

    def launch(phase):
        for n, (dt, db) in enumerate(WAYS):

            @pl.when(exists(dt, db))
            def _():
                copy(phase, n).start()

    def arrive(phase):
        for n, (dt, db) in enumerate(WAYS):

            @pl.when(exists(-dt, -db))
            def _():
                copy(phase, n).wait_recv()

    def depart(phase):
        for n, (dt, db) in enumerate(WAYS):

            @pl.when(exists(dt, db))
            def _():
                copy(phase, n).wait_send()

    def pack(phase, ref):
        for side in range(2):
            for r in range(rows):
                line = ref[r, side * (cols - 1) : side * (cols - 1) + 1]
                col_send2[phase - 1, side, r : r + 1] = line
        for n, (dt, db) in enumerate(WAYS[4:]):
            r, c = (dt > 0) * (rows - 1), (db > 0) * (cols - 1)
            corner_send2[phase - 1, n, 0:1] = ref[r, c : c + 1]

    fields = [(pos_ref, d) for d in range(3)] + [(p_ref, None)]
    for d, (ref, at) in enumerate(fields):
        view = ref if at is None else ref.at[at]
        for side in range(2):
            row_send[side, d] = view[side * (rows - 1)]
            for r in range(rows):
                line = view[r, side * (cols - 1) : side * (cols - 1) + 1]
                col_send[side, d, r : r + 1] = line
        for n, (dt, db) in enumerate(WAYS[4:]):
            r, c = (dt > 0) * (rows - 1), (db > 0) * (cols - 1)
            corner_send[n, d : d + 1] = view[r, c : c + 1]

    along = 1 + (t > 0).astype(jnp.int32) + (t < tiles - 1).astype(jnp.int32)
    across = 1 + (b > 0).astype(jnp.int32) + (b < parts - 1).astype(jnp.int32)
    pl.semaphore_wait(barrier, along * across - 1)
    launch(0)

    build_own(pos_ref, lhs_ref, stage_ref, bx, by)

    def near_row(r, carry):
        x = (pos_ref[0, r] - centre(bx + r, cols, 0)) * UNIT
        y = (pos_ref[1, r] - centre(by, cols, 1)) * UNIT
        z = (pos_ref[2, r] - 0.5) * UNIT
        build_near(tab_ref, ((r + 1) * (cols + 2) + 1) * TABLE, 1, x, y, z)
        return carry

    lax.fori_loop(0, rows, near_row, 0)

    def fill(ref):
        for r in range(rows):
            val_ref[(r + 1) * 16 + 1 : (r + 1) * 16 + 1 + cols] = ref[r]

    def slots(n):
        dt, db = WAYS[n]
        return (0 if dt > 0 else rows + 1), (0 if db > 0 else cols + 1)

    def halo_values(phase):
        for n, (dt, db) in enumerate(WAYS):
            ok = exists(-dt, -db)
            r, c = slots(n)
            if n < 2:
                got = row_in[n, 3] if phase == 0 else row_in2[phase - 1, n]
                val_ref[r * 16 + 1 : r * 16 + 1 + cols] = jnp.where(ok, got, 0.0)
            elif n < 4:
                got = col_in[n - 2, 3] if phase == 0 else col_in2[phase - 1, n - 2]
                val_ref[pl.ds(16 + c, rows, stride=16), :] = jnp.where(ok, got, 0.0)
            else:
                got = (
                    corner_in[n - 4, 3:4]
                    if phase == 0
                    else corner_in2[phase - 1, n - 4, 0:1]
                )
                val_ref[r * 16 + c : r * 16 + c + 1] = jnp.where(ok, got, 0.0)

    def halo_tables():
        for n, (dt, db) in enumerate(WAYS):
            ok = exists(-dt, -db)
            r, c = slots(n)
            across_r = bx - 1 if dt > 0 else bx + rows
            across_c = by - 1 if db > 0 else by + cols
            if n < 2:
                x, y, z = [jnp.where(ok, row_in[n, d], 0.0) for d in range(3)]
                x = x - centre(across_r, cols, 0)
                y = y - centre(by, cols, 1)
                start, stride = (r * (cols + 2) + 1) * TABLE, 1
            elif n < 4:
                x, y, z = [jnp.where(ok, col_in[n - 2, d], 0.0) for d in range(3)]
                x = x - centre(bx, rows, 1)
                y = y - centre(across_c, rows, 0)
                start, stride = (cols + 2 + c) * TABLE, cols + 2
            else:
                x, y, z = [jnp.where(ok, corner_in[n - 4, d : d + 1], 0.0) for d in range(3)]
                x = x - centre(across_r, 1, 0)
                y = y - centre(across_c, 1, 0)
                start, stride = (r * (cols + 2) + c) * TABLE, 1
            build_near(tab_ref, start, stride, x * UNIT, y * UNIT, (z - 0.5) * UNIT)

    def sweep(first, meet):
        def block(r, c):
            if first is None:
                wv = kept_block(r, c, near_ref, val_ref, keep_ref, cols)
            else:
                ws, wv = pair_block(
                    r, c, near_ref, tab_ref, val_ref, lhs_ref, keep_ref if first else None, cols
                )
                ws_ref[r, pl.ds(c, 1), :] = ws
            wv_ref[r, pl.ds(c, 1), :] = wv

        def column(c, carry):
            for r in range(1, rows - 1):
                block(r, c)
            return carry

        lax.fori_loop(1, cols - 1, column, 0)
        meet()
        lax.fori_loop(0, 2, lambda i, carry: column(i * (cols - 1), carry), 0)

        def end(i, carry):
            for c in range(cols):
                block(i * (rows - 1), c)
            return carry

        lax.fori_loop(0, 2, end, 0)

    fill(p_ref)

    def meet(phase):
        arrive(phase)
        if phase == 0:
            halo_tables()
        halo_values(phase)

    def relax(before_ref, after_ref):
        pressure = before_ref[...]
        diagonal = stiff_ref[...] + ws_ref[...]
        residual = source_ref[...] - (diagonal * pressure - wv_ref[...])
        after_ref[...] = jnp.maximum(pressure + relax_factor * residual / diagonal, 0.0)
        return residual

    sweep(True, lambda: meet(0))
    relax(p_ref, mid_ref)
    pack(1, mid_ref)
    launch(1)
    fill(mid_ref)
    build_own(wall_ref, lhs_ref, stage_ref, bx, by)
    sweep(None, lambda: meet(1))
    residual = relax(mid_ref, p_out)
    pack(2, p_out)
    launch(2)
    error_out[...] = jnp.sum(residual * residual, axis=0)
    fill(p_out)
    sweep(False, lambda: meet(2))
    wp_out[...] = wv_ref[...] / (wall_offset + ws_ref[...]) * live_ref[...].astype(F32)
    for phase in range(3):
        depart(phase)


def fluid(near, pos, p, source, stiff, wall, live):
    rows, cols, _ = p.shape
    small = shape((rows, cols, 128))
    return pl.pallas_call(
        fluid_kernel,
        out_shape=(small, small, shape((cols, 128))),
        in_specs=[pl.BlockSpec(memory_space=SMEM)] + [pl.BlockSpec(memory_space=VMEM)] * 6,
        out_specs=(pl.BlockSpec(memory_space=VMEM),) * 3,
        scratch_shapes=[
            VMEM(((rows + 2) * (cols + 2) * TABLE, 8, 128), F32),
            VMEM(((rows + 2) * 16, 128), F32),
            VMEM((rows * cols * 128, 128), BF16),
            VMEM((rows * cols * near.shape[0] * 128, 128), F32),
            VMEM((GROUP, DEPTH * cols, 128), F32),
            VMEM((rows, cols, 128), F32),
            VMEM((rows, cols, 128), F32),
            VMEM((rows, cols, 128), F32),
            VMEM((2, 4, cols, 128), F32),
            VMEM((2, 4, cols, 128), F32),
            VMEM((2, 4, rows, 128), F32),
            VMEM((2, 4, rows, 128), F32),
            VMEM((4, 8, 128), F32),
            VMEM((4, 8, 128), F32),
            VMEM((2, 2, cols, 128), F32),
            VMEM((2, 2, rows, 128), F32),
            VMEM((2, 2, rows, 128), F32),
            VMEM((2, 4, 8, 128), F32),
            VMEM((2, 4, 8, 128), F32),
            pltpu.SemaphoreType.DMA((3, 8)),
            pltpu.SemaphoreType.DMA((3, 8)),
        ],
        compiler_params=pltpu.CompilerParams(
            collective_id=1, has_side_effects=True, vmem_limit_bytes=62 * 2**20
        ),
        name="fluid",
    )(near, pos, p, source, stiff, wall, live)


def split(x, n):
    if n & (n - 1):
        return lax.div(x, n), lax.rem(x, n)
    return x >> (n.bit_length() - 1), x & (n - 1)


def scatter_kernel(
    shard,
    owned,
    spare,
    p_ref,
    wp_ref,
    normal_ref,
    arm_ref,
    body_ref,
    error_ref,
    p_out,
    wp_out,
    acc_ref,
    first_ref,
    last_ref,
    stage_ref,
    hot_ref,
):
    rows, cols = wp_ref.shape[0], wp_ref.shape[1]
    for r in range(rows):
        top, _ = two_level(body_ref[r], owned, shard)
        first_ref[r] = jnp.min(top)
        last_ref[r] = jnp.max(top)
    p_out[...] = p_ref[...]
    wp_out[...] = wp_ref[...]
    acc_ref[...] = jnp.zeros_like(acc_ref)
    stage_ref[...] = jnp.zeros_like(stage_ref)
    low_iota = lax.broadcasted_iota(jnp.int32, (LOW, 128), 0).astype(F32).astype(BF16)
    one, zero = jnp.ones((LOW, 128), BF16), jnp.zeros((LOW, 128), BF16)
    lines = WINDOW * 16

    def window(r, e, start):
        wp = wp_ref[r]
        fx, fy, fz = [wp * normal_ref[d, r] for d in range(3)]
        ax, ay, az = [arm_ref[d, r] for d in range(3)]
        values = [fx, fy, fz, ay * fz - az * fy, az * fx - ax * fz, ax * fy - ay * fx]
        top, _ = two_level(body_ref[r], owned, shard)
        here = [top == start + w for w in range(WINDOW)]
        for q, value in enumerate(values):
            for s, piece in enumerate(pieces(value, 2)):
                for w in range(WINDOW):
                    at = (w * 16 + s * 8 + q) * cols
                    stage_ref[e, at : at + cols] = jnp.where(here[w], piece, 0.0)
        total = jnp.zeros((lines, LOW), F32)
        for c in range(0, cols, 2):
            lhs = jnp.concatenate(
                [stage_ref[e, pl.ds(c + k, lines, stride=cols), :] for k in range(2)], axis=1
            )
            total = total + lax.dot_general(
                lhs.astype(BF16),
                hot_ref[e, :, c * 128 : (c + 2) * 128],
                (((1,), (1,)), ((), ())),
                preferred_element_type=F32,
            )
        return [total[w * 16 : w * 16 + 8] + total[w * 16 + 8 : w * 16 + 16] for w in range(WINDOW)]

    def add(start, found):
        for w in range(WINDOW):
            acc_ref[start + w] += found[w]

    def group(i, carry):
        found = []
        for e in range(GROUP):
            r = i * GROUP + e
            _, low = two_level(body_ref[r], owned, shard)
            low = low.astype(F32)
            for c in range(cols):
                line = jnp.broadcast_to(low[c : c + 1], (LOW, 128)).astype(BF16)
                hot_ref[e, :, c * 128 : (c + 1) * 128] = jnp.where(low_iota == line, one, zero)
            found.append(window(r, e, first_ref[r]))
        for e in range(GROUP):
            add(first_ref[i * GROUP + e], found[e])
        for e in range(GROUP):
            r = i * GROUP + e

            def more(j, carry):
                start = first_ref[r] + j * WINDOW
                add(start, window(r, e, start))
                return carry

            lax.fori_loop(1, split(last_ref[r] - first_ref[r], WINDOW)[0] + 1, more, 0)
        return carry

    lax.fori_loop(0, rows // GROUP, group, 0)
    lane = lax.broadcasted_iota(jnp.int32, (8, LOW), 1)
    acc_ref[spare] = jnp.where(lane == 0, jnp.sum(error_ref[...]), 0.0)


def gather_kernel(
    per,
    lines,
    owned,
    first_ref,
    last_ref,
    table_ref,
    arm_ref,
    body_ref,
    out_ref,
    own_ref,
    error_ref,
):
    rows, cols = body_ref.shape[0], body_ref.shape[1]
    tiles, parts = lax.axis_size("tile"), lax.axis_size("body")
    chips, shard = tiles // 2, per * tiles
    spare = -(-owned // LOW)
    b = lax.axis_index("body")

    def place(top):
        p, rest = split(top, shard)
        t, n = split(rest, per)
        return (((t & 1) * parts + p) * chips + (t >> 1)) * lines + n

    def window(top, low, start, last, got):
        got = list(got)
        for w in range(WINDOW):
            here = top == start + w
            at = place(jnp.minimum(start + w, last))
            for q in range(6):
                line = jnp.broadcast_to(table_ref[pl.ds(at + q * per, 1), :], (cols, LOW))
                found = jnp.take_along_axis(line, low, axis=1, mode="promise_in_bounds")
                got[q] = jnp.where(here, found, got[q])
        return tuple(got)

    def group(i, carry):
        both, ends, states = [], [], []
        zero = jnp.zeros((cols, LOW), F32)
        for e in range(GROUP):
            r = i * GROUP + e
            both.append(two_level(body_ref[r], owned, shard))
            ends.append((first_ref[r], last_ref[r]))
            states.append(window(*both[e], ends[e][0], ends[e][1], (zero,) * 6))
        for e in range(GROUP):
            r = i * GROUP + e
            first, last = ends[e]

            def more(j, got):
                return window(*both[e], first + j * WINDOW, last, got)

            count = split(last - first, WINDOW)[0] + 1
            vx, vy, vz, wx, wy, wz = lax.fori_loop(1, count, more, states[e])
            ax, ay, az = [arm_ref[d, r] for d in range(3)]
            out_ref[0, r] = vx + (wy * az - wz * ay)
            out_ref[1, r] = vy + (wz * ax - wx * az)
            out_ref[2, r] = vz + (wx * ay - wy * ax)
        return carry

    lax.fori_loop(0, rows // GROUP, group, 0)
    for n in range(spare):
        wide = min(LOW, owned - n * LOW)
        t = n // per
        at = b * (chips * lines) + ((t % 2) * parts * chips + t // 2) * lines + n % per
        for q in range(6):
            line = table_ref[pl.ds(at + q * per, 1), :]
            own_ref[q : q + 1, n * LOW : n * LOW + wide] = line[:, :wide]
    t = spare // per
    at = ((t % 2) * parts * chips + t // 2) * lines + spare % per
    error_ref[...] = table_ref[at : at + 1]


def remote(src, dst, send, recv, device):
    return pltpu.make_async_remote_copy(
        src_ref=src,
        dst_ref=dst,
        send_sem=send,
        recv_sem=recv,
        device_id=device,
        device_id_type=pl.DeviceIdType.MESH,
    )


def exchange_kernel(
    per,
    acc_ref,
    linear_ref,
    angular_ref,
    mass_ref,
    inertia_ref,
    g1_ref,
    par_ref,
    partial_ref,
    r1_ref,
    s1_ref,
    r2_ref,
    s2_ref,
    r3_ref,
    send1,
    recv1,
    send2,
    recv2,
    send3,
    recv3,
    send4,
    recv4,
    send5,
    recv5,
    send6,
    recv6,
):
    parts, chips = r1_ref.shape[0], r1_ref.shape[1]
    spare = mass_ref.shape[0]
    shard = per * chips * 2
    t, b = lax.axis_index("tile"), lax.axis_index("body")
    core, chip = t % 2, t // 2
    barrier = pltpu.get_barrier_semaphore()
    partner = (chip * 2 + 1 - core, b)
    others2 = [(chip + k) % chips for k in range(1, chips)]
    upper = b >= parts // 2
    others3 = [(b + jnp.where(upper, i, parts - i)) % parts for i in range(1, parts)]
    order, nearest = others3 + [b], others3[::-1]
    greeted = [partner] + [(g * 2 + core, b) for g in others2] + [(t, g) for g in others3]
    for device in greeted:
        pl.semaphore_signal(barrier, inc=1, device_id=device, device_id_type=pl.DeviceIdType.MESH)

    lines = partial_ref.shape[3]
    for k in range(2):
        for p in range(parts):
            for g in range(chips):
                at = p * shard + (g * 2 + k) * per
                if lines > 6 * per:
                    partial_ref[k, p, g] = jnp.zeros((lines, LOW), F32)
                for q in range(6):
                    line = acc_ref[pl.ds(at * 8 + q, per, stride=8), :]
                    partial_ref[k, p, g, q * per : (q + 1) * per] = line
    for n in range(per):
        row = t * per + n
        held = row < spare
        row = jnp.minimum(row, spare - 1)
        at = pl.multiple_of(row * LOW, LOW)
        for d in range(3):
            own = slice(n, n + 1)
            par_ref[d, own] = jnp.where(held, linear_ref[d : d + 1, pl.ds(at, LOW)], 0.0)
            par_ref[3 + d, own] = jnp.where(held, angular_ref[d : d + 1, pl.ds(at, LOW)], 0.0)
            par_ref[7 + d, own] = jnp.where(held, inertia_ref[d : d + 1, pl.ds(at, LOW)], 0.0)
        par_ref[6, n : n + 1] = jnp.where(held, mass_ref[pl.ds(row, 1), :], 1.0 / time_step)
    pl.semaphore_wait(barrier, len(greeted))

    started = []

    def go(*args):
        item = remote(*args)
        item.start()
        started.append(item)

    for p in order:
        go(partial_ref.at[1 - core, p], r1_ref.at[p], send1.at[p], recv1.at[p], partner)
    for p in order:
        remote(
            partial_ref.at[1 - core, p], r1_ref.at[p], send1.at[p], recv1.at[p], partner
        ).wait_recv()
        s1_ref[p] = partial_ref[core, p] + r1_ref[p]
        for g in others2:
            go(
                s1_ref.at[p, g],
                r2_ref.at[p, chip],
                send2.at[p, g],
                recv2.at[p, chip],
                (g * 2 + core, b),
            )
    for i, p in enumerate(order):
        total = s1_ref[p, chip]
        for g in others2:
            remote(
                s1_ref.at[p, g], r2_ref.at[p, g], send2.at[p, g], recv2.at[p, g], partner
            ).wait_recv()
            total = total + r2_ref[p, g]
        s2_ref[p] = total
        if i < parts - 1:
            go(s2_ref.at[p], r3_ref.at[b], send3.at[p], recv3.at[b], (t, p))
    total = s2_ref[b]
    for g in nearest:
        remote(s2_ref.at[g], r3_ref.at[g], send3.at[g], recv3.at[g], partner).wait_recv()
        total = total + r3_ref[g]

    if lines > 6 * per:
        g1_ref[core, b, chip] = total
    for q in range(6):
        moved = total[q * per : (q + 1) * per]
        if q < 3:
            state = par_ref[q] + time_step * (par_ref[6] * moved)
        else:
            state = par_ref[q] + time_step * par_ref[4 + q] * moved
        if q == 2:
            state = state + time_step * gravity_z
        g1_ref[core, b, chip, q * per : (q + 1) * per] = state

    mine = g1_ref.at[core, b, chip]
    for p in others3:
        go(mine, mine, send4.at[p], recv4.at[b], (t, p))

    def spread(p):
        part = g1_ref.at[core, p, chip]
        for g in others2:
            go(part, part, send5.at[p, g], recv5.at[p, chip], (g * 2 + core, b))

    spread(b)
    for p in nearest:
        part = g1_ref.at[core, p, chip]
        remote(part, part, send4.at[p], recv4.at[p], partner).wait_recv()
        spread(p)
    for p in [b] + nearest:
        for g in others2:
            part = g1_ref.at[core, p, g]
            remote(part, part, send5.at[p, g], recv5.at[p, g], partner).wait_recv()
        go(g1_ref.at[core, p], g1_ref.at[core, p], send6.at[p], recv6.at[p], partner)
    for p in [b] + nearest:
        part = g1_ref.at[1 - core, p]
        remote(part, part, send6.at[p], recv6.at[p], partner).wait_recv()
    for item in started:
        item.wait_send()


def exchange(acc, params, per):
    tiles, parts = lax.axis_size("tile"), lax.axis_size("body")
    chips = tiles // 2
    chunk = (-(-6 * per // 8) * 8, LOW)
    wide = (parts, chips)
    dma = pltpu.SemaphoreType.DMA
    return pl.pallas_call(
        functools.partial(exchange_kernel, per),
        out_shape=shape((2,) + wide + chunk),
        in_specs=[pl.BlockSpec(memory_space=VMEM)] * 5,
        out_specs=pl.BlockSpec(memory_space=VMEM),
        scratch_shapes=[
            VMEM((10, per, LOW), F32),
            VMEM((2,) + wide + chunk, F32),
            VMEM(wide + chunk, F32),
            VMEM(wide + chunk, F32),
            VMEM(wide + chunk, F32),
            VMEM((parts,) + chunk, F32),
            VMEM((parts,) + chunk, F32),
        ]
        + [dma(dims) for dims in ((parts,), wide, (parts,), (parts,), wide, (parts,)) for _ in range(2)],
        compiler_params=pltpu.CompilerParams(
            collective_id=9, has_side_effects=True, vmem_limit_bytes=32 * 2**20
        ),
        name="exchange",
    )(acc, *params)


def two_level(body, owned, shard):
    index = body
    for part in range(1, lax.axis_size("body")):
        index = index + jnp.where(body >= part * owned, shard * LOW - owned, 0)
    return index >> (LOW.bit_length() - 1), index & (LOW - 1)


def call(kernel, shapes, ins, scratch, spaces, name, outs=None, limit=60):
    outs = outs or jax.tree.map(lambda _: VMEM, shapes)
    return pl.pallas_call(
        kernel,
        out_shape=shapes,
        in_specs=[pl.BlockSpec(memory_space=s) for s in spaces],
        out_specs=jax.tree.map(lambda s: pl.BlockSpec(memory_space=s), outs),
        scratch_shapes=scratch,
        compiler_params=pltpu.CompilerParams(vmem_limit_bytes=limit * 2**20),
        name=name,
    )(*ins)


def shape(dims, kind=F32):
    return jax.ShapeDtypeStruct(tuple(dims), kind)


def shards(
    fluid_position,
    fluid_pressure,
    source,
    stiffness,
    neighbours,
    wall_position,
    wall_normal,
    wall_arm,
    wall_live,
    wall_body,
    linear_velocity,
    angular_velocity,
    inverse_mass,
    inverse_inertia,
):
    rows, cols, _ = fluid_pressure.shape
    small = shape((rows, cols, 128))
    near = jnp.transpose(neighbours, (2, 1, 0))
    pressure, wall_pressure, error = fluid(
        near, fluid_position, fluid_pressure, source, stiffness, wall_position, wall_live
    )
    particle_total = rows * cols * 128 * lax.axis_size("tile") * lax.axis_size("body")
    owned = inverse_mass.shape[0]
    tiles = lax.axis_size("tile")
    parts = lax.axis_size("body")
    spare = -(-owned // LOW)
    per = spare // tiles + 1
    shard = per * tiles
    spans = shape((rows,), jnp.int32)
    pressure, wall_pressure, acc, first, last = call(
        functools.partial(scatter_kernel, shard, owned, spare),
        (small, small, shape((parts * shard + WINDOW, 8, LOW)), spans, spans),
        (pressure, wall_pressure, wall_normal, wall_arm, wall_body, error),
        [
            VMEM((GROUP, WINDOW * 16 * cols, 128), F32),
            VMEM((GROUP, LOW, cols * 128), BF16),
        ],
        [VMEM] * 6,
        "scatter",
        (VMEM, VMEM, VMEM, SMEM, SMEM),
        16,
    )
    mass = jnp.pad(inverse_mass, (0, spare * LOW - owned)).reshape(spare, LOW)
    acc = acc.reshape(-1, LOW)
    table = exchange(acc, (linear_velocity, angular_velocity, mass, inverse_inertia), per)
    lines = table.shape[3]
    wall_velocity, own_state, error = call(
        functools.partial(gather_kernel, per, lines, owned),
        (shape((3, rows, cols, 128)), shape((6, owned)), shape((1, LOW))),
        (first, last, table.reshape(-1, LOW), wall_arm, wall_body),
        [],
        [SMEM] * 2 + [VMEM] * 3,
        "gather",
        None,
        16,
    )
    density_error = error[0, 0] / particle_total
    return (pressure, wall_pressure, own_state, wall_velocity, density_error)


def solution(mesh):
    placed = (
        P(None, "tile", "body", None),
        P("tile", "body", None),
        P("tile", "body", None),
        P("tile", "body", None),
        P("tile", "body", None),
        P(None, "tile", "body", None),
        P(None, "tile", "body", None),
        P(None, "tile", "body", None),
        P("tile", "body", None),
        P("tile", "body", None),
        P(None, "body"),
        P(None, "body"),
        P("body"),
        P(None, "body"),
    )
    return jax.shard_map(
        shards,
        mesh=mesh,
        in_specs=placed,
        out_specs=(
            P("tile", "body", None),
            P("tile", "body", None),
            P(None, "body"),
            P(None, "tile", "body", None),
            P(),
        ),
        check_vma=False,
    )
```

```python
import math
import functools
import jax
import jax.numpy as jnp
from jax import lax
from jax.experimental import pallas as pl
from jax.experimental.pallas import tpu as pltpu
from jax.sharding import PartitionSpec as P

SWEEPS = 2

relax_factor = 0.5
inv_width = 2.0
kernel_scale = 0.0078125
wall_offset = 0.5
time_step = 0.25
gravity_z = -9.81

UNIT = math.sqrt(inv_width / math.log(2.0))
DEPTH = 32
LOW = 128
WINDOW = 6
TABLE = 7
GROUP = 4
OWN_GROUP = 8
F32, BF16 = jnp.float32, jnp.bfloat16
VMEM = pltpu.VMEM
SMEM = pltpu.SMEM


def pieces(x, count):
    out = []
    for _ in range(count):
        piece = x.astype(BF16).astype(F32)
        out.append(piece)
        x = x - piece
    return out


def near_rows(x):
    h, m, l = pieces(x, 3)
    return [h, m, h, l, h] + pieces(-(x * x), 3)


def own_rows(x):
    h, m, l = pieces(2.0 * x, 3)
    one = jnp.ones_like(x)
    return [h, h, m, h, l, one, one, one]


def centre(first, size, axis):
    at = first + lax.broadcasted_iota(jnp.int32, (size, 128), 0) if axis else first
    return at.astype(F32) + 0.5


def build_near(tab_ref, start, stride, x, y, z):
    count = x.shape[0]
    groups = [near_rows(x + (v - 1) * UNIT) for v in range(3)]
    groups += [near_rows(y + (v - 1) * UNIT) for v in range(3)]
    groups += [near_rows(z)]
    for g, group in enumerate(groups):
        for k, value in enumerate(group):
            at = (start + g) * 8 + k
            if count == 1:
                tab_ref[pl.ds(at, 1), :] = value
            else:
                tab_ref[pl.ds(at, count, stride=stride * TABLE * 8), :] = value


def build_own(pos_ref, lhs_ref, stage_ref, bx, by):
    rows, cols = pos_ref.shape[1], pos_ref.shape[2]
    stage_ref[...] = jnp.zeros_like(stage_ref)

    def group(i, carry):
        for e in range(OWN_GROUP):
            r = i * OWN_GROUP + e
            x = (pos_ref[0, r] - centre(bx + r, cols, 0)) * UNIT
            y = (pos_ref[1, r] - centre(by, cols, 1)) * UNIT
            z = (pos_ref[2, r] - 0.5) * UNIT
            norm = pieces(-(x * x + y * y + z * z), 3)
            for k, value in enumerate(own_rows(x) + own_rows(y) + own_rows(z) + norm):
                stage_ref[e, k * cols : (k + 1) * cols] = value
        for e in range(OWN_GROUP):
            for c in range(cols):
                start = pl.multiple_of(((i * OWN_GROUP + e) * cols + c) * 128, 128)
                turned = stage_ref[e, pl.ds(c, DEPTH, stride=cols), :].astype(BF16).T
                lhs_ref[pl.ds(start, 128), 0:DEPTH] = turned
        return carry

    lax.fori_loop(0, rows // OWN_GROUP, group, 0)


def listed_near(r, c, k, near_ref):
    code = near_ref[k, c, r]
    up = (code * 11) >> 5
    return up, code - up * 3


def pair_exponents(r, c, near_ref, tab_ref, lhs_ref, cols):
    ones = (lax.broadcasted_iota(jnp.int32, (8, 128), 0) < 3).astype(F32)
    listed = near_ref.shape[0]
    sides = []
    for k in range(listed):
        up, side = listed_near(r, c, k, near_ref)
        base = ((r + up) * (cols + 2) + c + side) * TABLE
        rows = [tab_ref[pl.ds(at * 8, 8), :] for at in (base + up, base + 3 + side, base + 6)]
        sides.append(jnp.concatenate(rows + [ones], axis=0).astype(BF16))
    lhs = lhs_ref[pl.ds(pl.multiple_of((r * cols + c) * 128, 128), 128), 0:DEPTH]
    return [
        jnp.dot(lhs, jnp.concatenate(sides[k : k + 2], axis=1), preferred_element_type=F32)
        for k in range(0, listed, 2)
    ]


def pair_sums(r, c, exponents, near_ref, val_ref, keep_ref, cols):
    block = r * cols + c
    listed = near_ref.shape[0]
    ws = wv = None
    for k in range(listed):
        up, side = listed_near(r, c, k, near_ref)
        value = val_ref[pl.ds((r + up) * 16 + c + side, 1), :]
        part = jnp.exp2(exponents[k // 2][:, k % 2 * 128 : k % 2 * 128 + 128])
        if keep_ref is not None:
            at = pl.multiple_of((block * listed + k) * 128, 128)
            keep_ref[pl.ds(at, 128), :] = part
        product = part * value
        ws = part if ws is None else ws + part
        wv = product if wv is None else wv + product
    return [jnp.sum(total.T, axis=0, keepdims=True) * kernel_scale for total in (ws, wv)]


def kept_block(r, c, near_ref, val_ref, keep_ref, cols):
    listed = near_ref.shape[0]
    block = r * cols + c
    wv = None
    for k in range(listed):
        code = near_ref[k, c, r]
        up = (code * 11) >> 5
        value = val_ref[pl.ds((r + up) * 16 + c + code - up * 3, 1), :]
        at = pl.multiple_of((block * listed + k) * 128, 128)
        product = keep_ref[pl.ds(at, 128), :] * value
        wv = product if wv is None else wv + product
    return jnp.sum(wv.T, axis=0, keepdims=True) * kernel_scale


WAYS = ((-1, 0), (1, 0), (0, -1), (0, 1), (-1, -1), (-1, 1), (1, -1), (1, 1))


def fluid_kernel(
    near_ref,
    pos_ref,
    p_ref,
    source_ref,
    stiff_ref,
    wall_ref,
    live_ref,
    p_out,
    wp_out,
    error_out,
    tab_ref,
    val_ref,
    lhs_ref,
    keep_ref,
    stage_ref,
    ws_ref,
    wv_ref,
    mid_ref,
    row_send,
    row_in,
    col_send,
    col_in,
    corner_send,
    corner_in,
    row_in2,
    col_send2,
    col_in2,
    corner_send2,
    corner_in2,
    send,
    recv,
):
    rows, cols = p_ref.shape[0], p_ref.shape[1]
    tiles, parts = lax.axis_size("tile"), lax.axis_size("body")
    t, b = lax.axis_index("tile"), lax.axis_index("body")
    bx, by = t * rows, b * cols

    def exists(dt, db):
        ok = jnp.bool_(True)
        if dt:
            ok = (t > 0) if dt < 0 else (t < tiles - 1)
        if db:
            side = (b > 0) if db < 0 else (b < parts - 1)
            ok = jnp.logical_and(ok, side) if dt else side
        return ok

    barrier = pltpu.get_barrier_semaphore()
    for dt, db in WAYS:

        @pl.when(exists(dt, db))
        def _():
            pl.semaphore_signal(
                barrier, inc=1, device_id=(t + dt, b + db), device_id_type=pl.DeviceIdType.MESH
            )

    def copy(phase, n):
        dt, db = WAYS[n]
        if n < 2:
            src = row_send.at[n] if phase == 0 else (mid_ref, p_out)[phase - 1].at[n * (rows - 1)]
            dst = row_in.at[n] if phase == 0 else row_in2.at[phase - 1, n]
        elif n < 4:
            src = col_send.at[n - 2] if phase == 0 else col_send2.at[phase - 1, n - 2]
            dst = col_in.at[n - 2] if phase == 0 else col_in2.at[phase - 1, n - 2]
        else:
            src = corner_send.at[n - 4] if phase == 0 else corner_send2.at[phase - 1, n - 4]
            dst = corner_in.at[n - 4] if phase == 0 else corner_in2.at[phase - 1, n - 4]
        return remote(src, dst, send.at[phase, n], recv.at[phase, n], (t + dt, b + db))

    def launch(phase):
        for n, (dt, db) in enumerate(WAYS):

            @pl.when(exists(dt, db))
            def _():
                copy(phase, n).start()

    def arrive(phase):
        for n, (dt, db) in enumerate(WAYS):

            @pl.when(exists(-dt, -db))
            def _():
                copy(phase, n).wait_recv()

    def depart(phase):
        for n, (dt, db) in enumerate(WAYS):

            @pl.when(exists(dt, db))
            def _():
                copy(phase, n).wait_send()

    def pack(phase, ref):
        for side in range(2):
            for r in range(rows):
                line = ref[r, side * (cols - 1) : side * (cols - 1) + 1]
                col_send2[phase - 1, side, r : r + 1] = line
        for n, (dt, db) in enumerate(WAYS[4:]):
            r, c = (dt > 0) * (rows - 1), (db > 0) * (cols - 1)
            corner_send2[phase - 1, n, 0:1] = ref[r, c : c + 1]

    fields = [(pos_ref, d) for d in range(3)] + [(p_ref, None)]
    for d, (ref, at) in enumerate(fields):
        view = ref if at is None else ref.at[at]
        for side in range(2):
            row_send[side, d] = view[side * (rows - 1)]
            for r in range(rows):
                line = view[r, side * (cols - 1) : side * (cols - 1) + 1]
                col_send[side, d, r : r + 1] = line
        for n, (dt, db) in enumerate(WAYS[4:]):
            r, c = (dt > 0) * (rows - 1), (db > 0) * (cols - 1)
            corner_send[n, d : d + 1] = view[r, c : c + 1]

    along = 1 + (t > 0).astype(jnp.int32) + (t < tiles - 1).astype(jnp.int32)
    across = 1 + (b > 0).astype(jnp.int32) + (b < parts - 1).astype(jnp.int32)
    build_own(pos_ref, lhs_ref, stage_ref, bx, by)

    def near_row(r, carry):
        x = (pos_ref[0, r] - centre(bx + r, cols, 0)) * UNIT
        y = (pos_ref[1, r] - centre(by, cols, 1)) * UNIT
        z = (pos_ref[2, r] - 0.5) * UNIT
        build_near(tab_ref, ((r + 1) * (cols + 2) + 1) * TABLE, 1, x, y, z)
        return carry

    lax.fori_loop(0, rows, near_row, 0)
    pl.semaphore_wait(barrier, along * across - 1)
    launch(0)

    def fill(ref):
        for r in range(rows):
            val_ref[(r + 1) * 16 + 1 : (r + 1) * 16 + 1 + cols] = ref[r]

    def slots(n):
        dt, db = WAYS[n]
        return (0 if dt > 0 else rows + 1), (0 if db > 0 else cols + 1)

    def halo_values(phase):
        for n, (dt, db) in enumerate(WAYS):
            ok = exists(-dt, -db)
            r, c = slots(n)
            if n < 2:
                got = row_in[n, 3] if phase == 0 else row_in2[phase - 1, n]
                val_ref[r * 16 + 1 : r * 16 + 1 + cols] = jnp.where(ok, got, 0.0)
            elif n < 4:
                got = col_in[n - 2, 3] if phase == 0 else col_in2[phase - 1, n - 2]
                val_ref[pl.ds(16 + c, rows, stride=16), :] = jnp.where(ok, got, 0.0)
            else:
                got = (
                    corner_in[n - 4, 3:4]
                    if phase == 0
                    else corner_in2[phase - 1, n - 4, 0:1]
                )
                val_ref[r * 16 + c : r * 16 + c + 1] = jnp.where(ok, got, 0.0)

    def halo_tables():
        for n, (dt, db) in enumerate(WAYS):
            ok = exists(-dt, -db)
            r, c = slots(n)
            across_r = bx - 1 if dt > 0 else bx + rows
            across_c = by - 1 if db > 0 else by + cols
            if n < 2:
                x, y, z = [jnp.where(ok, row_in[n, d], 0.0) for d in range(3)]
                x = x - centre(across_r, cols, 0)
                y = y - centre(by, cols, 1)
                start, stride = (r * (cols + 2) + 1) * TABLE, 1
            elif n < 4:
                x, y, z = [jnp.where(ok, col_in[n - 2, d], 0.0) for d in range(3)]
                x = x - centre(bx, rows, 1)
                y = y - centre(across_c, rows, 0)
                start, stride = (cols + 2 + c) * TABLE, cols + 2
            else:
                x, y, z = [jnp.where(ok, corner_in[n - 4, d : d + 1], 0.0) for d in range(3)]
                x = x - centre(across_r, 1, 0)
                y = y - centre(across_c, 1, 0)
                start, stride = (r * (cols + 2) + c) * TABLE, 1
            build_near(tab_ref, start, stride, x * UNIT, y * UNIT, (z - 0.5) * UNIT)

    def sweep(first, meet):
        def block(r, c):
            if first is None:
                wv = kept_block(r, c, near_ref, val_ref, keep_ref, cols)
            else:
                exponents = pair_exponents(r, c, near_ref, tab_ref, lhs_ref, cols)
                ws, wv = pair_sums(
                    r, c, exponents, near_ref, val_ref, keep_ref if first else None, cols
                )
                ws_ref[r, pl.ds(c, 1), :] = ws
            wv_ref[r, pl.ds(c, 1), :] = wv

        def column(c, carry):
            for r in range(1, rows - 1):
                block(r, c)
            return carry

        lax.fori_loop(1, cols - 1, column, 0)
        meet()
        lax.fori_loop(0, 2, lambda i, carry: column(i * (cols - 1), carry), 0)
        for r in (0, rows - 1):
            for c in range(cols):
                block(r, c)

    fill(p_ref)

    def meet(phase):
        arrive(phase)
        if phase == 0:
            halo_tables()
        halo_values(phase)

    def relax(before_ref, after_ref):
        pressure = before_ref[...]
        diagonal = stiff_ref[...] + ws_ref[...]
        residual = source_ref[...] - (diagonal * pressure - wv_ref[...])
        after_ref[...] = jnp.maximum(pressure + relax_factor * residual / diagonal, 0.0)
        return residual

    sweep(True, lambda: meet(0))
    relax(p_ref, mid_ref)
    pack(1, mid_ref)
    launch(1)
    fill(mid_ref)
    build_own(wall_ref, lhs_ref, stage_ref, bx, by)
    sweep(None, lambda: meet(1))
    residual = relax(mid_ref, p_out)
    pack(2, p_out)
    launch(2)
    error_out[...] = jnp.sum(residual * residual, axis=0)
    fill(p_out)
    sweep(False, lambda: meet(2))
    wp_out[...] = wv_ref[...] / (wall_offset + ws_ref[...]) * live_ref[...].astype(F32)
    for phase in range(3):
        depart(phase)


def fluid(near, pos, p, source, stiff, wall, live):
    rows, cols, _ = p.shape
    small = shape((rows, cols, 128))
    return pl.pallas_call(
        fluid_kernel,
        out_shape=(small, small, shape((cols, 128))),
        in_specs=[pl.BlockSpec(memory_space=SMEM)] + [pl.BlockSpec(memory_space=VMEM)] * 6,
        out_specs=(pl.BlockSpec(memory_space=VMEM),) * 3,
        scratch_shapes=[
            VMEM(((rows + 2) * (cols + 2) * TABLE * 8, 128), F32),
            VMEM(((rows + 2) * 16, 128), F32),
            VMEM((rows * cols * 128, 128), BF16),
            VMEM((rows * cols * near.shape[0] * 128, 128), F32),
            VMEM((OWN_GROUP, DEPTH * cols, 128), F32),
            VMEM((rows, cols, 128), F32),
            VMEM((rows, cols, 128), F32),
            VMEM((rows, cols, 128), F32),
            VMEM((2, 4, cols, 128), F32),
            VMEM((2, 4, cols, 128), F32),
            VMEM((2, 4, rows, 128), F32),
            VMEM((2, 4, rows, 128), F32),
            VMEM((4, 8, 128), F32),
            VMEM((4, 8, 128), F32),
            VMEM((2, 2, cols, 128), F32),
            VMEM((2, 2, rows, 128), F32),
            VMEM((2, 2, rows, 128), F32),
            VMEM((2, 4, 8, 128), F32),
            VMEM((2, 4, 8, 128), F32),
            pltpu.SemaphoreType.DMA((3, 8)),
            pltpu.SemaphoreType.DMA((3, 8)),
        ],
        compiler_params=pltpu.CompilerParams(
            collective_id=1, has_side_effects=True, vmem_limit_bytes=62 * 2**20
        ),
        name="fluid",
    )(near, pos, p, source, stiff, wall, live)


def split(x, n):
    if n & (n - 1):
        return lax.div(x, n), lax.rem(x, n)
    return x >> (n.bit_length() - 1), x & (n - 1)


def scatter_kernel(
    shard,
    owned,
    spare,
    wp_ref,
    normal_ref,
    arm_ref,
    body_ref,
    error_ref,
    acc_ref,
    first_ref,
    last_ref,
    stage_ref,
    hot_ref,
):
    rows, cols = wp_ref.shape[0], wp_ref.shape[1]
    acc_ref[...] = jnp.zeros_like(acc_ref)
    stage_ref[...] = jnp.zeros_like(stage_ref)
    for r in range(rows):
        top, _ = two_level(body_ref[r], owned, shard)
        first_ref[r] = jnp.min(top)
        last_ref[r] = jnp.max(top)
    low_iota = lax.broadcasted_iota(jnp.int32, (LOW, 128), 0).astype(F32).astype(BF16)
    one, zero = jnp.ones((LOW, 128), BF16), jnp.zeros((LOW, 128), BF16)
    lines = WINDOW * 16

    def window(r, e, start):
        wp = wp_ref[r]
        fx, fy, fz = [wp * normal_ref[d, r] for d in range(3)]
        ax, ay, az = [arm_ref[d, r] for d in range(3)]
        values = [fx, fy, fz, ay * fz - az * fy, az * fx - ax * fz, ax * fy - ay * fx]
        top, _ = two_level(body_ref[r], owned, shard)
        here = [top == start + w for w in range(WINDOW)]
        for q, value in enumerate(values):
            for s, piece in enumerate(pieces(value, 2)):
                for w in range(WINDOW):
                    at = (w * 16 + s * 8 + q) * cols
                    stage_ref[e, at : at + cols] = jnp.where(here[w], piece, 0.0)
        total = jnp.zeros((lines, LOW), F32)
        for c in range(0, cols, 2):
            lhs = jnp.concatenate(
                [stage_ref[e, pl.ds(c + k, lines, stride=cols), :] for k in range(2)], axis=1
            )
            total = total + lax.dot_general(
                lhs.astype(BF16),
                hot_ref[e, :, c * 128 : (c + 2) * 128],
                (((1,), (1,)), ((), ())),
                preferred_element_type=F32,
            )
        return [total[w * 16 : w * 16 + 8] + total[w * 16 + 8 : w * 16 + 16] for w in range(WINDOW)]

    def add(start, found):
        for w in range(WINDOW):
            acc_ref[start + w] += found[w]

    def group(i, carry):
        found = []
        for e in range(GROUP):
            r = i * GROUP + e
            _, low = two_level(body_ref[r], owned, shard)
            low = low.astype(F32)
            for c in range(cols):
                line = jnp.broadcast_to(low[c : c + 1], (LOW, 128)).astype(BF16)
                hot_ref[e, :, c * 128 : (c + 1) * 128] = jnp.where(low_iota == line, one, zero)
            found.append(window(r, e, first_ref[r]))
        for e in range(GROUP):
            add(first_ref[i * GROUP + e], found[e])
        for e in range(GROUP):
            r = i * GROUP + e

            def more(j, carry):
                start = first_ref[r] + j * WINDOW
                add(start, window(r, e, start))
                return carry

            lax.fori_loop(1, split(last_ref[r] - first_ref[r], WINDOW)[0] + 1, more, 0)
        return carry

    lax.fori_loop(0, rows // GROUP, group, 0)
    lane = lax.broadcasted_iota(jnp.int32, (8, LOW), 1)
    acc_ref[spare] = jnp.where(lane == 0, jnp.sum(error_ref[...]), 0.0)


def gather_kernel(
    per,
    lines,
    owned,
    first_ref,
    last_ref,
    table_ref,
    arm_ref,
    body_ref,
    p_ref,
    wp_ref,
    p_out,
    wp_out,
    out_ref,
    own_ref,
    error_ref,
):
    rows, cols = body_ref.shape[0], body_ref.shape[1]
    tiles, parts = lax.axis_size("tile"), lax.axis_size("body")
    chips, shard = tiles // 2, per * tiles
    spare = -(-owned // LOW)
    b = lax.axis_index("body")
    p_out[...] = p_ref[...]
    wp_out[...] = wp_ref[...]

    def place(top):
        p, rest = split(top, shard)
        t, n = split(rest, per)
        return (((t & 1) * parts + p) * chips + (t >> 1)) * lines + n

    def window(top, low, start, last, got):
        got = list(got)
        for w in range(WINDOW):
            here = top == start + w
            at = place(jnp.minimum(start + w, last))
            for q in range(6):
                line = jnp.broadcast_to(table_ref[pl.ds(at + q * per, 1), :], (cols, LOW))
                found = jnp.take_along_axis(line, low, axis=1, mode="promise_in_bounds")
                got[q] = jnp.where(here, found, got[q])
        return tuple(got)

    def group(i, carry):
        both, ends, states = [], [], []
        zero = jnp.zeros((cols, LOW), F32)
        for e in range(GROUP):
            r = i * GROUP + e
            both.append(two_level(body_ref[r], owned, shard))
            ends.append((first_ref[r], last_ref[r]))
            states.append(window(*both[e], ends[e][0], ends[e][1], (zero,) * 6))
        for e in range(GROUP):
            r = i * GROUP + e
            first, last = ends[e]

            def more(j, got):
                return window(*both[e], first + j * WINDOW, last, got)

            count = split(last - first, WINDOW)[0] + 1
            vx, vy, vz, wx, wy, wz = lax.fori_loop(1, count, more, states[e])
            ax, ay, az = [arm_ref[d, r] for d in range(3)]
            out_ref[0, r] = vx + (wy * az - wz * ay)
            out_ref[1, r] = vy + (wz * ax - wx * az)
            out_ref[2, r] = vz + (wx * ay - wy * ax)
        return carry

    lax.fori_loop(0, rows // GROUP, group, 0)
    for n in range(spare):
        wide = min(LOW, owned - n * LOW)
        t = n // per
        at = b * (chips * lines) + ((t % 2) * parts * chips + t // 2) * lines + n % per
        for q in range(6):
            line = table_ref[pl.ds(at + q * per, 1), :]
            own_ref[q : q + 1, n * LOW : n * LOW + wide] = line[:, :wide]
    t = spare // per
    at = ((t % 2) * parts * chips + t // 2) * lines + spare % per
    error_ref[...] = table_ref[at : at + 1]


def remote(src, dst, send, recv, device):
    return pltpu.make_async_remote_copy(
        src_ref=src,
        dst_ref=dst,
        send_sem=send,
        recv_sem=recv,
        device_id=device,
        device_id_type=pl.DeviceIdType.MESH,
    )


def exchange_kernel(
    per,
    acc_in,
    linear_in,
    angular_in,
    mass_in,
    inertia_in,
    g1_ref,
    acc_ref,
    linear_ref,
    angular_ref,
    mass_ref,
    inertia_ref,
    loaded,
    par_ref,
    partial_ref,
    r1_ref,
    s1_ref,
    r2_ref,
    s2_ref,
    r3_ref,
    send1,
    recv1,
    send2,
    recv2,
    send3,
    recv3,
    send4,
    recv4,
    send5,
    recv5,
    send6,
    recv6,
):
    parts, chips = r1_ref.shape[0], r1_ref.shape[1]
    spare = mass_ref.shape[0]
    shard = per * chips * 2
    t, b = lax.axis_index("tile"), lax.axis_index("body")
    core, chip = t % 2, t // 2
    barrier = pltpu.get_barrier_semaphore()
    partner = (chip * 2 + 1 - core, b)
    others2 = [(chip + k) % chips for k in range(1, chips)]
    upper = b >= parts // 2
    loads = [
        (acc_in, acc_ref),
        (linear_in, linear_ref),
        (angular_in, angular_ref),
        (mass_in, mass_ref),
        (inertia_in, inertia_ref),
    ]
    loads = [pltpu.make_async_copy(src, dst, loaded.at[n]) for n, (src, dst) in enumerate(loads)]
    for load in loads:
        load.start()
    others3 = [(b + jnp.where(upper, i, parts - i)) % parts for i in range(1, parts)]
    order, nearest = others3 + [b], others3[::-1]
    greeted = [partner] + [(g * 2 + core, b) for g in others2] + [(t, g) for g in others3]
    for device in greeted:
        pl.semaphore_signal(barrier, inc=1, device_id=device, device_id_type=pl.DeviceIdType.MESH)

    lines = partial_ref.shape[3]
    for load in loads:
        load.wait()
    for k in range(2):
        for p in range(parts):
            for g in range(chips):
                at = p * shard + (g * 2 + k) * per
                if lines > 6 * per:
                    partial_ref[k, p, g] = jnp.zeros((lines, LOW), F32)
                for q in range(6):
                    line = acc_ref[pl.ds(at * 8 + q, per, stride=8), :]
                    partial_ref[k, p, g, q * per : (q + 1) * per] = line
    for n in range(per):
        row = t * per + n
        held = row < spare
        row = jnp.minimum(row, spare - 1)
        at = pl.multiple_of(row * LOW, LOW)
        for d in range(3):
            own = slice(n, n + 1)
            par_ref[d, own] = jnp.where(held, linear_ref[d : d + 1, pl.ds(at, LOW)], 0.0)
            par_ref[3 + d, own] = jnp.where(held, angular_ref[d : d + 1, pl.ds(at, LOW)], 0.0)
            par_ref[7 + d, own] = jnp.where(held, inertia_ref[d : d + 1, pl.ds(at, LOW)], 0.0)
        par_ref[6, n : n + 1] = jnp.where(held, mass_ref[pl.ds(row, 1), :], 1.0 / time_step)
    pl.semaphore_wait(barrier, len(greeted))

    started = []

    def go(*args):
        item = remote(*args)
        item.start()
        started.append(item)

    for p in order:
        go(partial_ref.at[1 - core, p], r1_ref.at[p], send1.at[p], recv1.at[p], partner)
    for p in order:
        remote(
            partial_ref.at[1 - core, p], r1_ref.at[p], send1.at[p], recv1.at[p], partner
        ).wait_recv()
        s1_ref[p] = partial_ref[core, p] + r1_ref[p]
        for g in others2:
            go(
                s1_ref.at[p, g],
                r2_ref.at[p, chip],
                send2.at[p, g],
                recv2.at[p, chip],
                (g * 2 + core, b),
            )
    for i, p in enumerate(order):
        total = s1_ref[p, chip]
        for g in others2:
            remote(
                s1_ref.at[p, g], r2_ref.at[p, g], send2.at[p, g], recv2.at[p, g], partner
            ).wait_recv()
            total = total + r2_ref[p, g]
        s2_ref[p] = total
        if i < parts - 1:
            go(s2_ref.at[p], r3_ref.at[b], send3.at[p], recv3.at[b], (t, p))
    total = s2_ref[b]
    for g in nearest:
        remote(s2_ref.at[g], r3_ref.at[g], send3.at[g], recv3.at[g], partner).wait_recv()
        total = total + r3_ref[g]

    if lines > 6 * per:
        g1_ref[core, b, chip] = total
    for q in range(6):
        moved = total[q * per : (q + 1) * per]
        if q < 3:
            state = par_ref[q] + time_step * (par_ref[6] * moved)
        else:
            state = par_ref[q] + time_step * par_ref[4 + q] * moved
        if q == 2:
            state = state + time_step * gravity_z
        g1_ref[core, b, chip, q * per : (q + 1) * per] = state

    mine = g1_ref.at[core, b, chip]
    for p in others3:
        go(mine, mine, send4.at[p], recv4.at[b], (t, p))

    def spread(p):
        part = g1_ref.at[core, p, chip]
        for g in others2:
            go(part, part, send5.at[p, g], recv5.at[p, chip], (g * 2 + core, b))

    spread(b)
    for p in nearest:
        part = g1_ref.at[core, p, chip]
        remote(part, part, send4.at[p], recv4.at[p], partner).wait_recv()
        spread(p)
    for p in [b] + nearest:
        for g in others2:
            part = g1_ref.at[core, p, g]
            remote(part, part, send5.at[p, g], recv5.at[p, g], partner).wait_recv()
        go(g1_ref.at[core, p], g1_ref.at[core, p], send6.at[p], recv6.at[p], partner)
    for p in [b] + nearest:
        part = g1_ref.at[1 - core, p]
        remote(part, part, send6.at[p], recv6.at[p], partner).wait_recv()
    for item in started:
        item.wait_send()


def exchange(acc, params, per):
    tiles, parts = lax.axis_size("tile"), lax.axis_size("body")
    chips = tiles // 2
    chunk = (-(-6 * per // 8) * 8, LOW)
    wide = (parts, chips)
    dma = pltpu.SemaphoreType.DMA
    return pl.pallas_call(
        functools.partial(exchange_kernel, per),
        out_shape=shape((2,) + wide + chunk),
        in_specs=[pl.BlockSpec(memory_space=pl.ANY)] * 5,
        out_specs=pl.BlockSpec(memory_space=VMEM),
        scratch_shapes=[VMEM(ref.shape, F32) for ref in (acc, *params)]
        + [
            dma((5,)),
            VMEM((10, per, LOW), F32),
            VMEM((2,) + wide + chunk, F32),
            VMEM(wide + chunk, F32),
            VMEM(wide + chunk, F32),
            VMEM(wide + chunk, F32),
            VMEM((parts,) + chunk, F32),
            VMEM((parts,) + chunk, F32),
        ]
        + [dma(dims) for dims in ((parts,), wide, (parts,), (parts,), wide, (parts,)) for _ in range(2)],
        compiler_params=pltpu.CompilerParams(
            collective_id=9, has_side_effects=True, vmem_limit_bytes=52 * 2**20
        ),
        name="exchange",
    )(acc, *params)


def two_level(body, owned, shard):
    index = body
    for part in range(1, lax.axis_size("body")):
        index = index + jnp.where(body >= part * owned, shard * LOW - owned, 0)
    return index >> (LOW.bit_length() - 1), index & (LOW - 1)


def call(kernel, shapes, ins, scratch, spaces, name, outs=None, limit=60):
    outs = outs or jax.tree.map(lambda _: VMEM, shapes)
    return pl.pallas_call(
        kernel,
        out_shape=shapes,
        in_specs=[pl.BlockSpec(memory_space=s) for s in spaces],
        out_specs=jax.tree.map(lambda s: pl.BlockSpec(memory_space=s), outs),
        scratch_shapes=scratch,
        compiler_params=pltpu.CompilerParams(vmem_limit_bytes=limit * 2**20),
        name=name,
    )(*ins)


def shape(dims, kind=F32):
    return jax.ShapeDtypeStruct(tuple(dims), kind)


def shards(
    fluid_position,
    fluid_pressure,
    source,
    stiffness,
    neighbours,
    wall_position,
    wall_normal,
    wall_arm,
    wall_live,
    wall_body,
    linear_velocity,
    angular_velocity,
    inverse_mass,
    inverse_inertia,
):
    rows, cols, _ = fluid_pressure.shape
    small = shape((rows, cols, 128))
    near = jnp.transpose(neighbours, (2, 1, 0))
    pressure, wall_pressure, error = fluid(
        near, fluid_position, fluid_pressure, source, stiffness, wall_position, wall_live
    )
    particle_total = rows * cols * 128 * lax.axis_size("tile") * lax.axis_size("body")
    owned = inverse_mass.shape[0]
    tiles = lax.axis_size("tile")
    parts = lax.axis_size("body")
    spare = -(-owned // LOW)
    per = spare // tiles + 1
    shard = per * tiles
    spans = shape((rows,), jnp.int32)
    acc, first, last = call(
        functools.partial(scatter_kernel, shard, owned, spare),
        (shape((parts * shard + WINDOW, 8, LOW)), spans, spans),
        (wall_pressure, wall_normal, wall_arm, wall_body, error),
        [
            VMEM((GROUP, WINDOW * 16 * cols, 128), F32),
            VMEM((GROUP, LOW, cols * 128), BF16),
        ],
        [VMEM] * 5,
        "scatter",
        (VMEM, SMEM, SMEM),
        60,
    )
    mass = jnp.pad(inverse_mass, (0, spare * LOW - owned)).reshape(spare, LOW)
    acc = acc.reshape(-1, LOW)
    table = exchange(acc, (linear_velocity, angular_velocity, mass, inverse_inertia), per)
    lines = table.shape[3]
    pressure, wall_pressure, wall_velocity, own_state, error = call(
        functools.partial(gather_kernel, per, lines, owned),
        (small, small, shape((3, rows, cols, 128)), shape((6, owned)), shape((1, LOW))),
        (first, last, table.reshape(-1, LOW), wall_arm, wall_body, pressure, wall_pressure),
        [],
        [SMEM] * 2 + [VMEM] * 5,
        "gather",
        None,
        16,
    )
    density_error = error[0, 0] / particle_total
    return (pressure, wall_pressure, own_state, wall_velocity, density_error)


def solution(mesh):
    placed = (
        P(None, "tile", "body", None),
        P("tile", "body", None),
        P("tile", "body", None),
        P("tile", "body", None),
        P("tile", "body", None),
        P(None, "tile", "body", None),
        P(None, "tile", "body", None),
        P(None, "tile", "body", None),
        P("tile", "body", None),
        P("tile", "body", None),
        P(None, "body"),
        P(None, "body"),
        P("body"),
        P(None, "body"),
    )
    return jax.shard_map(
        shards,
        mesh=mesh,
        in_specs=placed,
        out_specs=(
            P("tile", "body", None),
            P("tile", "body", None),
            P(None, "body"),
            P(None, "tile", "body", None),
            P(),
        ),
        check_vma=False,
    )
```

```python
import math
import functools
import jax
import jax.numpy as jnp
from jax import lax
from jax.experimental import pallas as pl
from jax.experimental.pallas import tpu as pltpu
from jax.sharding import PartitionSpec as P

SWEEPS = 2

relax_factor = 0.5
inv_width = 2.0
kernel_scale = 0.0078125
wall_offset = 0.5
time_step = 0.25
gravity_z = -9.81

UNIT = math.sqrt(inv_width / math.log(2.0))
DEPTH = 32
LOW = 128
WINDOW = 6
TABLE = 7
GROUP = 4
OWN_GROUP = 8
F32, BF16 = jnp.float32, jnp.bfloat16
VMEM = pltpu.VMEM
SMEM = pltpu.SMEM


def pieces(x, count):
    out = []
    for _ in range(count):
        piece = x.astype(BF16).astype(F32)
        out.append(piece)
        x = x - piece
    return out


def near_rows(x):
    h, m, l = pieces(x, 3)
    return [h, m, h, l, h] + pieces(-(x * x), 3)


def own_rows(x):
    h, m, l = pieces(2.0 * x, 3)
    one = jnp.ones_like(x)
    return [h, h, m, h, l, one, one, one]


def centre(first, size, axis):
    at = first + lax.broadcasted_iota(jnp.int32, (size, 128), 0) if axis else first
    return at.astype(F32) + 0.5


def build_near(tab_ref, start, stride, x, y, z):
    count = x.shape[0]
    groups = [near_rows(x + (v - 1) * UNIT) for v in range(3)]
    groups += [near_rows(y + (v - 1) * UNIT) for v in range(3)]
    groups += [near_rows(z)]
    for g, group in enumerate(groups):
        for k, value in enumerate(group):
            at = (start + g) * 8 + k
            if count == 1:
                tab_ref[pl.ds(at, 1), :] = value
            else:
                tab_ref[pl.ds(at, count, stride=stride * TABLE * 8), :] = value


def build_own(pos_ref, lhs_ref, stage_ref, bx, by):
    rows, cols = pos_ref.shape[1], pos_ref.shape[2]
    stage_ref[...] = jnp.zeros_like(stage_ref)

    def group(i, carry):
        for e in range(OWN_GROUP):
            r = i * OWN_GROUP + e
            x = (pos_ref[0, r] - centre(bx + r, cols, 0)) * UNIT
            y = (pos_ref[1, r] - centre(by, cols, 1)) * UNIT
            z = (pos_ref[2, r] - 0.5) * UNIT
            norm = pieces(-(x * x + y * y + z * z), 3)
            for k, value in enumerate(own_rows(x) + own_rows(y) + own_rows(z) + norm):
                stage_ref[e, k * cols : (k + 1) * cols] = value
        for e in range(OWN_GROUP):
            for c in range(cols):
                start = pl.multiple_of(((i * OWN_GROUP + e) * cols + c) * 128, 128)
                turned = stage_ref[e, pl.ds(c, DEPTH, stride=cols), :].astype(BF16).T
                lhs_ref[pl.ds(start, 128), 0:DEPTH] = turned
        return carry

    lax.fori_loop(0, rows // OWN_GROUP, group, 0)


def listed_near(r, c, k, near_ref):
    code = near_ref[k, c, r]
    up = (code * 11) >> 5
    return up, code - up * 3


def pair_exponents(r, c, near_ref, tab_ref, lhs_ref, cols):
    ones = (lax.broadcasted_iota(jnp.int32, (8, 128), 0) < 3).astype(F32)
    listed = near_ref.shape[0]
    sides = []
    for k in range(listed):
        up, side = listed_near(r, c, k, near_ref)
        base = ((r + up) * (cols + 2) + c + side) * TABLE
        rows = [tab_ref[pl.ds(at * 8, 8), :] for at in (base + up, base + 3 + side, base + 6)]
        sides.append(jnp.concatenate(rows + [ones], axis=0).astype(BF16))
    lhs = lhs_ref[pl.ds(pl.multiple_of((r * cols + c) * 128, 128), 128), 0:DEPTH]
    return [
        jnp.dot(lhs, jnp.concatenate(sides[k : k + 2], axis=1), preferred_element_type=F32)
        for k in range(0, listed, 2)
    ]


def pair_sums(r, c, exponents, near_ref, val_ref, keep_ref, cols):
    block = r * cols + c
    listed = near_ref.shape[0]
    ws = wv = None
    for k in range(listed):
        up, side = listed_near(r, c, k, near_ref)
        value = val_ref[pl.ds((r + up) * 16 + c + side, 1), :]
        part = jnp.exp2(exponents[k // 2][:, k % 2 * 128 : k % 2 * 128 + 128])
        if keep_ref is not None:
            at = pl.multiple_of((block * listed + k) * 128, 128)
            keep_ref[pl.ds(at, 128), :] = part
        product = part * value
        ws = part if ws is None else ws + part
        wv = product if wv is None else wv + product
    return [jnp.sum(total.T, axis=0, keepdims=True) * kernel_scale for total in (ws, wv)]


def kept_block(r, c, near_ref, val_ref, keep_ref, cols):
    listed = near_ref.shape[0]
    block = r * cols + c
    wv = None
    for k in range(listed):
        code = near_ref[k, c, r]
        up = (code * 11) >> 5
        value = val_ref[pl.ds((r + up) * 16 + c + code - up * 3, 1), :]
        at = pl.multiple_of((block * listed + k) * 128, 128)
        product = keep_ref[pl.ds(at, 128), :] * value
        wv = product if wv is None else wv + product
    return jnp.sum(wv.T, axis=0, keepdims=True) * kernel_scale


WAYS = ((-1, 0), (1, 0), (0, -1), (0, 1), (-1, -1), (-1, 1), (1, -1), (1, 1))


def fluid_kernel(
    near_ref,
    pos_ref,
    p_ref,
    source_ref,
    stiff_ref,
    wall_ref,
    live_ref,
    p_out,
    wp_out,
    error_out,
    tab_ref,
    val_ref,
    lhs_ref,
    keep_ref,
    stage_ref,
    ws_ref,
    wv_ref,
    mid_ref,
    row_send,
    row_in,
    col_send,
    col_in,
    corner_send,
    corner_in,
    row_in2,
    col_send2,
    col_in2,
    corner_send2,
    corner_in2,
    send,
    recv,
):
    rows, cols = p_ref.shape[0], p_ref.shape[1]
    tiles, parts = lax.axis_size("tile"), lax.axis_size("body")
    t, b = lax.axis_index("tile"), lax.axis_index("body")
    bx, by = t * rows, b * cols

    def exists(dt, db):
        ok = jnp.bool_(True)
        if dt:
            ok = (t > 0) if dt < 0 else (t < tiles - 1)
        if db:
            side = (b > 0) if db < 0 else (b < parts - 1)
            ok = jnp.logical_and(ok, side) if dt else side
        return ok

    barrier = pltpu.get_barrier_semaphore()
    for dt, db in WAYS:

        @pl.when(exists(dt, db))
        def _():
            pl.semaphore_signal(
                barrier, inc=1, device_id=(t + dt, b + db), device_id_type=pl.DeviceIdType.MESH
            )

    def copy(phase, n):
        dt, db = WAYS[n]
        if n < 2:
            src = row_send.at[n] if phase == 0 else (mid_ref, p_out)[phase - 1].at[n * (rows - 1)]
            dst = row_in.at[n] if phase == 0 else row_in2.at[phase - 1, n]
        elif n < 4:
            src = col_send.at[n - 2] if phase == 0 else col_send2.at[phase - 1, n - 2]
            dst = col_in.at[n - 2] if phase == 0 else col_in2.at[phase - 1, n - 2]
        else:
            src = corner_send.at[n - 4] if phase == 0 else corner_send2.at[phase - 1, n - 4]
            dst = corner_in.at[n - 4] if phase == 0 else corner_in2.at[phase - 1, n - 4]
        return remote(src, dst, send.at[phase, n], recv.at[phase, n], (t + dt, b + db))

    def launch(phase):
        for n, (dt, db) in enumerate(WAYS):

            @pl.when(exists(dt, db))
            def _():
                copy(phase, n).start()

    def arrive(phase):
        for n, (dt, db) in enumerate(WAYS):

            @pl.when(exists(-dt, -db))
            def _():
                copy(phase, n).wait_recv()

    def depart(phase):
        for n, (dt, db) in enumerate(WAYS):

            @pl.when(exists(dt, db))
            def _():
                copy(phase, n).wait_send()

    def pack(phase, ref):
        for side in range(2):
            for r in range(rows):
                line = ref[r, side * (cols - 1) : side * (cols - 1) + 1]
                col_send2[phase - 1, side, r : r + 1] = line
        for n, (dt, db) in enumerate(WAYS[4:]):
            r, c = (dt > 0) * (rows - 1), (db > 0) * (cols - 1)
            corner_send2[phase - 1, n, 0:1] = ref[r, c : c + 1]

    fields = [(pos_ref, d) for d in range(3)] + [(p_ref, None)]
    for d, (ref, at) in enumerate(fields):
        view = ref if at is None else ref.at[at]
        for side in range(2):
            row_send[side, d] = view[side * (rows - 1)]
            for r in range(rows):
                line = view[r, side * (cols - 1) : side * (cols - 1) + 1]
                col_send[side, d, r : r + 1] = line
        for n, (dt, db) in enumerate(WAYS[4:]):
            r, c = (dt > 0) * (rows - 1), (db > 0) * (cols - 1)
            corner_send[n, d : d + 1] = view[r, c : c + 1]

    along = 1 + (t > 0).astype(jnp.int32) + (t < tiles - 1).astype(jnp.int32)
    across = 1 + (b > 0).astype(jnp.int32) + (b < parts - 1).astype(jnp.int32)
    build_own(pos_ref, lhs_ref, stage_ref, bx, by)

    def near_row(r, carry):
        x = (pos_ref[0, r] - centre(bx + r, cols, 0)) * UNIT
        y = (pos_ref[1, r] - centre(by, cols, 1)) * UNIT
        z = (pos_ref[2, r] - 0.5) * UNIT
        build_near(tab_ref, ((r + 1) * (cols + 2) + 1) * TABLE, 1, x, y, z)
        return carry

    lax.fori_loop(0, rows, near_row, 0)
    pl.semaphore_wait(barrier, along * across - 1)
    launch(0)

    def fill(ref):
        for r in range(rows):
            val_ref[(r + 1) * 16 + 1 : (r + 1) * 16 + 1 + cols] = ref[r]

    def slots(n):
        dt, db = WAYS[n]
        return (0 if dt > 0 else rows + 1), (0 if db > 0 else cols + 1)

    def halo_values(phase):
        for n, (dt, db) in enumerate(WAYS):
            ok = exists(-dt, -db)
            r, c = slots(n)
            if n < 2:
                got = row_in[n, 3] if phase == 0 else row_in2[phase - 1, n]
                val_ref[r * 16 + 1 : r * 16 + 1 + cols] = jnp.where(ok, got, 0.0)
            elif n < 4:
                got = col_in[n - 2, 3] if phase == 0 else col_in2[phase - 1, n - 2]
                val_ref[pl.ds(16 + c, rows, stride=16), :] = jnp.where(ok, got, 0.0)
            else:
                got = (
                    corner_in[n - 4, 3:4]
                    if phase == 0
                    else corner_in2[phase - 1, n - 4, 0:1]
                )
                val_ref[r * 16 + c : r * 16 + c + 1] = jnp.where(ok, got, 0.0)

    def halo_tables():
        for n, (dt, db) in enumerate(WAYS):
            ok = exists(-dt, -db)
            r, c = slots(n)
            across_r = bx - 1 if dt > 0 else bx + rows
            across_c = by - 1 if db > 0 else by + cols
            if n < 2:
                x, y, z = [jnp.where(ok, row_in[n, d], 0.0) for d in range(3)]
                x = x - centre(across_r, cols, 0)
                y = y - centre(by, cols, 1)
                start, stride = (r * (cols + 2) + 1) * TABLE, 1
            elif n < 4:
                x, y, z = [jnp.where(ok, col_in[n - 2, d], 0.0) for d in range(3)]
                x = x - centre(bx, rows, 1)
                y = y - centre(across_c, rows, 0)
                start, stride = (cols + 2 + c) * TABLE, cols + 2
            else:
                x, y, z = [jnp.where(ok, corner_in[n - 4, d : d + 1], 0.0) for d in range(3)]
                x = x - centre(across_r, 1, 0)
                y = y - centre(across_c, 1, 0)
                start, stride = (r * (cols + 2) + c) * TABLE, 1
            build_near(tab_ref, start, stride, x * UNIT, y * UNIT, (z - 0.5) * UNIT)

    def sweep(first, meet):
        def block(r, c):
            if first is None:
                wv = kept_block(r, c, near_ref, val_ref, keep_ref, cols)
            else:
                exponents = pair_exponents(r, c, near_ref, tab_ref, lhs_ref, cols)
                ws, wv = pair_sums(
                    r, c, exponents, near_ref, val_ref, keep_ref if first else None, cols
                )
                ws_ref[r, pl.ds(c, 1), :] = ws
            wv_ref[r, pl.ds(c, 1), :] = wv

        def columns(*chosen):
            for c in chosen:
                for r in range(1, rows - 1):
                    block(r, c)

        def inner(i, carry):
            columns(*[1 + i * wide + e for e in range(wide)])
            return carry

        def side(i, carry):
            columns(i * (cols - 1))
            return carry

        wide = 2 if (cols - 2) % 2 == 0 else 1
        lax.fori_loop(0, (cols - 2) // wide, inner, 0)
        meet()
        lax.fori_loop(0, 2, side, 0)
        for r in (0, rows - 1):
            for c in range(cols):
                block(r, c)

    fill(p_ref)

    def meet(phase):
        arrive(phase)
        if phase == 0:
            halo_tables()
        halo_values(phase)

    def relax(before_ref, after_ref):
        pressure = before_ref[...]
        diagonal = stiff_ref[...] + ws_ref[...]
        residual = source_ref[...] - (diagonal * pressure - wv_ref[...])
        after_ref[...] = jnp.maximum(pressure + relax_factor * residual / diagonal, 0.0)
        return residual

    sweep(True, lambda: meet(0))
    relax(p_ref, mid_ref)
    pack(1, mid_ref)
    launch(1)
    fill(mid_ref)
    build_own(wall_ref, lhs_ref, stage_ref, bx, by)
    sweep(None, lambda: meet(1))
    residual = relax(mid_ref, p_out)
    pack(2, p_out)
    launch(2)
    error_out[...] = jnp.sum(residual * residual, axis=0)
    fill(p_out)
    sweep(False, lambda: meet(2))
    wp_out[...] = wv_ref[...] / (wall_offset + ws_ref[...]) * live_ref[...].astype(F32)
    for phase in range(3):
        depart(phase)


def fluid(near, pos, p, source, stiff, wall, live):
    rows, cols, _ = p.shape
    small = shape((rows, cols, 128))
    return pl.pallas_call(
        fluid_kernel,
        out_shape=(small, small, shape((cols, 128))),
        in_specs=[pl.BlockSpec(memory_space=SMEM)] + [pl.BlockSpec(memory_space=VMEM)] * 6,
        out_specs=(pl.BlockSpec(memory_space=VMEM),) * 3,
        scratch_shapes=[
            VMEM(((rows + 2) * (cols + 2) * TABLE * 8, 128), F32),
            VMEM(((rows + 2) * 16, 128), F32),
            VMEM((rows * cols * 128, 128), BF16),
            VMEM((rows * cols * near.shape[0] * 128, 128), F32),
            VMEM((OWN_GROUP, DEPTH * cols, 128), F32),
            VMEM((rows, cols, 128), F32),
            VMEM((rows, cols, 128), F32),
            VMEM((rows, cols, 128), F32),
            VMEM((2, 4, cols, 128), F32),
            VMEM((2, 4, cols, 128), F32),
            VMEM((2, 4, rows, 128), F32),
            VMEM((2, 4, rows, 128), F32),
            VMEM((4, 8, 128), F32),
            VMEM((4, 8, 128), F32),
            VMEM((2, 2, cols, 128), F32),
            VMEM((2, 2, rows, 128), F32),
            VMEM((2, 2, rows, 128), F32),
            VMEM((2, 4, 8, 128), F32),
            VMEM((2, 4, 8, 128), F32),
            pltpu.SemaphoreType.DMA((3, 8)),
            pltpu.SemaphoreType.DMA((3, 8)),
        ],
        compiler_params=pltpu.CompilerParams(
            collective_id=1, has_side_effects=True, vmem_limit_bytes=62 * 2**20
        ),
        name="fluid",
    )(near, pos, p, source, stiff, wall, live)


def split(x, n):
    if n & (n - 1):
        return lax.div(x, n), lax.rem(x, n)
    return x >> (n.bit_length() - 1), x & (n - 1)


def scatter_kernel(
    per,
    owned,
    spare,
    wp_in,
    normal_in,
    arm_in,
    body_in,
    error_in,
    out_ref,
    first_ref,
    last_ref,
    wp_ref,
    normal_ref,
    arm_ref,
    body_ref,
    error_ref,
    acc_ref,
    part_ref,
    stage_ref,
    hot_ref,
    loaded,
    stored,
):
    rows, cols = wp_ref.shape[0], wp_ref.shape[1]
    parts, chips, lines = part_ref.shape[1:4]
    shard = per * chips * 2
    loads = [(body_in, body_ref), (wp_in, wp_ref), (normal_in, normal_ref), (arm_in, arm_ref)]
    loads += [(error_in, error_ref)]
    loads = [pltpu.make_async_copy(src, dst, loaded.at[n]) for n, (src, dst) in enumerate(loads)]
    for load in loads:
        load.start()
    acc_ref[...] = jnp.zeros_like(acc_ref)
    stage_ref[...] = jnp.zeros_like(stage_ref)
    loads[0].wait()
    for r in range(rows):
        top, _ = two_level(body_ref[r], owned, shard)
        first_ref[r] = jnp.min(top)
        last_ref[r] = jnp.max(top)
    for load in loads[1:]:
        load.wait()
    low_iota = lax.broadcasted_iota(jnp.int32, (LOW, 128), 0).astype(F32).astype(BF16)
    one, zero = jnp.ones((LOW, 128), BF16), jnp.zeros((LOW, 128), BF16)
    tall = WINDOW * 16

    def window(r, e, start):
        wp = wp_ref[r]
        fx, fy, fz = [wp * normal_ref[d, r] for d in range(3)]
        ax, ay, az = [arm_ref[d, r] for d in range(3)]
        values = [fx, fy, fz, ay * fz - az * fy, az * fx - ax * fz, ax * fy - ay * fx]
        top, _ = two_level(body_ref[r], owned, shard)
        here = [top == start + w for w in range(WINDOW)]
        for q, value in enumerate(values):
            for s, piece in enumerate(pieces(value, 2)):
                for w in range(WINDOW):
                    at = (w * 16 + s * 8 + q) * cols
                    stage_ref[e, at : at + cols] = jnp.where(here[w], piece, 0.0)
        total = jnp.zeros((tall, LOW), F32)
        for c in range(0, cols, 2):
            lhs = jnp.concatenate(
                [stage_ref[e, pl.ds(c + k, tall, stride=cols), :] for k in range(2)], axis=1
            )
            total = total + lax.dot_general(
                lhs.astype(BF16),
                hot_ref[e, :, c * 128 : (c + 2) * 128],
                (((1,), (1,)), ((), ())),
                preferred_element_type=F32,
            )
        return [total[w * 16 : w * 16 + 8] + total[w * 16 + 8 : w * 16 + 16] for w in range(WINDOW)]

    def add(start, found):
        for w in range(WINDOW):
            at = pl.multiple_of((start + w) * 8, 8)
            acc_ref[pl.ds(at, 8), :] += found[w]

    def group(i, carry):
        found = []
        for e in range(GROUP):
            r = i * GROUP + e
            _, low = two_level(body_ref[r], owned, shard)
            low = low.astype(F32)
            for c in range(cols):
                line = jnp.broadcast_to(low[c : c + 1], (LOW, 128)).astype(BF16)
                hot_ref[e, :, c * 128 : (c + 1) * 128] = jnp.where(low_iota == line, one, zero)
            found.append(window(r, e, first_ref[r]))
        for e in range(GROUP):
            add(first_ref[i * GROUP + e], found[e])
        for e in range(GROUP):
            r = i * GROUP + e

            def more(j, carry):
                start = first_ref[r] + j * WINDOW
                add(start, window(r, e, start))
                return carry

            lax.fori_loop(1, split(last_ref[r] - first_ref[r], WINDOW)[0] + 1, more, 0)
        return carry

    lax.fori_loop(0, rows // GROUP, group, 0)
    lane = lax.broadcasted_iota(jnp.int32, (8, LOW), 1)
    acc_ref[spare * 8 : spare * 8 + 8] = jnp.where(lane == 0, jnp.sum(error_ref[...]), 0.0)
    stores = []
    for p in range(parts):
        for k in range(2):
            for g in range(chips):
                at = p * shard + (g * 2 + k) * per
                if lines > 6 * per:
                    part_ref[k, p, g] = jnp.zeros((lines, LOW), F32)
                for q in range(6):
                    line = acc_ref[pl.ds(at * 8 + q, per, stride=8), :]
                    part_ref[k, p, g, q * per : (q + 1) * per] = line
            out = out_ref.at[k, p, :, 0:lines]
            move = pltpu.make_async_copy(part_ref.at[k, p], out, stored.at[k, p])
            move.start()
            stores.append(move)
    for move in stores:
        move.wait()


def gather_kernel(
    per,
    lines,
    owned,
    first_ref,
    last_ref,
    table_ref,
    arm_ref,
    body_ref,
    p_ref,
    wp_ref,
    p_out,
    wp_out,
    out_ref,
    own_ref,
    error_ref,
):
    rows, cols = body_ref.shape[0], body_ref.shape[1]
    tiles, parts = lax.axis_size("tile"), lax.axis_size("body")
    chips, shard = tiles // 2, per * tiles
    spare = -(-owned // LOW)
    b = lax.axis_index("body")
    p_out[...] = p_ref[...]
    wp_out[...] = wp_ref[...]

    def place(top):
        p, rest = split(top, shard)
        t, n = split(rest, per)
        return (((t & 1) * parts + p) * chips + (t >> 1)) * lines + n

    def window(top, low, start, last, got):
        got = list(got)
        for w in range(WINDOW):
            here = top == start + w
            at = place(jnp.minimum(start + w, last))
            for q in range(6):
                line = jnp.broadcast_to(table_ref[pl.ds(at + q * per, 1), :], (cols, LOW))
                found = jnp.take_along_axis(line, low, axis=1, mode="promise_in_bounds")
                got[q] = jnp.where(here, found, got[q])
        return tuple(got)

    def group(i, carry):
        both, ends, states = [], [], []
        zero = jnp.zeros((cols, LOW), F32)
        for e in range(GROUP):
            r = i * GROUP + e
            both.append(two_level(body_ref[r], owned, shard))
            ends.append((first_ref[r], last_ref[r]))
            states.append(window(*both[e], ends[e][0], ends[e][1], (zero,) * 6))
        for e in range(GROUP):
            r = i * GROUP + e
            first, last = ends[e]

            def more(j, got):
                return window(*both[e], first + j * WINDOW, last, got)

            count = split(last - first, WINDOW)[0] + 1
            vx, vy, vz, wx, wy, wz = lax.fori_loop(1, count, more, states[e])
            ax, ay, az = [arm_ref[d, r] for d in range(3)]
            out_ref[0, r] = vx + (wy * az - wz * ay)
            out_ref[1, r] = vy + (wz * ax - wx * az)
            out_ref[2, r] = vz + (wx * ay - wy * ax)
        return carry

    lax.fori_loop(0, rows // GROUP, group, 0)
    for n in range(spare):
        wide = min(LOW, owned - n * LOW)
        t = n // per
        at = b * (chips * lines) + ((t % 2) * parts * chips + t // 2) * lines + n % per
        for q in range(6):
            line = table_ref[pl.ds(at + q * per, 1), :]
            own_ref[q : q + 1, n * LOW : n * LOW + wide] = line[:, :wide]
    t = spare // per
    at = ((t % 2) * parts * chips + t // 2) * lines + spare % per
    error_ref[...] = table_ref[at : at + 1]


def remote(src, dst, send, recv, device):
    return pltpu.make_async_remote_copy(
        src_ref=src,
        dst_ref=dst,
        send_sem=send,
        recv_sem=recv,
        device_id=device,
        device_id_type=pl.DeviceIdType.MESH,
    )


def exchange_kernel(
    per,
    partial_ref,
    linear_in,
    angular_in,
    mass_in,
    inertia_in,
    g1_ref,
    held_ref,
    linear_ref,
    angular_ref,
    mass_ref,
    inertia_ref,
    loaded,
    par_ref,
    r1_ref,
    s1_ref,
    r2_ref,
    s2_ref,
    r3_ref,
    send1,
    recv1,
    send2,
    recv2,
    send3,
    recv3,
    send4,
    recv4,
    send5,
    recv5,
    send6,
    recv6,
):
    parts, chips = r1_ref.shape[0], r1_ref.shape[1]
    spare = mass_ref.shape[0]
    shard = per * chips * 2
    t, b = lax.axis_index("tile"), lax.axis_index("body")
    core, chip = t % 2, t // 2
    barrier = pltpu.get_barrier_semaphore()
    partner = (chip * 2 + 1 - core, b)
    others2 = [(chip + k) % chips for k in range(1, chips)]
    upper = b >= parts // 2
    lines = r1_ref.shape[2]
    loads = [
        (partial_ref.at[core, :, :, 0:lines], held_ref),
        (linear_in, linear_ref),
        (angular_in, angular_ref),
        (mass_in, mass_ref),
        (inertia_in, inertia_ref),
    ]
    loads = [pltpu.make_async_copy(src, dst, loaded.at[n]) for n, (src, dst) in enumerate(loads)]
    for load in loads:
        load.start()
    others3 = [(b + jnp.where(upper, i, parts - i)) % parts for i in range(1, parts)]
    order, nearest = others3 + [b], others3[::-1]
    greeted = [partner] + [(g * 2 + core, b) for g in others2] + [(t, g) for g in others3]
    for device in greeted:
        pl.semaphore_signal(barrier, inc=1, device_id=device, device_id_type=pl.DeviceIdType.MESH)

    for load in loads:
        load.wait()
    for n in range(per):
        row = t * per + n
        held = row < spare
        row = jnp.minimum(row, spare - 1)
        at = pl.multiple_of(row * LOW, LOW)
        for d in range(3):
            own = slice(n, n + 1)
            par_ref[d, own] = jnp.where(held, linear_ref[d : d + 1, pl.ds(at, LOW)], 0.0)
            par_ref[3 + d, own] = jnp.where(held, angular_ref[d : d + 1, pl.ds(at, LOW)], 0.0)
            par_ref[7 + d, own] = jnp.where(held, inertia_ref[d : d + 1, pl.ds(at, LOW)], 0.0)
        par_ref[6, n : n + 1] = jnp.where(held, mass_ref[pl.ds(row, 1), :], 1.0 / time_step)
    pl.semaphore_wait(barrier, len(greeted))

    started = []

    def go(*args):
        item = remote(*args)
        item.start()
        started.append(item)

    for p in order:
        piece = partial_ref.at[1 - core, p, :, 0:lines]
        go(piece, r1_ref.at[p], send1.at[p], recv1.at[p], partner)
    for p in order:
        piece = partial_ref.at[1 - core, p, :, 0:lines]
        remote(piece, r1_ref.at[p], send1.at[p], recv1.at[p], partner).wait_recv()
        s1_ref[p] = held_ref[p] + r1_ref[p]
        for g in others2:
            go(
                s1_ref.at[p, g],
                r2_ref.at[p, chip],
                send2.at[p, g],
                recv2.at[p, chip],
                (g * 2 + core, b),
            )
    for i, p in enumerate(order):
        total = s1_ref[p, chip]
        for g in others2:
            remote(
                s1_ref.at[p, g], r2_ref.at[p, g], send2.at[p, g], recv2.at[p, g], partner
            ).wait_recv()
            total = total + r2_ref[p, g]
        s2_ref[p] = total
        if i < parts - 1:
            go(s2_ref.at[p], r3_ref.at[b], send3.at[p], recv3.at[b], (t, p))
    total = s2_ref[b]
    for g in nearest:
        remote(s2_ref.at[g], r3_ref.at[g], send3.at[g], recv3.at[g], partner).wait_recv()
        total = total + r3_ref[g]

    if lines > 6 * per:
        g1_ref[core, b, chip] = total
    for q in range(6):
        moved = total[q * per : (q + 1) * per]
        if q < 3:
            state = par_ref[q] + time_step * (par_ref[6] * moved)
        else:
            state = par_ref[q] + time_step * par_ref[4 + q] * moved
        if q == 2:
            state = state + time_step * gravity_z
        g1_ref[core, b, chip, q * per : (q + 1) * per] = state

    mine = g1_ref.at[core, b, chip]
    for p in others3:
        go(mine, mine, send4.at[p], recv4.at[b], (t, p))

    def spread(p):
        part = g1_ref.at[core, p, chip]
        for g in others2:
            go(part, part, send5.at[p, g], recv5.at[p, chip], (g * 2 + core, b))

    spread(b)
    for p in nearest:
        part = g1_ref.at[core, p, chip]
        remote(part, part, send4.at[p], recv4.at[p], partner).wait_recv()
        spread(p)
    for p in [b] + nearest:
        for g in others2:
            part = g1_ref.at[core, p, g]
            remote(part, part, send5.at[p, g], recv5.at[p, g], partner).wait_recv()
        go(g1_ref.at[core, p], g1_ref.at[core, p], send6.at[p], recv6.at[p], partner)
    for p in [b] + nearest:
        part = g1_ref.at[1 - core, p]
        remote(part, part, send6.at[p], recv6.at[p], partner).wait_recv()
    for item in started:
        item.wait_send()


def exchange(partials, params, per, lines):
    tiles, parts = lax.axis_size("tile"), lax.axis_size("body")
    chips = tiles // 2
    chunk = (lines, LOW)
    wide = (parts, chips)
    dma = pltpu.SemaphoreType.DMA
    return pl.pallas_call(
        functools.partial(exchange_kernel, per),
        out_shape=shape((2,) + wide + chunk),
        in_specs=[pl.BlockSpec(memory_space=pl.ANY)] * 5,
        out_specs=pl.BlockSpec(memory_space=VMEM),
        scratch_shapes=[VMEM(dims, F32) for dims in [wide + chunk] + [x.shape for x in params]]
        + [
            dma((5,)),
            VMEM((10, per, LOW), F32),
            VMEM(wide + chunk, F32),
            VMEM(wide + chunk, F32),
            VMEM(wide + chunk, F32),
            VMEM((parts,) + chunk, F32),
            VMEM((parts,) + chunk, F32),
        ]
        + [dma(dims) for dims in ((parts,), wide, (parts,), (parts,), wide, (parts,)) for _ in range(2)],
        compiler_params=pltpu.CompilerParams(
            collective_id=9, has_side_effects=True, vmem_limit_bytes=52 * 2**20
        ),
        name="exchange",
    )(partials, *params)


def two_level(body, owned, shard):
    index = body
    for part in range(1, lax.axis_size("body")):
        index = index + jnp.where(body >= part * owned, shard * LOW - owned, 0)
    return index >> (LOW.bit_length() - 1), index & (LOW - 1)


def call(kernel, shapes, ins, scratch, spaces, name, outs=None, limit=60):
    outs = outs or jax.tree.map(lambda _: VMEM, shapes)
    return pl.pallas_call(
        kernel,
        out_shape=shapes,
        in_specs=[pl.BlockSpec(memory_space=s) for s in spaces],
        out_specs=jax.tree.map(lambda s: pl.BlockSpec(memory_space=s), outs),
        scratch_shapes=scratch,
        compiler_params=pltpu.CompilerParams(vmem_limit_bytes=limit * 2**20),
        name=name,
    )(*ins)


def shape(dims, kind=F32):
    return jax.ShapeDtypeStruct(tuple(dims), kind)


def shards(
    fluid_position,
    fluid_pressure,
    source,
    stiffness,
    neighbours,
    wall_position,
    wall_normal,
    wall_arm,
    wall_live,
    wall_body,
    linear_velocity,
    angular_velocity,
    inverse_mass,
    inverse_inertia,
):
    rows, cols, _ = fluid_pressure.shape
    small = shape((rows, cols, 128))
    near = jnp.transpose(neighbours, (2, 1, 0))
    pressure, wall_pressure, error = fluid(
        near, fluid_position, fluid_pressure, source, stiffness, wall_position, wall_live
    )
    particle_total = rows * cols * 128 * lax.axis_size("tile") * lax.axis_size("body")
    owned = inverse_mass.shape[0]
    tiles = lax.axis_size("tile")
    parts = lax.axis_size("body")
    spare = -(-owned // LOW)
    per = spare // tiles + 1
    shard = per * tiles
    spans = shape((rows,), jnp.int32)
    chunks = (2, parts, tiles // 2, -(-6 * per // 8) * 8, LOW)
    partials, first, last = call(
        functools.partial(scatter_kernel, per, owned, spare),
        (shape(chunks[:3] + (-(-chunks[3] // 6) * 8, LOW)), spans, spans),
        (wall_pressure, wall_normal, wall_arm, wall_body, error),
        [
            VMEM((rows, cols, 128), F32),
            VMEM((3, rows, cols, 128), F32),
            VMEM((3, rows, cols, 128), F32),
            VMEM((rows, cols, 128), jnp.int32),
            VMEM(error.shape, F32),
            VMEM(((parts * shard + WINDOW) * 8, LOW), F32),
            VMEM(chunks, F32),
            VMEM((GROUP, WINDOW * 16 * cols, 128), F32),
            VMEM((GROUP, LOW, cols * 128), BF16),
            pltpu.SemaphoreType.DMA((5,)),
            pltpu.SemaphoreType.DMA((2, parts)),
        ],
        [pl.ANY] * 5,
        "scatter",
        (pl.ANY, SMEM, SMEM),
        60,
    )
    mass = jnp.pad(inverse_mass, (0, spare * LOW - owned)).reshape(spare, LOW)
    lines = chunks[3]
    table = exchange(
        partials, (linear_velocity, angular_velocity, mass, inverse_inertia), per, lines
    )
    pressure, wall_pressure, wall_velocity, own_state, error = call(
        functools.partial(gather_kernel, per, lines, owned),
        (small, small, shape((3, rows, cols, 128)), shape((6, owned)), shape((1, LOW))),
        (first, last, table.reshape(-1, LOW), wall_arm, wall_body, pressure, wall_pressure),
        [],
        [SMEM] * 2 + [VMEM] * 5,
        "gather",
        None,
        16,
    )
    density_error = error[0, 0] / particle_total
    return (pressure, wall_pressure, own_state, wall_velocity, density_error)


def solution(mesh):
    placed = (
        P(None, "tile", "body", None),
        P("tile", "body", None),
        P("tile", "body", None),
        P("tile", "body", None),
        P("tile", "body", None),
        P(None, "tile", "body", None),
        P(None, "tile", "body", None),
        P(None, "tile", "body", None),
        P("tile", "body", None),
        P("tile", "body", None),
        P(None, "body"),
        P(None, "body"),
        P("body"),
        P(None, "body"),
    )
    return jax.shard_map(
        shards,
        mesh=mesh,
        in_specs=placed,
        out_specs=(
            P("tile", "body", None),
            P("tile", "body", None),
            P(None, "body"),
            P(None, "tile", "body", None),
            P(),
        ),
        check_vma=False,
    )
```

```python
import math
import functools
import jax
import jax.numpy as jnp
from jax import lax
from jax.experimental import pallas as pl
from jax.experimental.pallas import tpu as pltpu
from jax.sharding import PartitionSpec as P

SWEEPS = 2

relax_factor = 0.5
inv_width = 2.0
kernel_scale = 0.0078125
wall_offset = 0.5
time_step = 0.25
gravity_z = -9.81

UNIT = math.sqrt(inv_width / math.log(2.0))
DEPTH = 32
LOW = 128
WINDOW = 6
TABLE = 7
GROUP = 4
OWN_GROUP = 8
SCATTER_GROUP = 4
F32, BF16 = jnp.float32, jnp.bfloat16
VMEM = pltpu.VMEM
SMEM = pltpu.SMEM


def pieces(x, count):
    out = []
    for _ in range(count):
        piece = x.astype(BF16).astype(F32)
        out.append(piece)
        x = x - piece
    return out


def near_rows(x):
    h, m, l = pieces(x, 3)
    return [h, m, h, l, h] + pieces(-(x * x), 3)


def own_rows(x):
    h, m, l = pieces(2.0 * x, 3)
    one = jnp.ones_like(x)
    return [h, h, m, h, l, one, one, one]


def centre(first, size, axis):
    at = first + lax.broadcasted_iota(jnp.int32, (size, 128), 0) if axis else first
    return at.astype(F32) + 0.5


def build_near(tab_ref, start, stride, x, y, z):
    count = x.shape[0]
    groups = [near_rows(x + (v - 1) * UNIT) for v in range(3)]
    groups += [near_rows(y + (v - 1) * UNIT) for v in range(3)]
    groups += [near_rows(z)]
    for g, group in enumerate(groups):
        for k, value in enumerate(group):
            at = (start + g) * 8 + k
            if count == 1:
                tab_ref[pl.ds(at, 1), :] = value
            else:
                tab_ref[pl.ds(at, count, stride=stride * TABLE * 8), :] = value


def own_group(i, pos_ref, lhs_ref, stage_ref, bx, by, tab_ref=None):
    cols = pos_ref.shape[2]
    for e in range(OWN_GROUP):
        r = i * OWN_GROUP + e
        x = (pos_ref[0, r] - centre(bx + r, cols, 0)) * UNIT
        y = (pos_ref[1, r] - centre(by, cols, 1)) * UNIT
        z = (pos_ref[2, r] - 0.5) * UNIT
        norm = pieces(-(x * x + y * y + z * z), 3)
        for k, value in enumerate(own_rows(x) + own_rows(y) + own_rows(z) + norm):
            stage_ref[e, k * cols : (k + 1) * cols] = value
        if tab_ref is not None:
            build_near(tab_ref, ((r + 1) * (cols + 2) + 1) * TABLE, 1, x, y, z)
    for e in range(OWN_GROUP):
        for c in range(cols):
            start = pl.multiple_of(((i * OWN_GROUP + e) * cols + c) * 128, 128)
            turned = stage_ref[e, pl.ds(c, DEPTH, stride=cols), :].astype(BF16).T
            lhs_ref[pl.ds(start, 128), 0:DEPTH] = turned


def listed_near(r, c, k, near_ref):
    code = near_ref[k, c, r]
    up = (code * 11) >> 5
    return up, code - up * 3


def pair_exponents(r, c, near_ref, tab_ref, lhs_ref, cols):
    ones = (lax.broadcasted_iota(jnp.int32, (8, 128), 0) < 3).astype(F32)
    listed = near_ref.shape[0]
    sides = []
    for k in range(listed):
        up, side = listed_near(r, c, k, near_ref)
        base = ((r + up) * (cols + 2) + c + side) * TABLE
        rows = [tab_ref[pl.ds(at * 8, 8), :] for at in (base + up, base + 3 + side, base + 6)]
        sides.append(jnp.concatenate(rows + [ones], axis=0).astype(BF16))
    lhs = lhs_ref[pl.ds(pl.multiple_of((r * cols + c) * 128, 128), 128), 0:DEPTH]
    return [
        jnp.dot(lhs, jnp.concatenate(sides[k : k + 2], axis=1), preferred_element_type=F32)
        for k in range(0, listed, 2)
    ]


def pair_sums(r, c, exponents, near_ref, val_ref, keep_ref, cols):
    block = r * cols + c
    listed = near_ref.shape[0]
    ws = wv = None
    for k in range(listed):
        up, side = listed_near(r, c, k, near_ref)
        value = val_ref[pl.ds((r + up) * 16 + c + side, 1), :]
        part = jnp.exp2(exponents[k // 2][:, k % 2 * 128 : k % 2 * 128 + 128])
        if keep_ref is not None:
            at = pl.multiple_of((block * listed + k) * 128, 128)
            keep_ref[pl.ds(at, 128), :] = part
        product = part * value
        ws = part if ws is None else ws + part
        wv = product if wv is None else wv + product
    return [jnp.sum(total.T, axis=0, keepdims=True) * kernel_scale for total in (ws, wv)]


def kept_block(r, c, near_ref, val_ref, keep_ref, cols):
    listed = near_ref.shape[0]
    block = r * cols + c
    wv = None
    for k in range(listed):
        code = near_ref[k, c, r]
        up = (code * 11) >> 5
        value = val_ref[pl.ds((r + up) * 16 + c + code - up * 3, 1), :]
        at = pl.multiple_of((block * listed + k) * 128, 128)
        product = keep_ref[pl.ds(at, 128), :] * value
        wv = product if wv is None else wv + product
    return jnp.sum(wv.T, axis=0, keepdims=True) * kernel_scale


WAYS = ((-1, 0), (1, 0), (0, -1), (0, 1), (-1, -1), (-1, 1), (1, -1), (1, 1))


def fluid_kernel(
    near_ref,
    pos_ref,
    p_ref,
    source_ref,
    stiff_ref,
    wall_ref,
    live_ref,
    p_out,
    wp_out,
    error_out,
    tab_ref,
    val_ref,
    lhs_ref,
    keep_ref,
    stage_ref,
    ws_ref,
    wv_ref,
    mid_ref,
    row_send,
    row_in,
    col_send,
    col_in,
    corner_send,
    corner_in,
    row_in2,
    col_send2,
    col_in2,
    corner_send2,
    corner_in2,
    send,
    recv,
):
    rows, cols = p_ref.shape[0], p_ref.shape[1]
    tiles, parts = lax.axis_size("tile"), lax.axis_size("body")
    t, b = lax.axis_index("tile"), lax.axis_index("body")
    bx, by = t * rows, b * cols

    def exists(dt, db):
        ok = jnp.bool_(True)
        if dt:
            ok = (t > 0) if dt < 0 else (t < tiles - 1)
        if db:
            side = (b > 0) if db < 0 else (b < parts - 1)
            ok = jnp.logical_and(ok, side) if dt else side
        return ok

    barrier = pltpu.get_barrier_semaphore()
    for dt, db in WAYS:

        @pl.when(exists(dt, db))
        def _():
            pl.semaphore_signal(
                barrier, inc=1, device_id=(t + dt, b + db), device_id_type=pl.DeviceIdType.MESH
            )

    def copy(phase, n):
        dt, db = WAYS[n]
        if n < 2:
            src = row_send.at[n] if phase == 0 else (mid_ref, p_out)[phase - 1].at[n * (rows - 1)]
            dst = row_in.at[n] if phase == 0 else row_in2.at[phase - 1, n]
        elif n < 4:
            src = col_send.at[n - 2] if phase == 0 else col_send2.at[phase - 1, n - 2]
            dst = col_in.at[n - 2] if phase == 0 else col_in2.at[phase - 1, n - 2]
        else:
            src = corner_send.at[n - 4] if phase == 0 else corner_send2.at[phase - 1, n - 4]
            dst = corner_in.at[n - 4] if phase == 0 else corner_in2.at[phase - 1, n - 4]
        return remote(src, dst, send.at[phase, n], recv.at[phase, n], (t + dt, b + db))

    def launch(phase):
        for n, (dt, db) in enumerate(WAYS):

            @pl.when(exists(dt, db))
            def _():
                copy(phase, n).start()

    def arrive(phase):
        for n, (dt, db) in enumerate(WAYS):

            @pl.when(exists(-dt, -db))
            def _():
                copy(phase, n).wait_recv()

    def depart(phase):
        for n, (dt, db) in enumerate(WAYS):

            @pl.when(exists(dt, db))
            def _():
                copy(phase, n).wait_send()

    def pack(phase, ref):
        for side in range(2):
            for r in range(rows):
                line = ref[r, side * (cols - 1) : side * (cols - 1) + 1]
                col_send2[phase - 1, side, r : r + 1] = line
        for n, (dt, db) in enumerate(WAYS[4:]):
            r, c = (dt > 0) * (rows - 1), (db > 0) * (cols - 1)
            corner_send2[phase - 1, n, 0:1] = ref[r, c : c + 1]

    fields = [(pos_ref, d) for d in range(3)] + [(p_ref, None)]
    for d, (ref, at) in enumerate(fields):
        view = ref if at is None else ref.at[at]
        for side in range(2):
            row_send[side, d] = view[side * (rows - 1)]
            for r in range(rows):
                line = view[r, side * (cols - 1) : side * (cols - 1) + 1]
                col_send[side, d, r : r + 1] = line
        for n, (dt, db) in enumerate(WAYS[4:]):
            r, c = (dt > 0) * (rows - 1), (db > 0) * (cols - 1)
            corner_send[n, d : d + 1] = view[r, c : c + 1]

    along = 1 + (t > 0).astype(jnp.int32) + (t < tiles - 1).astype(jnp.int32)
    across = 1 + (b > 0).astype(jnp.int32) + (b < parts - 1).astype(jnp.int32)
    stage_ref[...] = jnp.zeros_like(stage_ref)
    groups = rows // OWN_GROUP

    def both(i, carry):
        own_group(i, pos_ref, lhs_ref, stage_ref, bx, by, tab_ref)
        return carry

    lax.fori_loop(0, groups, both, 0)
    pl.semaphore_wait(barrier, along * across - 1)
    launch(0)

    def fill(ref):
        for r in range(rows):
            val_ref[(r + 1) * 16 + 1 : (r + 1) * 16 + 1 + cols] = ref[r]

    def slots(n):
        dt, db = WAYS[n]
        return (0 if dt > 0 else rows + 1), (0 if db > 0 else cols + 1)

    def halo_values(phase):
        for n, (dt, db) in enumerate(WAYS):
            ok = exists(-dt, -db)
            r, c = slots(n)
            if n < 2:
                got = row_in[n, 3] if phase == 0 else row_in2[phase - 1, n]
                val_ref[r * 16 + 1 : r * 16 + 1 + cols] = jnp.where(ok, got, 0.0)
            elif n < 4:
                got = col_in[n - 2, 3] if phase == 0 else col_in2[phase - 1, n - 2]
                val_ref[pl.ds(16 + c, rows, stride=16), :] = jnp.where(ok, got, 0.0)
            else:
                got = (
                    corner_in[n - 4, 3:4]
                    if phase == 0
                    else corner_in2[phase - 1, n - 4, 0:1]
                )
                val_ref[r * 16 + c : r * 16 + c + 1] = jnp.where(ok, got, 0.0)

    def halo_tables():
        for n, (dt, db) in enumerate(WAYS):
            ok = exists(-dt, -db)
            r, c = slots(n)
            across_r = bx - 1 if dt > 0 else bx + rows
            across_c = by - 1 if db > 0 else by + cols
            if n < 2:
                x, y, z = [jnp.where(ok, row_in[n, d], 0.0) for d in range(3)]
                x = x - centre(across_r, cols, 0)
                y = y - centre(by, cols, 1)
                start, stride = (r * (cols + 2) + 1) * TABLE, 1
            elif n < 4:
                x, y, z = [jnp.where(ok, col_in[n - 2, d], 0.0) for d in range(3)]
                x = x - centre(bx, rows, 1)
                y = y - centre(across_c, rows, 0)
                start, stride = (cols + 2 + c) * TABLE, cols + 2
            else:
                x, y, z = [jnp.where(ok, corner_in[n - 4, d : d + 1], 0.0) for d in range(3)]
                x = x - centre(across_r, 1, 0)
                y = y - centre(across_c, 1, 0)
                start, stride = (r * (cols + 2) + c) * TABLE, 1
            build_near(tab_ref, start, stride, x * UNIT, y * UNIT, (z - 0.5) * UNIT)

    def sweep(first, meet):
        def block(r, c):
            if first is None:
                wv = kept_block(r, c, near_ref, val_ref, keep_ref, cols)
            else:
                exponents = pair_exponents(r, c, near_ref, tab_ref, lhs_ref, cols)
                ws, wv = pair_sums(
                    r, c, exponents, near_ref, val_ref, keep_ref if first else None, cols
                )
                ws_ref[r, pl.ds(c, 1), :] = ws
            wv_ref[r, pl.ds(c, 1), :] = wv

        def columns(*chosen):
            for c in chosen:
                for r in range(1, rows - 1):
                    block(r, c)

        def inner(i, carry):
            columns(*[1 + i * wide + e for e in range(wide)])
            return carry

        def side(i, carry):
            columns(i * (cols - 1))
            if first is None:
                for e in range(groups // 2):
                    own_group(i * (groups // 2) + e, wall_ref, lhs_ref, stage_ref, bx, by)
            return carry

        wide = 2 if (cols - 2) % 2 == 0 else 1
        lax.fori_loop(0, (cols - 2) // wide, inner, 0)
        meet()
        lax.fori_loop(0, 2, side, 0)
        for r in (0, rows - 1):
            for c in range(cols):
                block(r, c)

    fill(p_ref)

    def meet(phase):
        arrive(phase)
        if phase == 0:
            halo_tables()
        halo_values(phase)

    def relax(before_ref, after_ref):
        pressure = before_ref[...]
        diagonal = stiff_ref[...] + ws_ref[...]
        residual = source_ref[...] - (diagonal * pressure - wv_ref[...])
        after_ref[...] = jnp.maximum(pressure + relax_factor * residual / diagonal, 0.0)
        return residual

    sweep(True, lambda: meet(0))
    relax(p_ref, mid_ref)
    pack(1, mid_ref)
    launch(1)
    fill(mid_ref)
    sweep(None, lambda: meet(1))
    residual = relax(mid_ref, p_out)
    pack(2, p_out)
    launch(2)
    error_out[...] = jnp.sum(residual * residual, axis=0)
    fill(p_out)
    sweep(False, lambda: meet(2))
    wp_out[...] = wv_ref[...] / (wall_offset + ws_ref[...]) * live_ref[...].astype(F32)
    for phase in range(3):
        depart(phase)


def fluid(near, pos, p, source, stiff, wall, live):
    rows, cols, _ = p.shape
    small = shape((rows, cols, 128))
    return pl.pallas_call(
        fluid_kernel,
        out_shape=(small, small, shape((cols, 128))),
        in_specs=[pl.BlockSpec(memory_space=SMEM)] + [pl.BlockSpec(memory_space=VMEM)] * 6,
        out_specs=(pl.BlockSpec(memory_space=VMEM),) * 3,
        scratch_shapes=[
            VMEM(((rows + 2) * (cols + 2) * TABLE * 8, 128), F32),
            VMEM(((rows + 2) * 16, 128), F32),
            VMEM((rows * cols * 128, 128), BF16),
            VMEM((rows * cols * near.shape[0] * 128, 128), F32),
            VMEM((OWN_GROUP, DEPTH * cols, 128), F32),
            VMEM((rows, cols, 128), F32),
            VMEM((rows, cols, 128), F32),
            VMEM((rows, cols, 128), F32),
            VMEM((2, 4, cols, 128), F32),
            VMEM((2, 4, cols, 128), F32),
            VMEM((2, 4, rows, 128), F32),
            VMEM((2, 4, rows, 128), F32),
            VMEM((4, 8, 128), F32),
            VMEM((4, 8, 128), F32),
            VMEM((2, 2, cols, 128), F32),
            VMEM((2, 2, rows, 128), F32),
            VMEM((2, 2, rows, 128), F32),
            VMEM((2, 4, 8, 128), F32),
            VMEM((2, 4, 8, 128), F32),
            pltpu.SemaphoreType.DMA((3, 8)),
            pltpu.SemaphoreType.DMA((3, 8)),
        ],
        compiler_params=pltpu.CompilerParams(
            collective_id=1, has_side_effects=True, vmem_limit_bytes=62 * 2**20
        ),
        name="fluid",
    )(near, pos, p, source, stiff, wall, live)


def split(x, n):
    if n & (n - 1):
        return lax.div(x, n), lax.rem(x, n)
    return x >> (n.bit_length() - 1), x & (n - 1)


def find_spans(body_ref, first_ref, last_ref, owned, shard):
    for r in range(body_ref.shape[0]):
        top, _ = two_level(body_ref[r], owned, shard)
        first_ref[r] = jnp.min(top)
        last_ref[r] = jnp.max(top)


def scatter_kernel(
    per,
    owned,
    spare,
    wp_in,
    normal_in,
    arm_in,
    body_in,
    error_in,
    out_ref,
    first_ref,
    last_ref,
    wp_ref,
    normal_ref,
    arm_ref,
    body_ref,
    error_ref,
    acc_ref,
    part_ref,
    stage_ref,
    hot_ref,
    loaded,
    stored,
):
    rows, cols = wp_ref.shape[0], wp_ref.shape[1]
    parts, chips, lines = part_ref.shape[1:4]
    shard = per * chips * 2
    loads = [(body_in, body_ref), (wp_in, wp_ref), (normal_in, normal_ref), (arm_in, arm_ref)]
    loads += [(error_in, error_ref)]
    loads = [pltpu.make_async_copy(src, dst, loaded.at[n]) for n, (src, dst) in enumerate(loads)]
    for load in loads:
        load.start()
    acc_ref[...] = jnp.zeros_like(acc_ref)
    stage_ref[...] = jnp.zeros_like(stage_ref)
    loads[0].wait()
    find_spans(body_ref, first_ref, last_ref, owned, shard)
    for load in loads[1:]:
        load.wait()
    low_iota = lax.broadcasted_iota(jnp.int32, (LOW, 128), 0).astype(F32).astype(BF16)
    one, zero = jnp.ones((LOW, 128), BF16), jnp.zeros((LOW, 128), BF16)
    tall = WINDOW * 16

    def window(r, e, start):
        wp = wp_ref[r]
        fx, fy, fz = [wp * normal_ref[d, r] for d in range(3)]
        ax, ay, az = [arm_ref[d, r] for d in range(3)]
        values = [fx, fy, fz, ay * fz - az * fy, az * fx - ax * fz, ax * fy - ay * fx]
        top, _ = two_level(body_ref[r], owned, shard)
        here = [top == start + w for w in range(WINDOW)]
        for q, value in enumerate(values):
            for s, piece in enumerate(pieces(value, 2)):
                for w in range(WINDOW):
                    at = (w * 16 + s * 8 + q) * cols
                    stage_ref[e, at : at + cols] = jnp.where(here[w], piece, 0.0)
        total = jnp.zeros((tall, LOW), F32)
        for c in range(0, cols, 2):
            lhs = jnp.concatenate(
                [stage_ref[e, pl.ds(c + k, tall, stride=cols), :] for k in range(2)], axis=1
            )
            total = total + lax.dot_general(
                lhs.astype(BF16),
                hot_ref[e, :, c * 128 : (c + 2) * 128],
                (((1,), (1,)), ((), ())),
                preferred_element_type=F32,
            )
        return [total[w * 16 : w * 16 + 8] + total[w * 16 + 8 : w * 16 + 16] for w in range(WINDOW)]

    def add(start, found):
        for w in range(WINDOW):
            at = pl.multiple_of((start + w) * 8, 8)
            acc_ref[pl.ds(at, 8), :] += found[w]

    def group(i, carry):
        found = []
        for e in range(SCATTER_GROUP):
            r = i * SCATTER_GROUP + e
            _, low = two_level(body_ref[r], owned, shard)
            low = low.astype(F32)
            for c in range(cols):
                line = jnp.broadcast_to(low[c : c + 1], (LOW, 128)).astype(BF16)
                hot_ref[e, :, c * 128 : (c + 1) * 128] = jnp.where(low_iota == line, one, zero)
            found.append(window(r, e, first_ref[r]))
        for e in range(SCATTER_GROUP):
            add(first_ref[i * SCATTER_GROUP + e], found[e])
        for e in range(SCATTER_GROUP):
            r = i * SCATTER_GROUP + e

            def more(j, carry):
                start = first_ref[r] + j * WINDOW
                add(start, window(r, e, start))
                return carry

            lax.fori_loop(1, split(last_ref[r] - first_ref[r], WINDOW)[0] + 1, more, 0)
        return carry

    lax.fori_loop(0, rows // SCATTER_GROUP, group, 0)
    lane = lax.broadcasted_iota(jnp.int32, (8, LOW), 1)
    acc_ref[spare * 8 : spare * 8 + 8] = jnp.where(lane == 0, jnp.sum(error_ref[...]), 0.0)
    stores = []
    for p in range(parts):
        for k in range(2):
            for g in range(chips):
                at = p * shard + (g * 2 + k) * per
                if lines > 6 * per:
                    part_ref[k, p, g] = jnp.zeros((lines, LOW), F32)
                for q in range(6):
                    line = acc_ref[pl.ds(at * 8 + q, per, stride=8), :]
                    part_ref[k, p, g, q * per : (q + 1) * per] = line
            out = out_ref.at[k, p, :, 0:lines]
            move = pltpu.make_async_copy(part_ref.at[k, p], out, stored.at[k, p])
            move.start()
            stores.append(move)
    for move in stores:
        move.wait()


def gather_kernel(
    per,
    lines,
    owned,
    table_ref,
    arm_ref,
    body_ref,
    p_ref,
    wp_ref,
    p_out,
    wp_out,
    out_ref,
    own_ref,
    error_ref,
    first_ref,
    last_ref,
):
    rows, cols = body_ref.shape[0], body_ref.shape[1]
    tiles, parts = lax.axis_size("tile"), lax.axis_size("body")
    chips, shard = tiles // 2, per * tiles
    spare = -(-owned // LOW)
    b = lax.axis_index("body")
    find_spans(body_ref, first_ref, last_ref, owned, shard)
    p_out[...] = p_ref[...]
    wp_out[...] = wp_ref[...]

    def place(top):
        p, rest = split(top, shard)
        t, n = split(rest, per)
        return (((t & 1) * parts + p) * chips + (t >> 1)) * lines + n

    def window(top, low, start, last, got):
        got = list(got)
        for w in range(WINDOW):
            here = top == start + w
            at = place(jnp.minimum(start + w, last))
            for q in range(6):
                line = jnp.broadcast_to(table_ref[pl.ds(at + q * per, 1), :], (cols, LOW))
                found = jnp.take_along_axis(line, low, axis=1, mode="promise_in_bounds")
                got[q] = jnp.where(here, found, got[q])
        return tuple(got)

    def group(i, carry):
        both, ends, states = [], [], []
        zero = jnp.zeros((cols, LOW), F32)
        for e in range(GROUP):
            r = i * GROUP + e
            both.append(two_level(body_ref[r], owned, shard))
            ends.append((first_ref[r], last_ref[r]))
            states.append(window(*both[e], ends[e][0], ends[e][1], (zero,) * 6))
        for e in range(GROUP):
            r = i * GROUP + e
            first, last = ends[e]

            def more(j, got):
                return window(*both[e], first + j * WINDOW, last, got)

            count = split(last - first, WINDOW)[0] + 1
            vx, vy, vz, wx, wy, wz = lax.fori_loop(1, count, more, states[e])
            ax, ay, az = [arm_ref[d, r] for d in range(3)]
            out_ref[0, r] = vx + (wy * az - wz * ay)
            out_ref[1, r] = vy + (wz * ax - wx * az)
            out_ref[2, r] = vz + (wx * ay - wy * ax)
        return carry

    lax.fori_loop(0, rows // GROUP, group, 0)
    for n in range(spare):
        wide = min(LOW, owned - n * LOW)
        t = n // per
        at = b * (chips * lines) + ((t % 2) * parts * chips + t // 2) * lines + n % per
        for q in range(6):
            line = table_ref[pl.ds(at + q * per, 1), :]
            own_ref[q : q + 1, n * LOW : n * LOW + wide] = line[:, :wide]
    t = spare // per
    at = ((t % 2) * parts * chips + t // 2) * lines + spare % per
    error_ref[...] = table_ref[at : at + 1]


def remote(src, dst, send, recv, device):
    return pltpu.make_async_remote_copy(
        src_ref=src,
        dst_ref=dst,
        send_sem=send,
        recv_sem=recv,
        device_id=device,
        device_id_type=pl.DeviceIdType.MESH,
    )


def exchange_kernel(
    per,
    partial_ref,
    linear_in,
    angular_in,
    mass_in,
    inertia_in,
    g1_ref,
    held_ref,
    linear_ref,
    angular_ref,
    mass_ref,
    inertia_ref,
    loaded,
    par_ref,
    r1_ref,
    s1_ref,
    r2_ref,
    s2_ref,
    r3_ref,
    send1,
    recv1,
    send2,
    recv2,
    send3,
    recv3,
    send4,
    recv4,
    send5,
    recv5,
    send6,
    recv6,
):
    parts, chips = r1_ref.shape[0], r1_ref.shape[1]
    spare = mass_ref.shape[0]
    shard = per * chips * 2
    t, b = lax.axis_index("tile"), lax.axis_index("body")
    core, chip = t % 2, t // 2
    barrier = pltpu.get_barrier_semaphore()
    partner = (chip * 2 + 1 - core, b)
    others2 = [(chip + k) % chips for k in range(1, chips)]
    upper = b >= parts // 2
    lines = r1_ref.shape[2]
    loads = [
        (partial_ref.at[core, :, :, 0:lines], held_ref),
        (linear_in, linear_ref),
        (angular_in, angular_ref),
        (mass_in, mass_ref),
        (inertia_in, inertia_ref),
    ]
    loads = [pltpu.make_async_copy(src, dst, loaded.at[n]) for n, (src, dst) in enumerate(loads)]
    for load in loads:
        load.start()
    others3 = [(b + jnp.where(upper, i, parts - i)) % parts for i in range(1, parts)]
    order, nearest = others3 + [b], others3[::-1]
    greeted = [partner] + [(g * 2 + core, b) for g in others2] + [(t, g) for g in others3]
    for device in greeted:
        pl.semaphore_signal(barrier, inc=1, device_id=device, device_id_type=pl.DeviceIdType.MESH)

    for load in loads:
        load.wait()
    for n in range(per):
        row = t * per + n
        held = row < spare
        row = jnp.minimum(row, spare - 1)
        at = pl.multiple_of(row * LOW, LOW)
        for d in range(3):
            own = slice(n, n + 1)
            par_ref[d, own] = jnp.where(held, linear_ref[d : d + 1, pl.ds(at, LOW)], 0.0)
            par_ref[3 + d, own] = jnp.where(held, angular_ref[d : d + 1, pl.ds(at, LOW)], 0.0)
            par_ref[7 + d, own] = jnp.where(held, inertia_ref[d : d + 1, pl.ds(at, LOW)], 0.0)
        par_ref[6, n : n + 1] = jnp.where(held, mass_ref[pl.ds(row, 1), :], 1.0 / time_step)
    pl.semaphore_wait(barrier, len(greeted))

    started = []

    def go(*args):
        item = remote(*args)
        item.start()
        started.append(item)

    for p in order:
        piece = partial_ref.at[1 - core, p, :, 0:lines]
        go(piece, r1_ref.at[p], send1.at[p], recv1.at[p], partner)
    for p in order:
        piece = partial_ref.at[1 - core, p, :, 0:lines]
        remote(piece, r1_ref.at[p], send1.at[p], recv1.at[p], partner).wait_recv()
        s1_ref[p] = held_ref[p] + r1_ref[p]
        for g in others2:
            go(
                s1_ref.at[p, g],
                r2_ref.at[p, chip],
                send2.at[p, g],
                recv2.at[p, chip],
                (g * 2 + core, b),
            )
    for i, p in enumerate(order):
        total = s1_ref[p, chip]
        for g in others2:
            remote(
                s1_ref.at[p, g], r2_ref.at[p, g], send2.at[p, g], recv2.at[p, g], partner
            ).wait_recv()
            total = total + r2_ref[p, g]
        s2_ref[p] = total
        if i < parts - 1:
            go(s2_ref.at[p], r3_ref.at[b], send3.at[p], recv3.at[b], (t, p))
    total = s2_ref[b]
    for g in nearest:
        remote(s2_ref.at[g], r3_ref.at[g], send3.at[g], recv3.at[g], partner).wait_recv()
        total = total + r3_ref[g]

    if lines > 6 * per:
        g1_ref[core, b, chip] = total
    for q in range(6):
        moved = total[q * per : (q + 1) * per]
        if q < 3:
            state = par_ref[q] + time_step * (par_ref[6] * moved)
        else:
            state = par_ref[q] + time_step * par_ref[4 + q] * moved
        if q == 2:
            state = state + time_step * gravity_z
        g1_ref[core, b, chip, q * per : (q + 1) * per] = state

    mine = g1_ref.at[core, b, chip]
    for p in others3:
        go(mine, mine, send4.at[p], recv4.at[b], (t, p))

    def spread(p):
        part = g1_ref.at[core, p, chip]
        for g in others2:
            go(part, part, send5.at[p, g], recv5.at[p, chip], (g * 2 + core, b))

    spread(b)
    for p in nearest:
        part = g1_ref.at[core, p, chip]
        remote(part, part, send4.at[p], recv4.at[p], partner).wait_recv()
        spread(p)
    for p in [b] + nearest:
        for g in others2:
            part = g1_ref.at[core, p, g]
            remote(part, part, send5.at[p, g], recv5.at[p, g], partner).wait_recv()
        go(g1_ref.at[core, p], g1_ref.at[core, p], send6.at[p], recv6.at[p], partner)
    for p in [b] + nearest:
        part = g1_ref.at[1 - core, p]
        remote(part, part, send6.at[p], recv6.at[p], partner).wait_recv()
    for item in started:
        item.wait_send()


def exchange(partials, params, per, lines):
    tiles, parts = lax.axis_size("tile"), lax.axis_size("body")
    chips = tiles // 2
    chunk = (lines, LOW)
    wide = (parts, chips)
    dma = pltpu.SemaphoreType.DMA
    return pl.pallas_call(
        functools.partial(exchange_kernel, per),
        out_shape=shape((2,) + wide + chunk),
        in_specs=[pl.BlockSpec(memory_space=pl.ANY)] * 5,
        out_specs=pl.BlockSpec(memory_space=VMEM),
        scratch_shapes=[VMEM(dims, F32) for dims in [wide + chunk] + [x.shape for x in params]]
        + [
            dma((5,)),
            VMEM((10, per, LOW), F32),
            VMEM(wide + chunk, F32),
            VMEM(wide + chunk, F32),
            VMEM(wide + chunk, F32),
            VMEM((parts,) + chunk, F32),
            VMEM((parts,) + chunk, F32),
        ]
        + [dma(dims) for dims in ((parts,), wide, (parts,), (parts,), wide, (parts,)) for _ in range(2)],
        compiler_params=pltpu.CompilerParams(
            collective_id=9, has_side_effects=True, vmem_limit_bytes=52 * 2**20
        ),
        name="exchange",
    )(partials, *params)


def two_level(body, owned, shard):
    index = body
    for part in range(1, lax.axis_size("body")):
        index = index + jnp.where(body >= part * owned, shard * LOW - owned, 0)
    return index >> (LOW.bit_length() - 1), index & (LOW - 1)


def call(kernel, shapes, ins, scratch, spaces, name, outs=None, limit=60):
    outs = outs or jax.tree.map(lambda _: VMEM, shapes)
    return pl.pallas_call(
        kernel,
        out_shape=shapes,
        in_specs=[pl.BlockSpec(memory_space=s) for s in spaces],
        out_specs=jax.tree.map(lambda s: pl.BlockSpec(memory_space=s), outs),
        scratch_shapes=scratch,
        compiler_params=pltpu.CompilerParams(vmem_limit_bytes=limit * 2**20),
        name=name,
    )(*ins)


def shape(dims, kind=F32):
    return jax.ShapeDtypeStruct(tuple(dims), kind)


def shards(
    fluid_position,
    fluid_pressure,
    source,
    stiffness,
    neighbours,
    wall_position,
    wall_normal,
    wall_arm,
    wall_live,
    wall_body,
    linear_velocity,
    angular_velocity,
    inverse_mass,
    inverse_inertia,
):
    rows, cols, _ = fluid_pressure.shape
    small = shape((rows, cols, 128))
    near = jnp.transpose(neighbours, (2, 1, 0))
    pressure, wall_pressure, error = fluid(
        near, fluid_position, fluid_pressure, source, stiffness, wall_position, wall_live
    )
    particle_total = rows * cols * 128 * lax.axis_size("tile") * lax.axis_size("body")
    owned = inverse_mass.shape[0]
    tiles = lax.axis_size("tile")
    parts = lax.axis_size("body")
    spare = -(-owned // LOW)
    per = spare // tiles + 1
    shard = per * tiles
    chunks = (2, parts, tiles // 2, -(-6 * per // 8) * 8, LOW)
    spans = [SMEM((rows,), jnp.int32)] * 2
    partials = call(
        functools.partial(scatter_kernel, per, owned, spare),
        shape(chunks[:3] + (-(-chunks[3] // 6) * 8, LOW)),
        (wall_pressure, wall_normal, wall_arm, wall_body, error),
        spans
        + [
            VMEM((rows, cols, 128), F32),
            VMEM((3, rows, cols, 128), F32),
            VMEM((3, rows, cols, 128), F32),
            VMEM((rows, cols, 128), jnp.int32),
            VMEM(error.shape, F32),
            VMEM(((parts * shard + WINDOW) * 8, LOW), F32),
            VMEM(chunks, F32),
            VMEM((SCATTER_GROUP, WINDOW * 16 * cols, 128), F32),
            VMEM((SCATTER_GROUP, LOW, cols * 128), BF16),
            pltpu.SemaphoreType.DMA((5,)),
            pltpu.SemaphoreType.DMA((2, parts)),
        ],
        [pl.ANY] * 5,
        "scatter",
        pl.ANY,
        60,
    )
    mass = jnp.pad(inverse_mass, (0, spare * LOW - owned)).reshape(spare, LOW)
    lines = chunks[3]
    table = exchange(
        partials, (linear_velocity, angular_velocity, mass, inverse_inertia), per, lines
    )
    pressure, wall_pressure, wall_velocity, own_state, error = call(
        functools.partial(gather_kernel, per, lines, owned),
        (small, small, shape((3, rows, cols, 128)), shape((6, owned)), shape((1, LOW))),
        (table.reshape(-1, LOW), wall_arm, wall_body, pressure, wall_pressure),
        spans,
        [VMEM] * 5,
        "gather",
        None,
        16,
    )
    density_error = error[0, 0] / particle_total
    return (pressure, wall_pressure, own_state, wall_velocity, density_error)


def solution(mesh):
    placed = (
        P(None, "tile", "body", None),
        P("tile", "body", None),
        P("tile", "body", None),
        P("tile", "body", None),
        P("tile", "body", None),
        P(None, "tile", "body", None),
        P(None, "tile", "body", None),
        P(None, "tile", "body", None),
        P("tile", "body", None),
        P("tile", "body", None),
        P(None, "body"),
        P(None, "body"),
        P("body"),
        P(None, "body"),
    )
    return jax.shard_map(
        shards,
        mesh=mesh,
        in_specs=placed,
        out_specs=(
            P("tile", "body", None),
            P("tile", "body", None),
            P(None, "body"),
            P(None, "tile", "body", None),
            P(),
        ),
        check_vma=False,
    )
```

```python
import math
import functools
import jax
import jax.numpy as jnp
from jax import lax
from jax.experimental import pallas as pl
from jax.experimental.pallas import tpu as pltpu
from jax.sharding import PartitionSpec as P

SWEEPS = 2

relax_factor = 0.5
inv_width = 2.0
kernel_scale = 0.0078125
wall_offset = 0.5
time_step = 0.25
gravity_z = -9.81

UNIT = math.sqrt(inv_width / math.log(2.0))
DEPTH = 32
LOW = 128
WINDOW = 6
TABLE = 7
GROUP = 4
OWN_GROUP = 8
SCATTER_GROUP = 4
F32, BF16 = jnp.float32, jnp.bfloat16
VMEM = pltpu.VMEM
SMEM = pltpu.SMEM


def pieces(x, count):
    out = []
    for _ in range(count):
        piece = x.astype(BF16).astype(F32)
        out.append(piece)
        x = x - piece
    return out


def near_rows(x):
    h, m, l = pieces(x, 3)
    return [h, m, h, l, h] + pieces(-(x * x), 3)


def own_rows(x):
    h, m, l = pieces(2.0 * x, 3)
    one = jnp.ones_like(x)
    return [h, h, m, h, l, one, one, one]


def centre(first, size, axis):
    at = first + lax.broadcasted_iota(jnp.int32, (size, 128), 0) if axis else first
    return at.astype(F32) + 0.5


def build_near(tab_ref, start, stride, x, y, z):
    count = x.shape[0]
    groups = [near_rows(x + (v - 1) * UNIT) for v in range(3)]
    groups += [near_rows(y + (v - 1) * UNIT) for v in range(3)]
    groups += [near_rows(z)]
    for g, group in enumerate(groups):
        for k, value in enumerate(group):
            at = (start + g) * 8 + k
            if count == 1:
                tab_ref[pl.ds(at, 1), :] = value
            else:
                tab_ref[pl.ds(at, count, stride=stride * TABLE * 8), :] = value


def own_group(i, pos_ref, lhs_ref, stage_ref, bx, by, tab_ref=None):
    cols = pos_ref.shape[2]
    for e in range(OWN_GROUP):
        r = i * OWN_GROUP + e
        x = (pos_ref[0, r] - centre(bx + r, cols, 0)) * UNIT
        y = (pos_ref[1, r] - centre(by, cols, 1)) * UNIT
        z = (pos_ref[2, r] - 0.5) * UNIT
        norm = pieces(-(x * x + y * y + z * z), 3)
        for k, value in enumerate(own_rows(x) + own_rows(y) + own_rows(z) + norm):
            stage_ref[e, k * cols : (k + 1) * cols] = value
        if tab_ref is not None:
            build_near(tab_ref, ((r + 1) * (cols + 2) + 1) * TABLE, 1, x, y, z)
    for e in range(OWN_GROUP):
        for c in range(cols):
            start = pl.multiple_of(((i * OWN_GROUP + e) * cols + c) * 128, 128)
            turned = stage_ref[e, pl.ds(c, DEPTH, stride=cols), :].astype(BF16).T
            lhs_ref[pl.ds(start, 128), 0:DEPTH] = turned


def listed_near(r, c, k, near_ref):
    code = near_ref[k, c, r]
    up = (code * 11) >> 5
    return up, code - up * 3


def pair_exponents(r, c, near_ref, tab_ref, lhs_ref, cols):
    ones = (lax.broadcasted_iota(jnp.int32, (8, 128), 0) < 3).astype(F32)
    listed = near_ref.shape[0]
    sides = []
    for k in range(listed):
        up, side = listed_near(r, c, k, near_ref)
        base = ((r + up) * (cols + 2) + c + side) * TABLE
        rows = [tab_ref[pl.ds(at * 8, 8), :] for at in (base + up, base + 3 + side, base + 6)]
        sides.append(jnp.concatenate(rows + [ones], axis=0).astype(BF16))
    lhs = lhs_ref[pl.ds(pl.multiple_of((r * cols + c) * 128, 128), 128), 0:DEPTH]
    return [
        jnp.dot(lhs, jnp.concatenate(sides[k : k + 2], axis=1), preferred_element_type=F32)
        for k in range(0, listed, 2)
    ]


def pair_sums(r, c, exponents, near_ref, val_ref, keep_ref, cols):
    block = r * cols + c
    listed = near_ref.shape[0]
    ws = wv = None
    for k in range(listed):
        up, side = listed_near(r, c, k, near_ref)
        value = val_ref[pl.ds((r + up) * 16 + c + side, 1), :]
        part = jnp.exp2(exponents[k // 2][:, k % 2 * 128 : k % 2 * 128 + 128])
        if keep_ref is not None:
            at = pl.multiple_of((block * listed + k) * 128, 128)
            keep_ref[pl.ds(at, 128), :] = part
        product = part * value
        ws = part if ws is None else ws + part
        wv = product if wv is None else wv + product
    return [jnp.sum(total.T, axis=0, keepdims=True) * kernel_scale for total in (ws, wv)]


def kept_block(r, c, near_ref, val_ref, keep_ref, cols):
    listed = near_ref.shape[0]
    block = r * cols + c
    wv = None
    for k in range(listed):
        code = near_ref[k, c, r]
        up = (code * 11) >> 5
        value = val_ref[pl.ds((r + up) * 16 + c + code - up * 3, 1), :]
        at = pl.multiple_of((block * listed + k) * 128, 128)
        product = keep_ref[pl.ds(at, 128), :] * value
        wv = product if wv is None else wv + product
    return jnp.sum(wv.T, axis=0, keepdims=True) * kernel_scale


WAYS = ((-1, 0), (1, 0), (0, -1), (0, 1), (-1, -1), (-1, 1), (1, -1), (1, 1))


def fluid_kernel(
    near_ref,
    pos_ref,
    p_ref,
    source_ref,
    stiff_ref,
    wall_ref,
    live_ref,
    p_out,
    wp_out,
    error_out,
    tab_ref,
    val_ref,
    lhs_ref,
    keep_ref,
    stage_ref,
    ws_ref,
    wv_ref,
    mid_ref,
    row_send,
    row_in,
    col_send,
    col_in,
    corner_send,
    corner_in,
    row_in2,
    col_send2,
    col_in2,
    corner_send2,
    corner_in2,
    send,
    recv,
):
    rows, cols = p_ref.shape[0], p_ref.shape[1]
    tiles, parts = lax.axis_size("tile"), lax.axis_size("body")
    t, b = lax.axis_index("tile"), lax.axis_index("body")
    bx, by = t * rows, b * cols

    def exists(dt, db):
        ok = jnp.bool_(True)
        if dt:
            ok = (t > 0) if dt < 0 else (t < tiles - 1)
        if db:
            side = (b > 0) if db < 0 else (b < parts - 1)
            ok = jnp.logical_and(ok, side) if dt else side
        return ok

    barrier = pltpu.get_barrier_semaphore()
    for dt, db in WAYS:

        @pl.when(exists(dt, db))
        def _():
            pl.semaphore_signal(
                barrier, inc=1, device_id=(t + dt, b + db), device_id_type=pl.DeviceIdType.MESH
            )

    def copy(phase, n):
        dt, db = WAYS[n]
        if n < 2:
            src = row_send.at[n] if phase == 0 else (mid_ref, p_out)[phase - 1].at[n * (rows - 1)]
            dst = row_in.at[n] if phase == 0 else row_in2.at[phase - 1, n]
        elif n < 4:
            src = col_send.at[n - 2] if phase == 0 else col_send2.at[phase - 1, n - 2]
            dst = col_in.at[n - 2] if phase == 0 else col_in2.at[phase - 1, n - 2]
        else:
            src = corner_send.at[n - 4] if phase == 0 else corner_send2.at[phase - 1, n - 4]
            dst = corner_in.at[n - 4] if phase == 0 else corner_in2.at[phase - 1, n - 4]
        return remote(src, dst, send.at[phase, n], recv.at[phase, n], (t + dt, b + db))

    def launch(phase):
        for n, (dt, db) in enumerate(WAYS):

            @pl.when(exists(dt, db))
            def _():
                copy(phase, n).start()

    def arrive(phase):
        for n, (dt, db) in enumerate(WAYS):

            @pl.when(exists(-dt, -db))
            def _():
                copy(phase, n).wait_recv()

    def depart(phase):
        for n, (dt, db) in enumerate(WAYS):

            @pl.when(exists(dt, db))
            def _():
                copy(phase, n).wait_send()

    def pack(phase, ref):
        for side in range(2):
            for r in range(rows):
                line = ref[r, side * (cols - 1) : side * (cols - 1) + 1]
                col_send2[phase - 1, side, r : r + 1] = line
        for n, (dt, db) in enumerate(WAYS[4:]):
            r, c = (dt > 0) * (rows - 1), (db > 0) * (cols - 1)
            corner_send2[phase - 1, n, 0:1] = ref[r, c : c + 1]

    fields = [(pos_ref, d) for d in range(3)] + [(p_ref, None)]
    for d, (ref, at) in enumerate(fields):
        view = ref if at is None else ref.at[at]
        for side in range(2):
            row_send[side, d] = view[side * (rows - 1)]
            for r in range(rows):
                line = view[r, side * (cols - 1) : side * (cols - 1) + 1]
                col_send[side, d, r : r + 1] = line
        for n, (dt, db) in enumerate(WAYS[4:]):
            r, c = (dt > 0) * (rows - 1), (db > 0) * (cols - 1)
            corner_send[n, d : d + 1] = view[r, c : c + 1]

    along = 1 + (t > 0).astype(jnp.int32) + (t < tiles - 1).astype(jnp.int32)
    across = 1 + (b > 0).astype(jnp.int32) + (b < parts - 1).astype(jnp.int32)
    stage_ref[...] = jnp.zeros_like(stage_ref)
    groups = rows // OWN_GROUP

    def both(i, carry):
        own_group(i, pos_ref, lhs_ref, stage_ref, bx, by, tab_ref)
        return carry

    lax.fori_loop(0, groups, both, 0)
    pl.semaphore_wait(barrier, along * across - 1)
    launch(0)

    def fill(ref):
        for r in range(rows):
            val_ref[(r + 1) * 16 + 1 : (r + 1) * 16 + 1 + cols] = ref[r]

    def slots(n):
        dt, db = WAYS[n]
        return (0 if dt > 0 else rows + 1), (0 if db > 0 else cols + 1)

    def halo_values(phase):
        for n, (dt, db) in enumerate(WAYS):
            ok = exists(-dt, -db)
            r, c = slots(n)
            if n < 2:
                got = row_in[n, 3] if phase == 0 else row_in2[phase - 1, n]
                val_ref[r * 16 + 1 : r * 16 + 1 + cols] = jnp.where(ok, got, 0.0)
            elif n < 4:
                got = col_in[n - 2, 3] if phase == 0 else col_in2[phase - 1, n - 2]
                val_ref[pl.ds(16 + c, rows, stride=16), :] = jnp.where(ok, got, 0.0)
            else:
                got = (
                    corner_in[n - 4, 3:4]
                    if phase == 0
                    else corner_in2[phase - 1, n - 4, 0:1]
                )
                val_ref[r * 16 + c : r * 16 + c + 1] = jnp.where(ok, got, 0.0)

    def halo_tables():
        for n, (dt, db) in enumerate(WAYS):
            ok = exists(-dt, -db)
            r, c = slots(n)
            across_r = bx - 1 if dt > 0 else bx + rows
            across_c = by - 1 if db > 0 else by + cols
            if n < 2:
                x, y, z = [jnp.where(ok, row_in[n, d], 0.0) for d in range(3)]
                x = x - centre(across_r, cols, 0)
                y = y - centre(by, cols, 1)
                start, stride = (r * (cols + 2) + 1) * TABLE, 1
            elif n < 4:
                x, y, z = [jnp.where(ok, col_in[n - 2, d], 0.0) for d in range(3)]
                x = x - centre(bx, rows, 1)
                y = y - centre(across_c, rows, 0)
                start, stride = (cols + 2 + c) * TABLE, cols + 2
            else:
                x, y, z = [jnp.where(ok, corner_in[n - 4, d : d + 1], 0.0) for d in range(3)]
                x = x - centre(across_r, 1, 0)
                y = y - centre(across_c, 1, 0)
                start, stride = (r * (cols + 2) + c) * TABLE, 1
            build_near(tab_ref, start, stride, x * UNIT, y * UNIT, (z - 0.5) * UNIT)

    def sweep(first, meet):
        def block(r, c):
            if first is None:
                wv = kept_block(r, c, near_ref, val_ref, keep_ref, cols)
            else:
                exponents = pair_exponents(r, c, near_ref, tab_ref, lhs_ref, cols)
                ws, wv = pair_sums(
                    r, c, exponents, near_ref, val_ref, keep_ref if first else None, cols
                )
                ws_ref[r, pl.ds(c, 1), :] = ws
            wv_ref[r, pl.ds(c, 1), :] = wv

        def columns(*chosen):
            for c in chosen:
                for r in range(1, rows - 1):
                    block(r, c)

        def inner(i, carry):
            columns(*[1 + i * wide + e for e in range(wide)])
            return carry

        def side(i, carry):
            columns(i * (cols - 1))
            if first is None:
                for e in range(groups // 2):
                    own_group(i * (groups // 2) + e, wall_ref, lhs_ref, stage_ref, bx, by)
            return carry

        wide = 2 if (cols - 2) % 2 == 0 else 1
        lax.fori_loop(0, (cols - 2) // wide, inner, 0)
        meet()
        lax.fori_loop(0, 2, side, 0)
        for r in (0, rows - 1):
            for c in range(cols):
                block(r, c)

    fill(p_ref)

    def meet(phase):
        arrive(phase)
        if phase == 0:
            halo_tables()
        halo_values(phase)

    def relax(before_ref, after_ref):
        pressure = before_ref[...]
        diagonal = stiff_ref[...] + ws_ref[...]
        residual = source_ref[...] - (diagonal * pressure - wv_ref[...])
        after_ref[...] = jnp.maximum(pressure + relax_factor * residual / diagonal, 0.0)
        return residual

    sweep(True, lambda: meet(0))
    relax(p_ref, mid_ref)
    pack(1, mid_ref)
    launch(1)
    fill(mid_ref)
    sweep(None, lambda: meet(1))
    residual = relax(mid_ref, p_out)
    pack(2, p_out)
    launch(2)
    error_out[...] = jnp.sum(residual * residual, axis=0)
    fill(p_out)
    sweep(False, lambda: meet(2))
    wp_out[...] = wv_ref[...] / (wall_offset + ws_ref[...]) * live_ref[...].astype(F32)
    for phase in range(3):
        depart(phase)


def fluid(near, pos, p, source, stiff, wall, live):
    rows, cols, _ = p.shape
    small = shape((rows, cols, 128))
    return pl.pallas_call(
        fluid_kernel,
        out_shape=(small, small, shape((cols, 128))),
        in_specs=[pl.BlockSpec(memory_space=SMEM)] + [pl.BlockSpec(memory_space=VMEM)] * 6,
        out_specs=(pl.BlockSpec(memory_space=VMEM),) * 3,
        scratch_shapes=[
            VMEM(((rows + 2) * (cols + 2) * TABLE * 8, 128), F32),
            VMEM(((rows + 2) * 16, 128), F32),
            VMEM((rows * cols * 128, 128), BF16),
            VMEM((rows * cols * near.shape[0] * 128, 128), F32),
            VMEM((OWN_GROUP, DEPTH * cols, 128), F32),
            VMEM((rows, cols, 128), F32),
            VMEM((rows, cols, 128), F32),
            VMEM((rows, cols, 128), F32),
            VMEM((2, 4, cols, 128), F32),
            VMEM((2, 4, cols, 128), F32),
            VMEM((2, 4, rows, 128), F32),
            VMEM((2, 4, rows, 128), F32),
            VMEM((4, 8, 128), F32),
            VMEM((4, 8, 128), F32),
            VMEM((2, 2, cols, 128), F32),
            VMEM((2, 2, rows, 128), F32),
            VMEM((2, 2, rows, 128), F32),
            VMEM((2, 4, 8, 128), F32),
            VMEM((2, 4, 8, 128), F32),
            pltpu.SemaphoreType.DMA((3, 8)),
            pltpu.SemaphoreType.DMA((3, 8)),
        ],
        compiler_params=pltpu.CompilerParams(
            collective_id=1, has_side_effects=True, vmem_limit_bytes=62 * 2**20
        ),
        name="fluid",
    )(near, pos, p, source, stiff, wall, live)


def split(x, n):
    if n & (n - 1):
        return lax.div(x, n), lax.rem(x, n)
    return x >> (n.bit_length() - 1), x & (n - 1)


def find_spans(body_ref, first_ref, last_ref, owned, shard):
    for r in range(body_ref.shape[0]):
        top, _ = two_level(body_ref[r], owned, shard)
        first_ref[r] = jnp.min(top)
        last_ref[r] = jnp.max(top)


def scatter_kernel(
    per,
    owned,
    spare,
    wp_in,
    normal_in,
    arm_in,
    body_in,
    error_in,
    out_ref,
    first_ref,
    last_ref,
    wp_ref,
    normal_ref,
    arm_ref,
    body_ref,
    error_ref,
    acc_ref,
    part_ref,
    stage_ref,
    hot_ref,
    loaded,
    stored,
):
    rows, cols = wp_ref.shape[0], wp_ref.shape[1]
    parts, chips, lines = part_ref.shape[1:4]
    shard = per * chips * 2
    loads = [(body_in, body_ref), (wp_in, wp_ref), (normal_in, normal_ref), (arm_in, arm_ref)]
    loads += [(error_in, error_ref)]
    loads = [pltpu.make_async_copy(src, dst, loaded.at[n]) for n, (src, dst) in enumerate(loads)]
    for load in loads:
        load.start()
    acc_ref[...] = jnp.zeros_like(acc_ref)
    stage_ref[...] = jnp.zeros_like(stage_ref)
    loads[0].wait()
    find_spans(body_ref, first_ref, last_ref, owned, shard)
    for load in loads[1:]:
        load.wait()
    low_iota = lax.broadcasted_iota(jnp.int32, (LOW, 128), 0).astype(F32).astype(BF16)
    one, zero = jnp.ones((LOW, 128), BF16), jnp.zeros((LOW, 128), BF16)
    tall = WINDOW * 16

    def window(r, e, start):
        wp = wp_ref[r]
        fx, fy, fz = [wp * normal_ref[d, r] for d in range(3)]
        ax, ay, az = [arm_ref[d, r] for d in range(3)]
        values = [fx, fy, fz, ay * fz - az * fy, az * fx - ax * fz, ax * fy - ay * fx]
        top, _ = two_level(body_ref[r], owned, shard)
        here = [top == start + w for w in range(WINDOW)]
        for q, value in enumerate(values):
            for s, piece in enumerate(pieces(value, 2)):
                for w in range(WINDOW):
                    at = (w * 16 + s * 8 + q) * cols
                    stage_ref[e, at : at + cols] = jnp.where(here[w], piece, 0.0)
        total = jnp.zeros((tall, LOW), F32)
        for c in range(0, cols, 2):
            lhs = jnp.concatenate(
                [stage_ref[e, pl.ds(c + k, tall, stride=cols), :] for k in range(2)], axis=1
            )
            total = total + lax.dot_general(
                lhs.astype(BF16),
                hot_ref[e, :, c * 128 : (c + 2) * 128],
                (((1,), (1,)), ((), ())),
                preferred_element_type=F32,
            )
        return [total[w * 16 : w * 16 + 8] + total[w * 16 + 8 : w * 16 + 16] for w in range(WINDOW)]

    def add(start, found):
        for w in range(WINDOW):
            at = pl.multiple_of((start + w) * 8, 8)
            acc_ref[pl.ds(at, 8), :] += found[w]

    def group(i, carry):
        found = []
        for e in range(SCATTER_GROUP):
            r = i * SCATTER_GROUP + e
            _, low = two_level(body_ref[r], owned, shard)
            low = low.astype(F32)
            for c in range(cols):
                line = jnp.broadcast_to(low[c : c + 1], (LOW, 128)).astype(BF16)
                hot_ref[e, :, c * 128 : (c + 1) * 128] = jnp.where(low_iota == line, one, zero)
            found.append(window(r, e, first_ref[r]))
        for e in range(SCATTER_GROUP):
            add(first_ref[i * SCATTER_GROUP + e], found[e])
        for e in range(SCATTER_GROUP):
            r = i * SCATTER_GROUP + e

            def more(j, carry):
                start = first_ref[r] + j * WINDOW
                add(start, window(r, e, start))
                return carry

            lax.fori_loop(1, split(last_ref[r] - first_ref[r], WINDOW)[0] + 1, more, 0)
        return carry

    lax.fori_loop(0, rows // SCATTER_GROUP, group, 0)
    lane = lax.broadcasted_iota(jnp.int32, (8, LOW), 1)
    acc_ref[spare * 8 : spare * 8 + 8] = jnp.where(lane == 0, jnp.sum(error_ref[...]), 0.0)
    stores = []
    for p in range(parts):
        for k in range(2):
            for g in range(chips):
                at = p * shard + (g * 2 + k) * per
                if lines > 6 * per:
                    part_ref[k, p, g] = jnp.zeros((lines, LOW), F32)
                for q in range(6):
                    line = acc_ref[pl.ds(at * 8 + q, per, stride=8), :]
                    part_ref[k, p, g, q * per : (q + 1) * per] = line
            out = out_ref.at[k, p, :, 0:lines]
            move = pltpu.make_async_copy(part_ref.at[k, p], out, stored.at[k, p])
            move.start()
            stores.append(move)
    for move in stores:
        move.wait()


def gather_kernel(
    per,
    lines,
    owned,
    table_ref,
    arm_ref,
    body_ref,
    p_ref,
    wp_ref,
    p_out,
    wp_out,
    out_ref,
    own_ref,
    error_ref,
    first_ref,
    last_ref,
):
    rows, cols = body_ref.shape[0], body_ref.shape[1]
    tiles, parts = lax.axis_size("tile"), lax.axis_size("body")
    chips, shard = tiles // 2, per * tiles
    spare = -(-owned // LOW)
    b = lax.axis_index("body")
    find_spans(body_ref, first_ref, last_ref, owned, shard)
    p_out[...] = p_ref[...]
    wp_out[...] = wp_ref[...]

    def place(top):
        p, rest = split(top, shard)
        t, n = split(rest, per)
        return (((t & 1) * parts + p) * chips + (t >> 1)) * lines + n

    def window(top, low, start, last, got):
        got = list(got)
        for w in range(WINDOW):
            here = top == start + w
            at = place(jnp.minimum(start + w, last))
            for q in range(6):
                line = jnp.broadcast_to(table_ref[pl.ds(at + q * per, 1), :], (cols, LOW))
                found = jnp.take_along_axis(line, low, axis=1, mode="promise_in_bounds")
                got[q] = jnp.where(here, found, got[q])
        return tuple(got)

    def group(i, carry):
        both, ends, states = [], [], []
        zero = jnp.zeros((cols, LOW), F32)
        for e in range(GROUP):
            r = i * GROUP + e
            both.append(two_level(body_ref[r], owned, shard))
            ends.append((first_ref[r], last_ref[r]))
            states.append(window(*both[e], ends[e][0], ends[e][1], (zero,) * 6))
        for e in range(GROUP):
            r = i * GROUP + e
            first, last = ends[e]

            def more(j, got):
                return window(*both[e], first + j * WINDOW, last, got)

            count = split(last - first, WINDOW)[0] + 1
            vx, vy, vz, wx, wy, wz = lax.fori_loop(1, count, more, states[e])
            ax, ay, az = [arm_ref[d, r] for d in range(3)]
            out_ref[0, r] = vx + (wy * az - wz * ay)
            out_ref[1, r] = vy + (wz * ax - wx * az)
            out_ref[2, r] = vz + (wx * ay - wy * ax)
        return carry

    lax.fori_loop(0, rows // GROUP, group, 0)
    for n in range(spare):
        wide = min(LOW, owned - n * LOW)
        t = n // per
        at = b * (chips * lines) + ((t % 2) * parts * chips + t // 2) * lines + n % per
        for q in range(6):
            line = table_ref[pl.ds(at + q * per, 1), :]
            own_ref[q : q + 1, n * LOW : n * LOW + wide] = line[:, :wide]
    t = spare // per
    at = ((t % 2) * parts * chips + t // 2) * lines + spare % per
    error_ref[...] = table_ref[at : at + 1]


def remote(src, dst, send, recv, device):
    return pltpu.make_async_remote_copy(
        src_ref=src,
        dst_ref=dst,
        send_sem=send,
        recv_sem=recv,
        device_id=device,
        device_id_type=pl.DeviceIdType.MESH,
    )


def exchange_kernel(
    per,
    partial_ref,
    linear_in,
    angular_in,
    mass_in,
    inertia_in,
    g1_ref,
    held_ref,
    linear_ref,
    angular_ref,
    mass_ref,
    inertia_ref,
    loaded,
    par_ref,
    r1_ref,
    s1_ref,
    r2_ref,
    s2_ref,
    r3_ref,
    send1,
    recv1,
    send2,
    recv2,
    send3,
    recv3,
    send4,
    recv4,
    send5,
    recv5,
    send6,
    recv6,
):
    parts, chips = r1_ref.shape[0], r1_ref.shape[1]
    spare = mass_ref.shape[0]
    shard = per * chips * 2
    t, b = lax.axis_index("tile"), lax.axis_index("body")
    core, chip = t % 2, t // 2
    barrier = pltpu.get_barrier_semaphore()
    partner = (chip * 2 + 1 - core, b)
    others2 = [(chip + k) % chips for k in range(1, chips)]
    upper = b >= parts // 2
    lines = r1_ref.shape[2]
    loads = [
        (partial_ref.at[core, :, :, 0:lines], held_ref),
        (linear_in, linear_ref),
        (angular_in, angular_ref),
        (mass_in, mass_ref),
        (inertia_in, inertia_ref),
    ]
    loads = [pltpu.make_async_copy(src, dst, loaded.at[n]) for n, (src, dst) in enumerate(loads)]
    for load in loads:
        load.start()
    others3 = [(b + jnp.where(upper, i, parts - i)) % parts for i in range(1, parts)]
    order, nearest = others3 + [b], others3[::-1]
    greeted = [partner] + [(g * 2 + core, b) for g in others2] + [(t, g) for g in others3]
    for device in greeted:
        pl.semaphore_signal(barrier, inc=1, device_id=device, device_id_type=pl.DeviceIdType.MESH)

    pl.semaphore_wait(barrier, len(greeted))

    started = []

    def go(*args):
        item = remote(*args)
        item.start()
        started.append(item)

    for p in order:
        piece = partial_ref.at[1 - core, p, :, 0:lines]
        go(piece, r1_ref.at[p], send1.at[p], recv1.at[p], partner)
    for load in loads:
        load.wait()
    for n in range(per):
        row = t * per + n
        held = row < spare
        row = jnp.minimum(row, spare - 1)
        at = pl.multiple_of(row * LOW, LOW)
        for d in range(3):
            own = slice(n, n + 1)
            par_ref[d, own] = jnp.where(held, linear_ref[d : d + 1, pl.ds(at, LOW)], 0.0)
            par_ref[3 + d, own] = jnp.where(held, angular_ref[d : d + 1, pl.ds(at, LOW)], 0.0)
            par_ref[7 + d, own] = jnp.where(held, inertia_ref[d : d + 1, pl.ds(at, LOW)], 0.0)
        par_ref[6, n : n + 1] = jnp.where(held, mass_ref[pl.ds(row, 1), :], 1.0 / time_step)
    for p in order:
        piece = partial_ref.at[1 - core, p, :, 0:lines]
        remote(piece, r1_ref.at[p], send1.at[p], recv1.at[p], partner).wait_recv()
        s1_ref[p] = held_ref[p] + r1_ref[p]
        for g in others2:
            go(
                s1_ref.at[p, g],
                r2_ref.at[p, chip],
                send2.at[p, g],
                recv2.at[p, chip],
                (g * 2 + core, b),
            )
    for i, p in enumerate(order):
        total = s1_ref[p, chip]
        for g in others2:
            remote(
                s1_ref.at[p, g], r2_ref.at[p, g], send2.at[p, g], recv2.at[p, g], partner
            ).wait_recv()
            total = total + r2_ref[p, g]
        s2_ref[p] = total
        if i < parts - 1:
            go(s2_ref.at[p], r3_ref.at[b], send3.at[p], recv3.at[b], (t, p))
    total = s2_ref[b]
    for g in nearest:
        remote(s2_ref.at[g], r3_ref.at[g], send3.at[g], recv3.at[g], partner).wait_recv()
        total = total + r3_ref[g]

    if lines > 6 * per:
        g1_ref[core, b, chip] = total
    for q in range(6):
        moved = total[q * per : (q + 1) * per]
        if q < 3:
            state = par_ref[q] + time_step * (par_ref[6] * moved)
        else:
            state = par_ref[q] + time_step * par_ref[4 + q] * moved
        if q == 2:
            state = state + time_step * gravity_z
        g1_ref[core, b, chip, q * per : (q + 1) * per] = state

    mine = g1_ref.at[core, b, chip]
    for p in others3:
        go(mine, mine, send4.at[p], recv4.at[b], (t, p))

    def spread(p):
        part = g1_ref.at[core, p, chip]
        for g in others2:
            go(part, part, send5.at[p, g], recv5.at[p, chip], (g * 2 + core, b))

    spread(b)
    for p in nearest:
        part = g1_ref.at[core, p, chip]
        remote(part, part, send4.at[p], recv4.at[p], partner).wait_recv()
        spread(p)
    for p in [b] + nearest:
        for g in others2:
            part = g1_ref.at[core, p, g]
            remote(part, part, send5.at[p, g], recv5.at[p, g], partner).wait_recv()
        go(g1_ref.at[core, p], g1_ref.at[core, p], send6.at[p], recv6.at[p], partner)
    for p in [b] + nearest:
        part = g1_ref.at[1 - core, p]
        remote(part, part, send6.at[p], recv6.at[p], partner).wait_recv()
    for item in started:
        item.wait_send()


def exchange(partials, params, per, lines):
    tiles, parts = lax.axis_size("tile"), lax.axis_size("body")
    chips = tiles // 2
    chunk = (lines, LOW)
    wide = (parts, chips)
    dma = pltpu.SemaphoreType.DMA
    return pl.pallas_call(
        functools.partial(exchange_kernel, per),
        out_shape=shape((2,) + wide + chunk),
        in_specs=[pl.BlockSpec(memory_space=pl.ANY)] * 5,
        out_specs=pl.BlockSpec(memory_space=VMEM),
        scratch_shapes=[VMEM(dims, F32) for dims in [wide + chunk] + [x.shape for x in params]]
        + [
            dma((5,)),
            VMEM((10, per, LOW), F32),
            VMEM(wide + chunk, F32),
            VMEM(wide + chunk, F32),
            VMEM(wide + chunk, F32),
            VMEM((parts,) + chunk, F32),
            VMEM((parts,) + chunk, F32),
        ]
        + [dma(dims) for dims in ((parts,), wide, (parts,), (parts,), wide, (parts,)) for _ in range(2)],
        compiler_params=pltpu.CompilerParams(
            collective_id=9, has_side_effects=True, vmem_limit_bytes=52 * 2**20
        ),
        name="exchange",
    )(partials, *params)


def two_level(body, owned, shard):
    index = body
    for part in range(1, lax.axis_size("body")):
        index = index + jnp.where(body >= part * owned, shard * LOW - owned, 0)
    return index >> (LOW.bit_length() - 1), index & (LOW - 1)


def call(kernel, shapes, ins, scratch, spaces, name, outs=None, limit=60):
    outs = outs or jax.tree.map(lambda _: VMEM, shapes)
    return pl.pallas_call(
        kernel,
        out_shape=shapes,
        in_specs=[pl.BlockSpec(memory_space=s) for s in spaces],
        out_specs=jax.tree.map(lambda s: pl.BlockSpec(memory_space=s), outs),
        scratch_shapes=scratch,
        compiler_params=pltpu.CompilerParams(vmem_limit_bytes=limit * 2**20),
        name=name,
    )(*ins)


def shape(dims, kind=F32):
    return jax.ShapeDtypeStruct(tuple(dims), kind)


def shards(
    fluid_position,
    fluid_pressure,
    source,
    stiffness,
    neighbours,
    wall_position,
    wall_normal,
    wall_arm,
    wall_live,
    wall_body,
    linear_velocity,
    angular_velocity,
    inverse_mass,
    inverse_inertia,
):
    rows, cols, _ = fluid_pressure.shape
    small = shape((rows, cols, 128))
    near = jnp.transpose(neighbours, (2, 1, 0))
    pressure, wall_pressure, error = fluid(
        near, fluid_position, fluid_pressure, source, stiffness, wall_position, wall_live
    )
    particle_total = rows * cols * 128 * lax.axis_size("tile") * lax.axis_size("body")
    owned = inverse_mass.shape[0]
    tiles = lax.axis_size("tile")
    parts = lax.axis_size("body")
    spare = -(-owned // LOW)
    per = spare // tiles + 1
    shard = per * tiles
    chunks = (2, parts, tiles // 2, -(-6 * per // 8) * 8, LOW)
    spans = [SMEM((rows,), jnp.int32)] * 2
    partials = call(
        functools.partial(scatter_kernel, per, owned, spare),
        shape(chunks[:3] + (-(-chunks[3] // 6) * 8, LOW)),
        (wall_pressure, wall_normal, wall_arm, wall_body, error),
        spans
        + [
            VMEM((rows, cols, 128), F32),
            VMEM((3, rows, cols, 128), F32),
            VMEM((3, rows, cols, 128), F32),
            VMEM((rows, cols, 128), jnp.int32),
            VMEM(error.shape, F32),
            VMEM(((parts * shard + WINDOW) * 8, LOW), F32),
            VMEM(chunks, F32),
            VMEM((SCATTER_GROUP, WINDOW * 16 * cols, 128), F32),
            VMEM((SCATTER_GROUP, LOW, cols * 128), BF16),
            pltpu.SemaphoreType.DMA((5,)),
            pltpu.SemaphoreType.DMA((2, parts)),
        ],
        [pl.ANY] * 5,
        "scatter",
        pl.ANY,
        60,
    )
    mass = jnp.pad(inverse_mass, (0, spare * LOW - owned)).reshape(spare, LOW)
    lines = chunks[3]
    table = exchange(
        partials, (linear_velocity, angular_velocity, mass, inverse_inertia), per, lines
    )
    pressure, wall_pressure, wall_velocity, own_state, error = call(
        functools.partial(gather_kernel, per, lines, owned),
        (small, small, shape((3, rows, cols, 128)), shape((6, owned)), shape((1, LOW))),
        (table.reshape(-1, LOW), wall_arm, wall_body, pressure, wall_pressure),
        spans,
        [VMEM] * 5,
        "gather",
        None,
        16,
    )
    density_error = error[0, 0] / particle_total
    return (pressure, wall_pressure, own_state, wall_velocity, density_error)


def solution(mesh):
    placed = (
        P(None, "tile", "body", None),
        P("tile", "body", None),
        P("tile", "body", None),
        P("tile", "body", None),
        P("tile", "body", None),
        P(None, "tile", "body", None),
        P(None, "tile", "body", None),
        P(None, "tile", "body", None),
        P("tile", "body", None),
        P("tile", "body", None),
        P(None, "body"),
        P(None, "body"),
        P("body"),
        P(None, "body"),
    )
    return jax.shard_map(
        shards,
        mesh=mesh,
        in_specs=placed,
        out_specs=(
            P("tile", "body", None),
            P("tile", "body", None),
            P(None, "body"),
            P(None, "tile", "body", None),
            P(),
        ),
        check_vma=False,
    )
```
